256 devices in a mesh: peer: 8 (over x, z_hi), depth: 4 (over z_lo), row: 8 (over y, core).
Axes of the slice: x: 4, y: 4, z: 8 (z_hi: 2, z_lo: 4; z = z_hi * 4 + z_lo), core: 2. Of those that a mesh axis runs over, the one named last changes fastest.
Arguments:
- features: bfloat16 [12, 64, 2048], P('depth', 'row'), may hold values from -6 to 6
- labels: int32 [12, 64, 64], P('depth', 'row'), may hold values from 0 to 103
- conv_weights: bfloat16 [8, 4, 864, 32], P('peer'), may hold values from -0.21875 to 0.21875
- head_weights: bfloat16 [8, 32, 104], P('peer'), may hold values from -4 to 4
- matching: int32 [12, 8], P('depth'), may hold values from 0 to 7, each once within a row
Outputs:
- conv_grads: float32 [8, 4, 864, 32], P('peer')
- head_grads: float32 [8, 32, 104], P('peer')
- input_grads: bfloat16 [8, 12, 64, 2048], P('peer', 'depth', 'row')
The draws below stay inside these ranges and needn't reach their ends.
Inputs may be any that keep to these rules, and one draw needn't show every extreme that they name: `matching`: in every depth plane every peer is distilled by exactly one peer.
All inputs are finite; a program needn't handle non-finite values.
Results may differ from the reference program's by a relative error of at most 0.019.
Values may be sent and summed in bfloat16 or wider, within the bound.
A program may use at most 64 MiB of HBM per device.

```python
import jax
import jax.numpy as jnp
from jax import lax

C = 32
K = 104
LAYERS = 4
WIDTH = 64
PEERS = 8
DEPTH = 12
ROWS = 64
N_PEER = 8


def with_ends(array, own_key, low, largest):
    index_at = [jax.random.randint(jax.random.fold_in(own_key, axis), (), 0, length) for axis, length in enumerate(array.shape)]
    main_axis = array.shape.index(max(array.shape))
    beside = index_at[:main_axis] + [(index_at[main_axis] + 1) % array.shape[main_axis]] + index_at[main_axis + 1:]
    return array.at[tuple(index_at)].set(low).at[tuple(beside)].set(largest)


def block_levels(stream_key, dims, cuts, least, largest):
    def one(dim, blocks):
        steps = jax.random.uniform(jax.random.fold_in(jax.random.fold_in(stream_key, 6), dim), (blocks,), jnp.float32, least / len(cuts), largest / len(cuts))
        return jnp.repeat(jnp.exp(steps), dims[dim] // blocks).reshape((-1,) + (1,) * (len(dims) - dim - 1))

    loudness = one(*cuts[0])
    for cut in cuts[1:]:
        loudness = loudness * one(*cut)
    return loudness


def noise(own_key, extent, width, limit, split=(), kind=jnp.bfloat16):
    values = jax.random.normal(own_key, extent, jnp.float32) * width
    if len(split) > 0:
        values = block_levels(own_key, extent, split, -0.22, 0.18) * values
    return jnp.clip(values, min=-limit, max=limit).astype(kind)


def setup_inputs(seed: int = 0) -> dict:
    seeds = jax.random.split(jax.random.key(seed), 6)
    features = noise(seeds[0], (DEPTH, ROWS, WIDTH * C), 1.0, 6.0, ((0, 4), (1, 8)))
    labels = with_ends(jax.random.randint(seeds[1], (DEPTH, ROWS, WIDTH), 0, K), jax.random.fold_in(seeds[1], 1), 0, K - 1).astype(jnp.int32)
    conv_weights = noise(seeds[2], (PEERS, LAYERS, 27 * C, C), (27 * C) ** -0.5, 0.21875, ((0, 8),))
    head_weights = noise(seeds[3], (PEERS, C, K), (C // 16) ** -0.5, 4.0, ((0, 8),))
    matching = jax.vmap(lambda own: jax.random.permutation(own, PEERS))(jax.random.split(seeds[4], DEPTH)).reshape((DEPTH, PEERS)).astype(jnp.int32)
    return {"features": features, "labels": labels, "conv_weights": conv_weights, "head_weights": head_weights, "matching": matching}


def columns(block, rows_out, width_out):
    pieces = []
    for depth_off in range(3):
        for row_off in range(3):
            for col_off in range(3):
                pieces.append(block[depth_off, row_off:row_off + rows_out, col_off:col_off + width_out, :])
    return jnp.concatenate(pieces, axis=-1).reshape(rows_out * width_out, -1)

def widened(padded, channels):
    depth_in, rows_in, merged = padded.shape
    volume = padded.reshape(depth_in, rows_in, merged // channels, channels)
    return jnp.pad(volume, ((0, 0), (0, 0), (1, 1), (0, 0)))

def convolve(padded, weight):
    channels = weight.shape[1]
    volume = widened(padded, channels)
    depth_out = padded.shape[0] - 2
    rows_out = padded.shape[1] - 2
    width_out = volume.shape[2] - 2
    weight_wide = weight.astype(jnp.float32)

    def one_slice(depth_index):
        block = lax.dynamic_slice_in_dim(volume, depth_index, 3, 0)
        cols = columns(block, rows_out, width_out).astype(jnp.float32)
        return jnp.dot(cols, weight_wide, precision=lax.Precision.HIGHEST)
    result = lax.map(one_slice, jnp.arange(depth_out, dtype=jnp.int32))
    return result.reshape(depth_out, rows_out, width_out * channels)

def weight_grad(padded, grad_out, channels):
    volume = widened(padded, channels)
    depth_out = padded.shape[0] - 2
    rows_out = padded.shape[1] - 2
    width_out = volume.shape[2] - 2
    grads = grad_out.reshape(depth_out, rows_out * width_out, channels)

    def accumulate(carry, depth_index):
        block = lax.dynamic_slice_in_dim(volume, depth_index, 3, 0)
        cols = columns(block, rows_out, width_out).astype(jnp.float32)
        slab = lax.dynamic_index_in_dim(grads, depth_index, 0, keepdims=False).astype(jnp.float32)
        return (carry + jnp.dot(cols.T, slab, precision=lax.Precision.HIGHEST), None)
    init = jnp.zeros((27 * channels, channels), jnp.float32)
    result, unused = lax.scan(accumulate, init, jnp.arange(depth_out, dtype=jnp.int32))
    return result

def flipped(weight):
    channels = weight.shape[1]
    return weight.reshape(27, channels, channels)[::-1].transpose(0, 2, 1).reshape(27 * channels, channels)

def padding(volume):
    return jnp.pad(volume, ((1, 1), (1, 1), (0, 0)))

def slope(pre):
    value = pre.astype(jnp.float32)
    sigma = jax.nn.sigmoid(value)
    return sigma * (1.0 + value * (1.0 - sigma))

def forward(features, kernels, head):
    layers = kernels.shape[0]
    current = features
    padded_list = []
    pre_list = []
    activations = [features]
    for layer in range(layers):
        padded = padding(current)
        padded_list.append(padded)
        pre_full = convolve(padded, kernels[layer])
        pre_list.append(pre_full.astype(jnp.bfloat16))
        current = jax.nn.silu(pre_full).astype(jnp.bfloat16)
        activations.append(current)
    channels = kernels.shape[2]
    hidden = current.reshape(-1, channels)
    logits = jnp.dot(hidden.astype(jnp.float32), head.astype(jnp.float32), precision=lax.Precision.HIGHEST)
    exponent = jnp.exp(logits)
    probs = exponent / lax.optimization_barrier(jnp.sum(exponent, axis=1, keepdims=True))
    return (padded_list, pre_list, hidden, probs)

def reference(features, labels, conv_weights, head_weights, matching):
    channels = conv_weights.shape[3]
    classes = head_weights.shape[2]
    layers = conv_weights.shape[1]
    depth_all, rows_all, merged = features.shape
    voxels = labels.size
    onehot = (labels.reshape(voxels, 1) == jnp.arange(classes, dtype=jnp.int32)[None, :]).astype(jnp.float32)

    def shared_of(peer):
        return forward(features, conv_weights[peer], head_weights[peer])[3].astype(jnp.bfloat16)
    all_shared = lax.map(shared_of, jnp.arange(N_PEER, dtype=jnp.int32))
    all_shared = all_shared.reshape(N_PEER, depth_all, voxels // depth_all, classes)

    def one_peer(peer):
        column = lax.dynamic_index_in_dim(matching, peer, 1, keepdims=False)

        def add(carry, source):
            piece = lax.dynamic_index_in_dim(all_shared, source, 0, keepdims=False).astype(jnp.float32)
            chosen = (column == source).astype(jnp.float32)
            return (carry + chosen[:, None, None] * piece, None)
        start = jnp.zeros((depth_all, voxels // depth_all, classes), jnp.float32)
        partner_shared, unused = lax.scan(add, start, jnp.arange(N_PEER, dtype=jnp.int32))
        partner_shared = partner_shared.reshape(voxels, classes)
        padded_list, pre_list, hidden, probs = forward(features, conv_weights[peer], head_weights[peer])
        mixed_grad = probs - 0.5 * onehot - 0.5 * partner_shared
        head_part = jnp.dot(hidden.astype(jnp.float32).T, mixed_grad, precision=lax.Precision.HIGHEST)
        back_hidden = jnp.dot(mixed_grad, head_weights[peer].astype(jnp.float32).T, precision=lax.Precision.HIGHEST)
        last_slope = slope(pre_list[layers - 1]).reshape(voxels, channels)
        grad_pre = (back_hidden * last_slope).astype(jnp.bfloat16).reshape(depth_all, rows_all, merged)
        kernel_grads = [None] * layers
        input_grad = None
        for layer in reversed(range(layers)):
            kernel_grads[layer] = weight_grad(padded_list[layer], grad_pre, channels)
            back_input = convolve(padding(grad_pre), flipped(conv_weights[peer, layer]))
            if layer > 0:
                grad_pre = (back_input * slope(pre_list[layer - 1])).astype(jnp.bfloat16)
            else:
                input_grad = back_input.astype(jnp.bfloat16)
        return (jnp.stack(kernel_grads), head_part, input_grad)
    return lax.map(one_peer, jnp.arange(N_PEER, dtype=jnp.int32))
```

```python
import functools

import jax
import jax.numpy as jnp
from jax import lax
from jax.experimental import pallas as pl
from jax.experimental.pallas import tpu as pltpu
from jax.sharding import PartitionSpec as P

MESH = pl.DeviceIdType.MESH
F32 = jnp.float32
BF16 = jnp.bfloat16
OFFSETS = [(i, j) for i in range(3) for j in range(3)]
NEIGHBOURS = [(0, 1), (0, -1), (1, 0), (-1, 0), (1, 1), (1, -1), (-1, 1), (-1, -1)]


def nt(a, b):
    return lax.dot_general(a, b, (((1,), (1,)), ((), ())), preferred_element_type=F32)


def nn(a, b):
    return lax.dot_general(a, b, (((1,), (0,)), ((), ())), preferred_element_type=F32)


def slope(pre):
    s = 1.0 / (1.0 + jnp.exp(-pre))
    return s * (1.0 + pre * (1.0 - s))


def kernel(
    sizes,
    x_ref, lab_ref, w_ref, head_ref, match_ref,
    cg_ref, hg_ref, ig_ref,
    xe, ge, wt, wpad, tmp, slp, hcat, tcat, hd, hzin, hzout, hall, zin, zout, part,
    pk, rsin, dep, fin,
    halo_s, halo_r, hx_s, hx_r, ax_s, ax_r, z_s, z_r, rs_s, rs_r, dp_s, dp_r, ag_s, ag_r,
):
    nx, nd, nr, slab, rows, classes, layers = sizes
    cells = slab * rows * 16
    peer = lax.axis_index("peer")
    depth = lax.axis_index("depth")
    row = lax.axis_index("row")
    xpos, zhalf = lax.div(peer, 2), lax.rem(peer, 2)
    zpos = zhalf * nd + depth

    def near(dp, dr):
        where = {}
        if dr:
            where["row"] = lax.rem(row + dr + nr, nr)
        if dp:
            z = lax.rem(zpos + dp + 2 * nd, 2 * nd)
            where["peer"] = 2 * xpos + lax.div(z, nd)
            where["depth"] = lax.rem(z, nd)
        return where

    def x_mate(s):
        return {"peer": 2 * lax.rem(xpos + s, nx) + zhalf}

    z_mate = {"peer": 2 * xpos + (1 - zhalf)}

    def row_mate(s):
        return {"row": lax.rem(row + s, nr)}

    def depth_mate(s):
        return {"depth": lax.rem(depth + s, nd)}

    xe[...] = jnp.zeros_like(xe)
    ge[...] = jnp.zeros_like(ge)
    mates = [near(*step) for step in NEIGHBOURS]
    mates += [x_mate(s) for s in range(1, nx)] + [z_mate]
    mates += [row_mate(s) for s in range(2, nr - 1)]
    mates += [depth_mate(s) for s in range(1, nd)]
    barrier = pltpu.get_barrier_semaphore()
    for mate in mates:
        pl.semaphore_signal(barrier, inc=1, device_id=mate, device_id_type=MESH)

    started = []

    def remote(src, dst, send, recv, mate):
        copy = pltpu.make_async_remote_copy(
            src_ref=src, dst_ref=dst, send_sem=send, recv_sem=recv, device_id=mate, device_id_type=MESH
        )
        return copy

    for d in range(slab):
        for b in range(16):
            tmp[pl.ds(d * rows * 16 + b, rows, stride=16), :] = x_ref[d, :, b * 128 : (b + 1) * 128].astype(F32)
    xe[0, 1 : slab + 1, 1 : rows + 1] = tmp[...].reshape(slab, rows, 16, 128).astype(BF16)

    hcat[...] = jnp.zeros_like(hcat)
    tcat[...] = jnp.zeros_like(tcat)
    tmp[0:32, :] = jnp.zeros((32, 128), F32)
    tmp[0:32, 0:classes] = head_ref[...].astype(F32)
    head = tmp[0:32, :].astype(BF16)
    hd[xpos] = head
    for a in range(4):
        hcat[a * 32 : (a + 1) * 32, a * 128 : (a + 1) * 128] = head

    pl.semaphore_wait(barrier, len(mates))

    def halo_copies(buf, layer, ex):
        copies = []
        for n, (dp, dr) in enumerate(NEIGHBOURS):
            if dp == 0:
                src_p, dst_p = pl.ds(1, slab), pl.ds(1, slab)
            elif dp == 1:
                src_p = pl.ds(slab, 1)
                dst_p = pl.ds(jnp.where(depth == nd - 1, slab + 2, 0), 1)
            else:
                src_p = pl.ds(1, 1)
                dst_p = pl.ds(jnp.where(depth == 0, slab + 3, slab + 1), 1)
            if dr == 0:
                src_r, dst_r = pl.ds(1, rows), pl.ds(1, rows)
            elif dr == 1:
                src_r = pl.ds(rows, 1)
                dst_r = pl.ds(jnp.where(row == nr - 1, rows + 2, 0), 1)
            else:
                src_r = pl.ds(1, 1)
                dst_r = pl.ds(jnp.where(row == 0, rows + 3, rows + 1), 1)
            copies.append(
                remote(
                    buf.at[layer, src_p, src_r], buf.at[layer, dst_p, dst_r],
                    halo_s.at[ex, n], halo_r.at[ex, n], near(dp, dr),
                )
            )
        return copies

    def start(copies):
        for copy in copies:
            copy.start()
        started.extend(copies)
        return copies

    def arrive(copies):
        for copy in copies:
            copy.wait_recv()

    halo = start(halo_copies(xe, 0, 0))
    head_x = start(
        [remote(hd.at[xpos], hd.at[xpos], hx_s.at[s], hx_r.at[s], x_mate(s)) for s in range(1, nx)]
    )

    lane = lax.broadcasted_iota(jnp.int32, (cells, 128), 1)
    block = lax.rem(lax.broadcasted_iota(jnp.int32, (cells, 128), 0), 16)
    low = lane < 64
    inside = jnp.where(low, block, 15 - block) > 0

    def spill(y):
        e = y[:, 128:]
        moved = jnp.where(low, pltpu.roll(e, 1, 0), pltpu.roll(e, cells - 1, 0))
        return y[:, :128] + jnp.where(inside, moved, 0.0)

    wpad[:, 0 : 27 * 32] = w_ref[...].reshape(layers * 32, 27 * 32).astype(F32)
    wt[:, 1, 1:3] = jnp.zeros((9, 2, layers * 32, 128), BF16)
    group = lax.div(lax.broadcasted_iota(jnp.int32, (layers * 32, 128), 1), 32)

    def rolled(v, groups):
        shift = (groups * 32) % 128
        return v if shift == 0 else pltpu.roll(v, shift, 1)

    for ij in range(9):
        blk = None
        for k in range(3):
            t, g = divmod(3 * ij + k, 4)
            piece = rolled(wpad[:, t * 128 : (t + 1) * 128], k - g)
            blk = piece if blk is None else jnp.where(group == k, piece, blk)
        r0 = rolled(blk, -1)
        wt[ij, 0, 0] = jnp.where(group < 2, r0, 0.0).astype(BF16)
        wt[ij, 1, 0] = jnp.where(group == 3, r0, 0.0).astype(BF16)
        wt[ij, 0, 1] = jnp.where(group < 3, blk, 0.0).astype(BF16)
        wt[ij, 0, 2] = jnp.where(group > 0, rolled(blk, 1), 0.0).astype(BF16)
        r3 = rolled(blk, 2)
        wt[ij, 0, 3] = jnp.where(group > 1, r3, 0.0).astype(BF16)
        wt[ij, 1, 3] = jnp.where(group == 0, r3, 0.0).astype(BF16)

    def window(buf, layer, i, j):
        return buf[layer, i : i + slab, j : j + rows].reshape(cells, 128)

    def weights(layer, ij, half):
        return wt[ij, half, :, layer * 32 : (layer + 1) * 32, :].reshape(128, 128)

    def forward(layer):
        cols = jnp.concatenate([window(xe, layer, i, j) for i, j in OFFSETS], axis=1)
        band = jnp.concatenate(
            [jnp.concatenate([weights(layer, ij, 0), weights(layer, ij, 1)], axis=0) for ij in range(9)], axis=1
        )
        return spill(nt(cols, band))

    def backward(layer):
        cols = jnp.concatenate([window(ge, layer, 2 - i, 2 - j) for i, j in OFFSETS], axis=1)
        band = jnp.concatenate(
            [jnp.concatenate([weights(layer, ij, 0), weights(layer, ij, 1)], axis=1) for ij in range(9)], axis=0
        )
        return spill(nn(cols, band))

    for layer in range(layers):
        arrive(halo)
        y = forward(layer)
        act = (y / (1.0 + jnp.exp(-y))).astype(BF16)
        if layer + 1 < layers:
            xe[layer + 1, 1 : slab + 1, 1 : rows + 1] = act.reshape(slab, rows, 16, 128)
            halo = start(halo_copies(xe, layer + 1, layer + 1))
        else:
            hall[xpos] = act.reshape(slab, rows * 16, 128)
            act_x = start(
                [remote(hall.at[xpos], hall.at[xpos], ax_s.at[s], ax_r.at[s], x_mate(s)) for s in range(1, nx)]
            )
        slp[layer] = slope(y.astype(BF16).astype(F32))
        if layer == 1:
            arrive(head_x)
            for d in range(slab):
                hzout[d] = hd[lax.div(match_ref[d, 2 * xpos + (1 - zhalf)], 2)]
            head_z = start([remote(hzout, hzin, z_s.at[0], z_r.at[0], z_mate)])

    hidden = act

    col_class = lax.broadcasted_iota(jnp.int32, (rows * 16, 128), 1)
    real = col_class < classes
    spread_r = lax.broadcasted_iota(jnp.int32, (cells, slab * rows), 0)
    spread_c = lax.broadcasted_iota(jnp.int32, (cells, slab * rows), 1)
    spread = jnp.where(lax.div(spread_r, 16) == spread_c, 1.0, 0.0).astype(BF16)
    lab = nn(spread, lab_ref[...].reshape(slab * rows, 64).astype(F32).astype(BF16))
    vox = lax.broadcasted_iota(jnp.int32, (cells, 64), 1)
    own = lax.rem(lax.broadcasted_iota(jnp.int32, (cells, 64), 0), 16)
    lab = jnp.where(lax.div(vox, 4) == own, lab, 0.0).astype(BF16)
    pick_r = lax.broadcasted_iota(jnp.int32, (64, 512), 0)
    pick_c = lax.broadcasted_iota(jnp.int32, (64, 512), 1)
    pick = jnp.where(lax.rem(pick_r, 4) == lax.div(pick_c, 128), 1.0, 0.0).astype(BF16)
    class_of = nn(lab, pick)

    def softmax(act_plane, heads):
        logits = nn(act_plane, heads)
        out = []
        for a in range(4):
            ex = jnp.where(real, jnp.exp(logits[:, a * 128 : (a + 1) * 128]), 0.0)
            out.append(ex / jnp.sum(ex, axis=1, keepdims=True))
        return out

    n = rows * 16
    col_f = col_class.astype(F32)
    for d in range(slab):
        probs = softmax(hidden[d * n : (d + 1) * n], hcat[...])
        for a in range(4):
            mark = jnp.where(class_of[d * n : (d + 1) * n, a * 128 : (a + 1) * 128] == col_f, 0.5, 0.0)
            part[d, :, a * 128 : (a + 1) * 128] = probs[a] - mark

    arrive(act_x)
    for d in range(slab):
        zout[d] = hall[lax.div(match_ref[d, 2 * xpos + (1 - zhalf)], 2), d]
    act_z = start([remote(zout, zin, z_s.at[1], z_r.at[1], z_mate)])
    arrive(head_z)
    arrive(act_z)
    grad_rows = []
    for d in range(slab):
        source = match_ref[d, peer]
        near_half = lax.rem(source, 2) == zhalf
        mine = lax.div(source, 2)
        target_head = jnp.where(near_half, hd[mine].astype(F32), hzin[d].astype(F32)).astype(BF16)
        target_act = jnp.where(near_half, hall[mine, d].astype(F32), zin[d].astype(F32)).astype(BF16)
        for a in range(4):
            tcat[d, a * 32 : (a + 1) * 32, a * 128 : (a + 1) * 128] = target_head
        target = softmax(target_act, tcat[d])
        grad_rows.append(
            jnp.concatenate(
                [
                    (part[d, :, a * 128 : (a + 1) * 128] - 0.5 * target[a].astype(BF16).astype(F32)).astype(BF16)
                    for a in range(4)
                ],
                axis=1,
            )
        )
    dlogits = jnp.concatenate(grad_rows, axis=0)
    g = nt(dlogits, hcat[...]) * slp[layers - 1]

    group32 = lax.div(lax.broadcasted_iota(jnp.int32, (32, 128), 1), 32)
    group288 = lax.div(lax.broadcasted_iota(jnp.int32, (288, 128), 1), 32)
    own_chunks = 8 // nr

    def weight_grad(layer, g):
        left = jnp.where(low, pltpu.roll(g, cells - 1, 0), pltpu.roll(g, 1, 0))
        ok = jnp.where(low, 15 - block, block) > 0
        edge = jnp.where((lane < 32) | (lane >= 96), jnp.where(ok, left, 0.0), 0.0)
        both = jnp.concatenate([g, edge], axis=1).astype(BF16).T
        cols = jnp.concatenate([window(xe, layer, i, j) for i, j in OFFSETS], axis=1)
        prod = nn(both, cols)

        def take(at):
            return jnp.concatenate([prod[at : at + 32, ij * 128 : (ij + 1) * 128] for ij in range(9)], axis=0)

        s0 = jnp.where(group288 == 3, take(128), take(0))
        s3 = jnp.where(group288 == 0, take(224), take(96))
        total = take(32) + pltpu.roll(s0, 32, 1) + pltpu.roll(take(64), 96, 1) + pltpu.roll(s3, 64, 1)
        for t in range(7):
            tile = None
            ks = [(gr, *divmod(4 * t + gr, 3)) for gr in range(4) if 4 * t + gr < 27]
            for ij in sorted({ij for _, ij, _ in ks}):
                mine = [(gr, k) for gr, at, k in ks if at == ij]
                moved = rolled(total[ij * 32 : (ij + 1) * 32], mine[0][0] - mine[0][1])
                tile = moved if tile is None else jnp.where(group32 >= mine[0][0], moved, tile)
            pk[layer, t // own_chunks, t % own_chunks] = tile.astype(BF16)

    def send_row(layer):
        return start(
            [
                remote(
                    pk.at[layer, lax.rem(row + s, nr)], rsin.at[layer, s], rs_s.at[layer, s], rs_r.at[layer, s], row_mate(s)
                )
                for s in range(1, nr)
            ]
        )

    def send_depth(layer, copies):
        arrive(copies)
        total = pk[layer, row].astype(F32)
        for s in range(1, nr):
            total = total + rsin[layer, s].astype(F32)
        dep[layer, depth] = total.astype(BF16)
        return start(
            [
                remote(
                    dep.at[layer, depth], dep.at[layer, depth], dp_s.at[layer, s], dp_r.at[layer, s], depth_mate(s)
                )
                for s in range(1, nd)
            ]
        )

    def send_all(layer, copies):
        arrive(copies)
        total = dep[layer, 0].astype(F32)
        for s in range(1, nd):
            total = total + dep[layer, s].astype(F32)
        fin[layer, row] = total.astype(BF16)
        return start(
            [
                remote(fin.at[layer, row], fin.at[layer, row], ag_s.at[layer, s], ag_r.at[layer, s], row_mate(s))
                for s in range(1, nr)
            ]
        )

    def finish(layer, copies):
        arrive(copies)
        for t in range(7):
            wide = min(128, 27 * 32 - t * 128)
            cg_ref[layer, :, t * 128 : t * 128 + wide] = fin[layer, t // own_chunks, t % own_chunks].astype(F32)[:, :wide]
        if layer == layers - 1:
            hg_ref[...] = fin[layer, 7 // own_chunks, 7 % own_chunks].astype(F32)[:, :classes]

    stage = {}
    for layer in reversed(range(layers)):
        ge[layer, 1 : slab + 1, 1 : rows + 1] = g.astype(BF16).reshape(slab, rows, 16, 128)
        halo = start(halo_copies(ge, layer, layers + layer))
        if layer == layers - 1:
            wide = nn(hidden.T, dlogits)
            heads = wide[0:32, 0:128]
            for a in range(1, 4):
                heads = heads + wide[a * 32 : (a + 1) * 32, a * 128 : (a + 1) * 128]
            pk[layer, 7 // own_chunks, 7 % own_chunks] = heads.astype(BF16)
        else:
            pk[layer, 7 // own_chunks, 7 % own_chunks] = jnp.zeros((32, 128), BF16)
        weight_grad(layer, g)
        stage[layer] = send_row(layer)
        if layer + 1 < layers:
            stage[layer + 1] = send_depth(layer + 1, stage[layer + 1])
        if layer + 2 < layers:
            stage[layer + 2] = send_all(layer + 2, stage[layer + 2])
        if layer + 3 < layers:
            finish(layer + 3, stage[layer + 3])
        arrive(halo)
        back = backward(layer)
        if layer > 0:
            g = back * slp[layer - 1]
    stage[0] = send_depth(0, stage[0])
    stage[1] = send_all(1, stage[1])
    finish(2, stage[2])
    tmp[...] = back
    for d in range(slab):
        for b in range(16):
            ig_ref[d, :, b * 128 : (b + 1) * 128] = tmp[pl.ds(d * rows * 16 + b, rows, stride=16), :].astype(BF16)
    stage[0] = send_all(0, stage[0])
    finish(1, stage[1])
    finish(0, stage[0])
    for copy in started:
        copy.wait_send()


def solution(mesh):
    np_, nd, nr = mesh.shape["peer"], mesh.shape["depth"], mesh.shape["row"]
    nx = np_ // 2

    def body(features, labels, conv_weights, head_weights, matching):
        slab, rows, merged = features.shape
        layers = conv_weights.shape[1]
        classes = head_weights.shape[2]
        cells = slab * rows * 16
        chunk = (8 // nr, 32, 128)
        ext = (layers, slab + 4, rows + 4, 16, 128)
        vmem = pl.BlockSpec(memory_space=pltpu.VMEM)
        dma = pltpu.SemaphoreType.DMA
        scratch = [
            pltpu.VMEM(ext, BF16),
            pltpu.VMEM(ext, BF16),
            pltpu.VMEM((9, 2, 4, layers * 32, 128), BF16),
            pltpu.VMEM((layers * 32, 896), F32),
            pltpu.VMEM((cells, 128), F32),
            pltpu.VMEM((layers, cells, 128), F32),
            pltpu.VMEM((128, 512), BF16),
            pltpu.VMEM((slab, 128, 512), BF16),
            pltpu.VMEM((nx, 32, 128), BF16),
            pltpu.VMEM((slab, 32, 128), BF16),
            pltpu.VMEM((slab, 32, 128), BF16),
            pltpu.VMEM((nx, slab, rows * 16, 128), BF16),
            pltpu.VMEM((slab, rows * 16, 128), BF16),
            pltpu.VMEM((slab, rows * 16, 128), BF16),
            pltpu.VMEM((slab, rows * 16, 512), F32),
            pltpu.VMEM((layers, nr) + chunk, BF16),
            pltpu.VMEM((layers, nr) + chunk, BF16),
            pltpu.VMEM((layers, nd) + chunk, BF16),
            pltpu.VMEM((layers, nr) + chunk, BF16),
            dma((2 * layers, 8)), dma((2 * layers, 8)),
            dma((nx,)), dma((nx,)),
            dma((nx,)), dma((nx,)),
            dma((2,)), dma((2,)),
            dma((layers, nr)), dma((layers, nr)),
            dma((layers, nd)), dma((layers, nd)),
            dma((layers, nr)), dma((layers, nr)),
        ]
        sizes = (nx, nd, nr, slab, rows, classes, layers)
        cg, hg, ig = pl.pallas_call(
            functools.partial(kernel, sizes),
            out_shape=(
                jax.ShapeDtypeStruct((layers, 32, 27 * 32), F32),
                jax.ShapeDtypeStruct((32, classes), F32),
                jax.ShapeDtypeStruct((slab, rows, merged), BF16),
            ),
            in_specs=[vmem, vmem, vmem, vmem, pl.BlockSpec(memory_space=pltpu.SMEM)],
            out_specs=(vmem, vmem, vmem),
            scratch_shapes=scratch,
            compiler_params=pltpu.CompilerParams(collective_id=0, has_side_effects=True),
        )(
            features,
            labels,
            conv_weights[0].transpose(0, 2, 1),
            head_weights[0],
            matching,
        )
        return cg.transpose(0, 2, 1)[None], hg[None], ig[None]

    return jax.shard_map(
        body,
        mesh=mesh,
        in_specs=(
            P("depth", "row", None),
            P("depth", "row", None),
            P("peer", None, None, None),
            P("peer", None, None),
            P("depth", None),
        ),
        out_specs=(
            P("peer", None, None, None),
            P("peer", None, None),
            P("peer", "depth", "row", None),
        ),
        check_vma=False,
    )
```

```python
import functools

import jax
import jax.numpy as jnp
from jax import lax
from jax.experimental import pallas as pl
from jax.experimental.pallas import tpu as pltpu
from jax.sharding import PartitionSpec as P

MESH = pl.DeviceIdType.MESH
F32 = jnp.float32
BF16 = jnp.bfloat16
OFFSETS = [(i, j) for i in range(3) for j in range(3)]
NEIGHBOURS = [(1, 1), (1, -1), (-1, 1), (-1, -1), (1, 0), (-1, 0), (0, 1), (0, -1)]


def nt(a, b):
    return lax.dot_general(a, b, (((1,), (1,)), ((), ())), preferred_element_type=F32)


def nn(a, b):
    return lax.dot_general(a, b, (((1,), (0,)), ((), ())), preferred_element_type=F32)


def slope(pre):
    s = 1.0 / (1.0 + jnp.exp(-pre))
    return s * (1.0 + pre * (1.0 - s))


def kernel(
    sizes,
    x_any, lab_any, w_any, head_any, match_any,
    cg_any, hg_any, ig_any,
    x_ref, lab_ref, w_ref, head_ref, match_ref, cg_ref, hg_ref, ig_ref,
    xh, gh, xo, go, wt, wpad, tmp, slo, slw, hcat, tcat, hd, hzin, hzout, hall, zin, zout, part,
    pk, rsin, dep, fin,
    in_s, out_s, halo_s, halo_r, hx_s, hx_r, ax_s, ax_r, z_s, z_r, rs_s, rs_r, dp_s, dp_r, ag_s, ag_r,
):
    nx, nd, nr, slab, rows, classes, layers = sizes
    cells = slab * rows * 16
    plane = rows * 16
    own_p, own_r = slice(2, slab + 2), slice(2, rows + 2)
    peer = lax.axis_index("peer")
    depth = lax.axis_index("depth")
    row = lax.axis_index("row")
    xpos, zhalf = lax.div(peer, 2), lax.rem(peer, 2)
    zpos = zhalf * nd + depth

    def near(dp, dr):
        where = {}
        if dr:
            where["row"] = lax.rem(row + dr + nr, nr)
        if dp:
            z = lax.rem(zpos + dp + 2 * nd, 2 * nd)
            where["peer"] = 2 * xpos + lax.div(z, nd)
            where["depth"] = lax.rem(z, nd)
        return where

    def x_mate(s):
        return {"peer": 2 * lax.rem(xpos + s, nx) + zhalf}

    z_mate = {"peer": 2 * xpos + (1 - zhalf)}

    def row_mate(s):
        return {"row": lax.rem(row + s, nr)}

    def depth_mate(s):
        return {"depth": lax.rem(depth + s, nd)}

    loads = [
        pltpu.make_async_copy(src, dst, in_s.at[n])
        for n, (src, dst) in enumerate(
            [(x_any, x_ref), (head_any, head_ref), (w_any, w_ref), (lab_any, lab_ref), (match_any, match_ref)]
        )
    ]
    for load in loads:
        load.start()

    mates = [near(*step) for step in NEIGHBOURS] + [near(2, 0), near(-2, 0)]
    mates += [x_mate(s) for s in range(1, nx)]
    mates += [row_mate(s) for s in range(2, nr - 1)]
    barrier = pltpu.get_barrier_semaphore()
    for mate in mates:
        pl.semaphore_signal(barrier, inc=1, device_id=mate, device_id_type=MESH)

    started = []

    def remote(src, dst, send, recv, mate):
        return pltpu.make_async_remote_copy(
            src_ref=src, dst_ref=dst, send_sem=send, recv_sem=recv, device_id=mate, device_id_type=MESH
        )

    def start(copies):
        for copy in copies:
            copy.start()
        started.extend(copies)
        return copies

    def arrive(copies):
        for copy in copies:
            copy.wait_recv()

    loads[0].wait()
    for d in range(slab):
        for b in range(16):
            tmp[pl.ds(d * plane + b, rows, stride=16), :] = x_ref[d, :, b * 128 : (b + 1) * 128].astype(F32)
    xh[0, own_p, own_r] = tmp[...].reshape(slab, rows, 16, 128).astype(BF16)

    loads[1].wait()
    tmp[0:32, :] = jnp.zeros((32, 128), F32)
    tmp[0:32, 0:classes] = head_ref[...].astype(F32)
    head = tmp[0:32, :].astype(BF16)
    hd[xpos] = head

    pl.semaphore_wait(barrier, len(mates))

    def halo_copies(buf, at, ex):
        copies = []
        for n, (dp, dr) in enumerate(NEIGHBOURS):
            if dp == 0:
                src_p, dst_p = pl.ds(2, slab), pl.ds(2, slab)
            elif dp == 1:
                src_p = pl.ds(slab, 2)
                dst_p = pl.ds(jnp.where(depth == nd - 1, slab + 4, 0), 2)
            else:
                src_p = pl.ds(2, 2)
                dst_p = pl.ds(jnp.where(depth == 0, slab + 6, slab + 2), 2)
            if dr == 0:
                src_r, dst_r = pl.ds(2, rows), pl.ds(2, rows)
            elif dr == 1:
                src_r = pl.ds(rows, 2)
                dst_r = pl.ds(jnp.where(row == nr - 1, rows + 4, 0), 2)
            else:
                src_r = pl.ds(2, 2)
                dst_r = pl.ds(jnp.where(row == 0, rows + 6, rows + 2), 2)
            copies.append(
                remote(
                    buf.at[at, src_p, src_r], buf.at[at, dst_p, dst_r],
                    halo_s.at[ex, n], halo_r.at[ex, n], near(dp, dr),
                )
            )
        return copies

    halo = start(halo_copies(xh, 0, 0))
    head_x = start(
        [remote(hd.at[xpos], hd.at[xpos], hx_s.at[s], hx_r.at[s], x_mate(s)) for s in range(1, nx)]
    )

    def clear_wide(buf, at):
        zero_p = jnp.zeros((2, rows + 4, 16, 128), BF16)
        buf[at, pl.ds(jnp.where(depth == 0, 0, slab + 4), 2), 0 : rows + 4] = zero_p
        buf[at, pl.ds(jnp.where(depth == nd - 1, slab + 2, slab + 6), 2), 0 : rows + 4] = zero_p
        zero_r = jnp.zeros((slab + 4, 2, 16, 128), BF16)
        buf[at, 0 : slab + 4, pl.ds(jnp.where(row == 0, 0, rows + 4), 2)] = zero_r
        buf[at, 0 : slab + 4, pl.ds(jnp.where(row == nr - 1, rows + 2, rows + 6), 2)] = zero_r

    def put_near(buf, at, value):
        buf[at, 0 : slab + 2, 0 : rows + 2] = value.astype(BF16)
        zero_p = jnp.zeros((1, rows + 2, 16, 128), BF16)
        buf[at, pl.ds(jnp.where(depth == 0, 0, slab + 2), 1), 0 : rows + 2] = zero_p
        buf[at, pl.ds(jnp.where(depth == nd - 1, slab + 1, slab + 3), 1), 0 : rows + 2] = zero_p
        zero_r = jnp.zeros((slab + 2, 1, 16, 128), BF16)
        buf[at, 0 : slab + 2, pl.ds(jnp.where(row == 0, 0, rows + 2), 1)] = zero_r
        buf[at, 0 : slab + 2, pl.ds(jnp.where(row == nr - 1, rows + 1, rows + 3), 1)] = zero_r

    for at in range(2):
        clear_wide(xh, at)
        clear_wide(gh, at)
    hcat[...] = jnp.zeros_like(hcat)
    tcat[...] = jnp.zeros_like(tcat)
    for a in range(4):
        hcat[a * 32 : (a + 1) * 32, a * 128 : (a + 1) * 128] = head

    lane = lax.broadcasted_iota(jnp.int32, (1, 16, 128), 2)
    block = lax.broadcasted_iota(jnp.int32, (1, 16, 128), 1)
    low = lane < 64
    inside = jnp.where(low, block, 15 - block) > 0

    def spill(y, shape):
        e = y[:, 128:].reshape(-1, 16, 128)
        moved = jnp.where(low, pltpu.roll(e, 1, 1), pltpu.roll(e, 15, 1))
        return (y[:, :128].reshape(-1, 16, 128) + jnp.where(inside, moved, 0.0)).reshape(*shape, 16, 128)

    loads[2].wait()
    wpad[:, 0 : 27 * 32] = w_ref[...].reshape(layers * 32, 27 * 32).astype(F32)
    wt[:, 1, 1:3] = jnp.zeros((9, 2, layers * 32, 128), BF16)
    group = lax.div(lax.broadcasted_iota(jnp.int32, (layers * 32, 128), 1), 32)

    def rolled(v, groups):
        shift = (groups * 32) % 128
        return v if shift == 0 else pltpu.roll(v, shift, 1)

    for ij in range(9):
        blk = None
        for k in range(3):
            t, g = divmod(3 * ij + k, 4)
            piece = rolled(wpad[:, t * 128 : (t + 1) * 128], k - g)
            blk = piece if blk is None else jnp.where(group == k, piece, blk)
        r0 = rolled(blk, -1)
        wt[ij, 0, 0] = jnp.where(group < 2, r0, 0.0).astype(BF16)
        wt[ij, 1, 0] = jnp.where(group == 3, r0, 0.0).astype(BF16)
        wt[ij, 0, 1] = jnp.where(group < 3, blk, 0.0).astype(BF16)
        wt[ij, 0, 2] = jnp.where(group > 0, rolled(blk, 1), 0.0).astype(BF16)
        r3 = rolled(blk, 2)
        wt[ij, 0, 3] = jnp.where(group > 1, r3, 0.0).astype(BF16)
        wt[ij, 1, 3] = jnp.where(group == 0, r3, 0.0).astype(BF16)

    def weights(layer, ij, half):
        return wt[ij, half, :, layer * 32 : (layer + 1) * 32, :].reshape(128, 128)

    def windows(buf, at, shape, base, order):
        return jnp.concatenate(
            [
                buf[at, base + i : base + i + shape[0], base + j : base + j + shape[1]].reshape(-1, 128)
                for i, j in order
            ],
            axis=1,
        )

    def forward(layer, cols, shape):
        band = jnp.concatenate(
            [jnp.concatenate([weights(layer, ij, 0), weights(layer, ij, 1)], axis=0) for ij in range(9)], axis=1
        )
        return spill(nt(cols, band), shape)

    def backward(layer, cols, shape):
        band = jnp.concatenate(
            [jnp.concatenate([weights(layer, ij, 0), weights(layer, ij, 1)], axis=1) for ij in range(9)], axis=0
        )
        return spill(nn(cols, band), shape)

    def silu(y):
        return (y / (1.0 + jnp.exp(-y))).astype(BF16)

    def slope_of(y):
        return slope(y.astype(BF16).astype(F32))

    mine = (slab, rows)
    wide = (slab + 2, rows + 2)
    mirrored = [(2 - i, 2 - j) for i, j in OFFSETS]

    loads[3].wait()
    loads[4].wait()

    for pair in range(2):
        arrive(halo)
        y = forward(2 * pair, windows(xh, pair, wide, 0, OFFSETS), wide)
        put_near(xo, pair, silu(y))
        y2 = forward(2 * pair + 1, windows(xo, pair, mine, 0, OFFSETS), mine)
        act = silu(y2)
        if pair == 0:
            xh[1, own_p, own_r] = act
            halo = start(halo_copies(xh, 1, 1))
        else:
            for d in range(slab):
                hall[d][xpos] = act[d].reshape(plane, 128)
            act_x = [
                start(
                    [
                        remote(hall[d].at[xpos], hall[d].at[xpos], ax_s.at[d, s], ax_r.at[d, s], x_mate(s))
                        for s in X_ORDER(nx)
                    ]
                )
                for d in range(slab)
            ]
            arrive(head_x)
            for d in range(slab):
                hzout[d] = hd[lax.div(match_ref[d, 2 * xpos + (1 - zhalf)], 2)]
            head_z = start([remote(hzout, hzin, z_s.at[slab], z_r.at[slab], z_mate)])
        slw[pair] = slope_of(y)
        slo[pair] = slope_of(y2)

    hidden = act.reshape(cells, 128)

    col_class = lax.broadcasted_iota(jnp.int32, (plane, 128), 1)
    real = col_class < classes
    spread_r = lax.broadcasted_iota(jnp.int32, (cells, slab * rows), 0)
    spread_c = lax.broadcasted_iota(jnp.int32, (cells, slab * rows), 1)
    spread = jnp.where(lax.div(spread_r, 16) == spread_c, 1.0, 0.0).astype(BF16)
    lab = nn(spread, lab_ref[...].reshape(slab * rows, 64).astype(F32).astype(BF16))
    vox = lax.broadcasted_iota(jnp.int32, (cells, 64), 1)
    own = lax.rem(lax.broadcasted_iota(jnp.int32, (cells, 64), 0), 16)
    lab = jnp.where(lax.div(vox, 4) == own, lab, 0.0).astype(BF16)
    pick_r = lax.broadcasted_iota(jnp.int32, (64, 512), 0)
    pick_c = lax.broadcasted_iota(jnp.int32, (64, 512), 1)
    pick = jnp.where(lax.rem(pick_r, 4) == lax.div(pick_c, 128), 1.0, 0.0).astype(BF16)
    class_of = nn(lab, pick)

    def softmax(act_plane, heads):
        logits = nn(act_plane, heads)
        out = []
        for a in range(4):
            ex = jnp.where(real, jnp.exp(logits[:, a * 128 : (a + 1) * 128]), 0.0)
            out.append(ex / jnp.sum(ex, axis=1, keepdims=True))
        return out

    col_f = col_class.astype(F32)
    for d in range(slab):
        probs = softmax(hidden[d * plane : (d + 1) * plane], hcat[...])
        for a in range(4):
            mark = jnp.where(class_of[d * plane : (d + 1) * plane, a * 128 : (a + 1) * 128] == col_f, 0.5, 0.0)
            part[d, :, a * 128 : (a + 1) * 128] = probs[a] - mark

    act_z = []
    for d in range(slab):
        arrive(act_x[d])
        zout[d] = hall[d][lax.div(match_ref[d, 2 * xpos + (1 - zhalf)], 2)]
        act_z.append(start([remote(zout.at[d], zin.at[d], z_s.at[d], z_r.at[d], z_mate)]))
    arrive(head_z)
    grad_rows = []
    for d in range(slab):
        source = match_ref[d, peer]
        near_half = lax.rem(source, 2) == zhalf
        near_at = lax.div(source, 2)
        target_head = jnp.where(near_half, hd[near_at].astype(F32), hzin[d].astype(F32)).astype(BF16)
        for a in range(4):
            tcat[d, a * 32 : (a + 1) * 32, a * 128 : (a + 1) * 128] = target_head
        arrive(act_z[d])
        target_act = jnp.where(near_half, hall[d][near_at].astype(F32), zin[d].astype(F32)).astype(BF16)
        target = softmax(target_act, tcat[d])
        grad_rows.append(
            jnp.concatenate(
                [
                    (part[d, :, a * 128 : (a + 1) * 128] - 0.5 * target[a].astype(BF16).astype(F32)).astype(BF16)
                    for a in range(4)
                ],
                axis=1,
            )
        )
    dlogits = jnp.concatenate(grad_rows, axis=0)
    g = nt(dlogits, hcat[...]).reshape(slab, rows, 16, 128) * slo[1]

    group32 = lax.div(lax.broadcasted_iota(jnp.int32, (32, 128), 1), 32)
    group288 = lax.div(lax.broadcasted_iota(jnp.int32, (288, 128), 1), 32)
    own_chunks = 8 // nr
    from_next = lane < 32
    from_last = lane >= 96

    def weight_grad(layer, g, cols):
        g = g.reshape(-1, 16, 128)
        ahead = jnp.where(from_next & (block < 15), pltpu.roll(g, 15, 1), 0.0)
        edge = jnp.where(from_last & (block > 0), pltpu.roll(g, 1, 1), ahead)
        both = jnp.concatenate([g.reshape(cells, 128), edge.reshape(cells, 128)], axis=1).astype(BF16).T
        prod = nn(both, cols)

        def take(at):
            return jnp.concatenate([prod[at : at + 32, ij * 128 : (ij + 1) * 128] for ij in range(9)], axis=0)

        s0 = jnp.where(group288 == 3, take(128), take(0))
        s3 = jnp.where(group288 == 0, take(224), take(96))
        total = take(32) + pltpu.roll(s0, 32, 1) + pltpu.roll(take(64), 96, 1) + pltpu.roll(s3, 64, 1)
        for t in range(7):
            tile = None
            ks = [(gr, *divmod(4 * t + gr, 3)) for gr in range(4) if 4 * t + gr < 27]
            for ij in sorted({ij for _, ij, _ in ks}):
                first = [(gr, k) for gr, at, k in ks if at == ij][0]
                moved = rolled(total[ij * 32 : (ij + 1) * 32], first[0] - first[1])
                tile = moved if tile is None else jnp.where(group32 >= first[0], moved, tile)
            pk[layer, t // own_chunks, t % own_chunks] = tile.astype(BF16)
        if layer < layers - 1:
            pk[layer, 7 // own_chunks, 7 % own_chunks] = jnp.zeros((32, 128), BF16)

    def span(layer_set):
        return pl.ds(layer_set[0], len(layer_set)), layer_set[0]

    def send_row(layer_set):
        at, n = span(layer_set)
        return start(
            [
                remote(pk.at[at, lax.rem(row + s, nr)], rsin.at[at, s], rs_s.at[n, s], rs_r.at[n, s], row_mate(s))
                for s in range(1, nr)
            ]
        )

    def send_depth(layer_set, copies):
        arrive(copies)
        at, n = span(layer_set)
        for layer in layer_set:
            total = pk[layer, row].astype(F32)
            for s in range(1, nr):
                total = total + rsin[layer, s].astype(F32)
            dep[layer, depth] = total.astype(BF16)
        return start(
            [
                remote(dep.at[at, depth], dep.at[at, depth], dp_s.at[n, s], dp_r.at[n, s], depth_mate(s))
                for s in range(1, nd)
            ]
        )

    def send_all(layer_set, copies):
        arrive(copies)
        at, n = span(layer_set)
        for layer in layer_set:
            total = dep[layer, 0].astype(F32)
            for s in range(1, nd):
                total = total + dep[layer, s].astype(F32)
            fin[layer, row] = total.astype(BF16)
        return start(
            [
                remote(fin.at[at, row], fin.at[at, row], ag_s.at[n, s], ag_r.at[n, s], row_mate(s))
                for s in range(1, nr)
            ]
        )

    stores = []

    def store(src, dst):
        copy = pltpu.make_async_copy(src, dst, out_s.at[len(stores)])
        copy.start()
        stores.append(copy)

    def finish(layer_set, copies):
        arrive(copies)
        at, _ = span(layer_set)
        for layer in layer_set:
            for t in range(7):
                lanes = min(128, 27 * 32 - t * 128)
                cg_ref[layer, :, t * 128 : t * 128 + lanes] = fin[layer, t // own_chunks, t % own_chunks].astype(F32)[:, :lanes]
            if layer == layers - 1:
                hg_ref[...] = fin[layer, 7 // own_chunks, 7 % own_chunks].astype(F32)[:, :classes]
                store(hg_ref, hg_any)
        store(cg_ref.at[at], cg_any.at[at])

    gh[1, own_p, own_r] = g.astype(BF16)
    halo = start(halo_copies(gh, 1, 3))
    wide_heads = nn(hidden.T, dlogits)
    heads = wide_heads[0:32, 0:128]
    for a in range(1, 4):
        heads = heads + wide_heads[a * 32 : (a + 1) * 32, a * 128 : (a + 1) * 128]
    pk[3, 7 // own_chunks, 7 % own_chunks] = heads.astype(BF16)
    weight_grad(3, g, windows(xo, 1, mine, 0, OFFSETS))
    first = send_row([3])
    arrive(halo)
    g3 = backward(3, windows(gh, 1, wide, 0, mirrored), wide) * slw[1]
    put_near(go, 1, g3)
    g2 = backward(2, windows(go, 1, mine, 0, mirrored), mine) * slo[0]
    gh[0, own_p, own_r] = g2.astype(BF16)
    halo = start(halo_copies(gh, 0, 2))
    weight_grad(2, g3[1 : slab + 1, 1 : rows + 1], windows(xh, 1, mine, 1, OFFSETS))
    weight_grad(1, g2, windows(xo, 0, mine, 0, OFFSETS))
    second = send_row([1, 2])
    first = send_depth([3], first)
    arrive(halo)
    g1 = backward(1, windows(gh, 0, wide, 0, mirrored), wide) * slw[0]
    put_near(go, 0, g1)
    weight_grad(0, g1[1 : slab + 1, 1 : rows + 1], windows(xh, 0, mine, 1, OFFSETS))
    last = send_row([0])
    second = send_depth([1, 2], second)
    first = send_all([3], first)
    back = backward(0, windows(go, 0, mine, 0, mirrored), mine)
    tmp[...] = back.reshape(cells, 128)
    for d in range(slab):
        for b in range(16):
            ig_ref[d, :, b * 128 : (b + 1) * 128] = tmp[pl.ds(d * plane + b, rows, stride=16), :].astype(BF16)
    store(ig_ref, ig_any)
    last = send_depth([0], last)
    second = send_all([1, 2], second)
    finish([3], first)
    last = send_all([0], last)
    finish([1, 2], second)
    for copy in started:
        copy.wait_send()
    finish([0], last)
    for copy in stores:
        copy.wait()


def X_ORDER(nx):
    return [s for s in (2, 1, 3) if s < nx]


def solution(mesh):
    np_, nd, nr = mesh.shape["peer"], mesh.shape["depth"], mesh.shape["row"]
    nx = np_ // 2

    def body(features, labels, conv_weights, head_weights, matching):
        slab, rows, merged = features.shape
        layers = conv_weights.shape[1]
        classes = head_weights.shape[2]
        cells = slab * rows * 16
        chunk = (8 // nr, 32, 128)
        far = (2, slab + 8, rows + 8, 16, 128)
        close = (2, slab + 4, rows + 4, 16, 128)
        anywhere = pl.BlockSpec(memory_space=pl.ANY)
        dma = pltpu.SemaphoreType.DMA
        scratch = [
            pltpu.VMEM((slab, rows, merged), BF16),
            pltpu.VMEM((slab, rows, merged // 32), jnp.int32),
            pltpu.VMEM((layers, 32, 27 * 32), BF16),
            pltpu.VMEM((32, classes), BF16),
            pltpu.SMEM((slab, np_), jnp.int32),
            pltpu.VMEM((layers, 32, 27 * 32), F32),
            pltpu.VMEM((32, classes), F32),
            pltpu.VMEM((slab, rows, merged), BF16),
            pltpu.VMEM(far, BF16),
            pltpu.VMEM(far, BF16),
            pltpu.VMEM(close, BF16),
            pltpu.VMEM(close, BF16),
            pltpu.VMEM((9, 2, 4, layers * 32, 128), BF16),
            pltpu.VMEM((layers * 32, 896), F32),
            pltpu.VMEM((cells, 128), F32),
            pltpu.VMEM((2, slab, rows, 16, 128), F32),
            pltpu.VMEM((2, slab + 2, rows + 2, 16, 128), F32),
            pltpu.VMEM((128, 512), BF16),
            pltpu.VMEM((slab, 128, 512), BF16),
            pltpu.VMEM((nx, 32, 128), BF16),
            pltpu.VMEM((slab, 32, 128), BF16),
            pltpu.VMEM((slab, 32, 128), BF16),
            [pltpu.VMEM((nx, rows * 16, 128), BF16) for _ in range(slab)],
            pltpu.VMEM((slab, rows * 16, 128), BF16),
            pltpu.VMEM((slab, rows * 16, 128), BF16),
            pltpu.VMEM((slab, rows * 16, 512), F32),
            pltpu.VMEM((layers, nr) + chunk, BF16),
            pltpu.VMEM((layers, nr) + chunk, BF16),
            pltpu.VMEM((layers, nd) + chunk, BF16),
            pltpu.VMEM((layers, nr) + chunk, BF16),
            dma((5,)), dma((5,)),
            dma((4, 8)), dma((4, 8)),
            dma((nx,)), dma((nx,)),
            dma((slab, nx)), dma((slab, nx)),
            dma((slab + 1,)), dma((slab + 1,)),
            dma((layers, nr)), dma((layers, nr)),
            dma((layers, nd)), dma((layers, nd)),
            dma((layers, nr)), dma((layers, nr)),
        ]
        sizes = (nx, nd, nr, slab, rows, classes, layers)
        cg, hg, ig = pl.pallas_call(
            functools.partial(kernel, sizes),
            out_shape=(
                jax.ShapeDtypeStruct((layers, 32, 27 * 32), F32),
                jax.ShapeDtypeStruct((32, classes), F32),
                jax.ShapeDtypeStruct((slab, rows, merged), BF16),
            ),
            in_specs=[anywhere] * 5,
            out_specs=(anywhere,) * 3,
            scratch_shapes=scratch,
            compiler_params=pltpu.CompilerParams(collective_id=0, has_side_effects=True),
        )(
            features,
            labels,
            conv_weights[0].transpose(0, 2, 1),
            head_weights[0],
            matching,
        )
        return cg.transpose(0, 2, 1)[None], hg[None], ig[None]

    return jax.shard_map(
        body,
        mesh=mesh,
        in_specs=(
            P("depth", "row", None),
            P("depth", "row", None),
            P("peer", None, None, None),
            P("peer", None, None),
            P("depth", None),
        ),
        out_specs=(
            P("peer", None, None, None),
            P("peer", None, None),
            P("peer", "depth", "row", None),
        ),
        check_vma=False,
    )
```

```python
import functools

import jax
import jax.numpy as jnp
from jax import lax
from jax.experimental import pallas as pl
from jax.experimental.pallas import tpu as pltpu
from jax.sharding import PartitionSpec as P

MESH = pl.DeviceIdType.MESH
F32 = jnp.float32
BF16 = jnp.bfloat16
OFFSETS = [(i, j) for i in range(3) for j in range(3)]
NEIGHBOURS = [(1, 1), (1, -1), (-1, 1), (-1, -1), (1, 0), (-1, 0), (0, 1), (0, -1)]


def nt(a, b):
    return lax.dot_general(a, b, (((1,), (1,)), ((), ())), preferred_element_type=F32)


def nn(a, b):
    return lax.dot_general(a, b, (((1,), (0,)), ((), ())), preferred_element_type=F32)


def slope(pre):
    s = 1.0 / (1.0 + jnp.exp(-pre))
    return s * (1.0 + pre * (1.0 - s))


def kernel(
    sizes,
    x_any, lab_any, w_any, head_any, match_any,
    cg_ref, hg_ref, ig_ref,
    x_ref, lab_ref, w_ref, head_ref, match_ref,
    xh, gh, xo, go, wt, wpad, tmp, slo, slw, hcat, tcat, hd, hzin, hzout, hall, zin, zout, part,
    pk, rsin, dep, fin,
    in_s, halo_s, halo_r, hx_s, hx_r, ax_s, ax_r, z_s, z_r, rs_s, rs_r, dp_s, dp_r, ag_s, ag_r,
):
    nx, nd, nr, slab, rows, classes, layers = sizes
    cells = slab * rows * 16
    plane = rows * 16
    own_p, own_r = slice(2, slab + 2), slice(2, rows + 2)
    peer = lax.axis_index("peer")
    depth = lax.axis_index("depth")
    row = lax.axis_index("row")
    xpos, zhalf = lax.div(peer, 2), lax.rem(peer, 2)
    zpos = zhalf * nd + depth

    def near(dp, dr):
        where = {}
        if dr:
            where["row"] = lax.rem(row + dr + nr, nr)
        if dp:
            z = lax.rem(zpos + dp + 2 * nd, 2 * nd)
            where["peer"] = 2 * xpos + lax.div(z, nd)
            where["depth"] = lax.rem(z, nd)
        return where

    def x_mate(s):
        return {"peer": 2 * lax.rem(xpos + s, nx) + zhalf}

    z_mate = {"peer": 2 * xpos + (1 - zhalf)}

    def row_mate(s):
        return {"row": lax.rem(row + s, nr)}

    def depth_mate(s):
        return {"depth": lax.rem(depth + s, nd)}

    loads = [
        pltpu.make_async_copy(src, dst, in_s.at[n])
        for n, (src, dst) in enumerate(
            [(x_any, x_ref), (head_any, head_ref), (w_any, w_ref), (lab_any, lab_ref), (match_any, match_ref)]
        )
    ]
    for load in loads:
        load.start()

    mates = [near(*step) for step in NEIGHBOURS] + [near(2, 0), near(-2, 0)]
    mates += [x_mate(s) for s in range(1, nx)]
    mates += [row_mate(s) for s in range(2, nr - 1)]
    barrier = pltpu.get_barrier_semaphore()
    for mate in mates:
        pl.semaphore_signal(barrier, inc=1, device_id=mate, device_id_type=MESH)

    started = []

    def remote(src, dst, send, recv, mate):
        return pltpu.make_async_remote_copy(
            src_ref=src, dst_ref=dst, send_sem=send, recv_sem=recv, device_id=mate, device_id_type=MESH
        )

    def start(copies):
        for copy in copies:
            copy.start()
        started.extend(copies)
        return copies

    def arrive(copies):
        for copy in copies:
            copy.wait_recv()

    loads[0].wait()
    for d in range(slab):
        for b in range(16):
            tmp[pl.ds(d * plane + b, rows, stride=16), :] = x_ref[d, :, b * 128 : (b + 1) * 128].astype(F32)
    xh[0, own_p, own_r] = tmp[...].reshape(slab, rows, 16, 128).astype(BF16)

    loads[1].wait()
    tmp[0:32, :] = jnp.zeros((32, 128), F32)
    tmp[0:32, 0:classes] = head_ref[...].astype(F32)
    head = tmp[0:32, :].astype(BF16)
    hd[xpos] = head

    pl.semaphore_wait(barrier, len(mates))

    def halo_copies(buf, at, ex):
        copies = []
        for n, (dp, dr) in enumerate(NEIGHBOURS):
            if dp == 0:
                src_p, dst_p = pl.ds(2, slab), pl.ds(2, slab)
            elif dp == 1:
                src_p = pl.ds(slab, 2)
                dst_p = pl.ds(jnp.where(depth == nd - 1, slab + 4, 0), 2)
            else:
                src_p = pl.ds(2, 2)
                dst_p = pl.ds(jnp.where(depth == 0, slab + 6, slab + 2), 2)
            if dr == 0:
                src_r, dst_r = pl.ds(2, rows), pl.ds(2, rows)
            elif dr == 1:
                src_r = pl.ds(rows, 2)
                dst_r = pl.ds(jnp.where(row == nr - 1, rows + 4, 0), 2)
            else:
                src_r = pl.ds(2, 2)
                dst_r = pl.ds(jnp.where(row == 0, rows + 6, rows + 2), 2)
            copies.append(
                remote(
                    buf.at[at, src_p, src_r], buf.at[at, dst_p, dst_r],
                    halo_s.at[ex, n], halo_r.at[ex, n], near(dp, dr),
                )
            )
        return copies

    halo = start(halo_copies(xh, 0, 0))
    head_x = start(
        [remote(hd.at[xpos], hd.at[xpos], hx_s.at[s], hx_r.at[s], x_mate(s)) for s in range(1, nx)]
    )

    def clear_wide(buf, at):
        zero_p = jnp.zeros((2, rows + 4, 16, 128), BF16)
        buf[at, pl.ds(jnp.where(depth == 0, 0, slab + 4), 2), 0 : rows + 4] = zero_p
        buf[at, pl.ds(jnp.where(depth == nd - 1, slab + 2, slab + 6), 2), 0 : rows + 4] = zero_p
        zero_r = jnp.zeros((slab + 4, 2, 16, 128), BF16)
        buf[at, 0 : slab + 4, pl.ds(jnp.where(row == 0, 0, rows + 4), 2)] = zero_r
        buf[at, 0 : slab + 4, pl.ds(jnp.where(row == nr - 1, rows + 2, rows + 6), 2)] = zero_r

    def put_near(buf, at, value):
        buf[at, 0 : slab + 2, 0 : rows + 2] = value.astype(BF16)
        zero_p = jnp.zeros((1, rows + 2, 16, 128), BF16)
        buf[at, pl.ds(jnp.where(depth == 0, 0, slab + 2), 1), 0 : rows + 2] = zero_p
        buf[at, pl.ds(jnp.where(depth == nd - 1, slab + 1, slab + 3), 1), 0 : rows + 2] = zero_p
        zero_r = jnp.zeros((slab + 2, 1, 16, 128), BF16)
        buf[at, 0 : slab + 2, pl.ds(jnp.where(row == 0, 0, rows + 2), 1)] = zero_r
        buf[at, 0 : slab + 2, pl.ds(jnp.where(row == nr - 1, rows + 1, rows + 3), 1)] = zero_r

    for at in range(2):
        clear_wide(xh, at)
        clear_wide(gh, at)
    hcat[...] = jnp.zeros_like(hcat)
    tcat[...] = jnp.zeros_like(tcat)
    for a in range(4):
        hcat[a * 32 : (a + 1) * 32, a * 128 : (a + 1) * 128] = head

    lane = lax.broadcasted_iota(jnp.int32, (1, 16, 128), 2)
    block = lax.broadcasted_iota(jnp.int32, (1, 16, 128), 1)
    low = lane < 64
    inside = jnp.where(low, block, 15 - block) > 0

    def spill(y, shape):
        e = y[:, 128:].reshape(-1, 16, 128)
        moved = jnp.where(low, pltpu.roll(e, 1, 1), pltpu.roll(e, 15, 1))
        return (y[:, :128].reshape(-1, 16, 128) + jnp.where(inside, moved, 0.0)).reshape(*shape, 16, 128)

    loads[2].wait()
    wpad[:, 0 : 27 * 32] = w_ref[...].reshape(layers * 32, 27 * 32).astype(F32)
    wt[:, 1, 1:3] = jnp.zeros((9, 2, layers * 32, 128), BF16)
    group = lax.div(lax.broadcasted_iota(jnp.int32, (layers * 32, 128), 1), 32)

    def rolled(v, groups):
        shift = (groups * 32) % 128
        return v if shift == 0 else pltpu.roll(v, shift, 1)

    for ij in range(9):
        blk = None
        for k in range(3):
            t, g = divmod(3 * ij + k, 4)
            piece = rolled(wpad[:, t * 128 : (t + 1) * 128], k - g)
            blk = piece if blk is None else jnp.where(group == k, piece, blk)
        r0 = rolled(blk, -1)
        wt[ij, 0, 0] = jnp.where(group < 2, r0, 0.0).astype(BF16)
        wt[ij, 1, 0] = jnp.where(group == 3, r0, 0.0).astype(BF16)
        wt[ij, 0, 1] = jnp.where(group < 3, blk, 0.0).astype(BF16)
        wt[ij, 0, 2] = jnp.where(group > 0, rolled(blk, 1), 0.0).astype(BF16)
        r3 = rolled(blk, 2)
        wt[ij, 0, 3] = jnp.where(group > 1, r3, 0.0).astype(BF16)
        wt[ij, 1, 3] = jnp.where(group == 0, r3, 0.0).astype(BF16)

    def weights(layer, ij, half):
        return wt[ij, half, :, layer * 32 : (layer + 1) * 32, :].reshape(128, 128)

    def windows(buf, at, shape, base, order):
        return jnp.concatenate(
            [
                buf[at, base + i : base + i + shape[0], base + j : base + j + shape[1]].reshape(-1, 128)
                for i, j in order
            ],
            axis=1,
        )

    def forward(layer, cols, shape):
        band = jnp.concatenate(
            [jnp.concatenate([weights(layer, ij, 0), weights(layer, ij, 1)], axis=0) for ij in range(9)], axis=1
        )
        return spill(nt(cols, band), shape)

    def backward(layer, cols, shape):
        band = jnp.concatenate(
            [jnp.concatenate([weights(layer, ij, 0), weights(layer, ij, 1)], axis=1) for ij in range(9)], axis=0
        )
        return spill(nn(cols, band), shape)

    def silu(y):
        return (y / (1.0 + jnp.exp(-y))).astype(BF16)

    def slope_of(y):
        return slope(y.astype(BF16).astype(F32))

    mine = (slab, rows)
    wide = (slab + 2, rows + 2)
    mirrored = [(2 - i, 2 - j) for i, j in OFFSETS]

    loads[3].wait()
    loads[4].wait()

    for pair in range(2):
        arrive(halo)
        y = forward(2 * pair, windows(xh, pair, wide, 0, OFFSETS), wide)
        put_near(xo, pair, silu(y))
        y2 = forward(2 * pair + 1, windows(xo, pair, mine, 0, OFFSETS), mine)
        act = silu(y2)
        if pair == 0:
            xh[1, own_p, own_r] = act
            halo = start(halo_copies(xh, 1, 1))
        else:
            for d in range(slab):
                hall[d][xpos] = act[d].reshape(plane, 128)
            act_x = [
                start(
                    [
                        remote(hall[d].at[xpos], hall[d].at[xpos], ax_s.at[d, s], ax_r.at[d, s], x_mate(s))
                        for s in X_ORDER(nx)
                    ]
                )
                for d in range(slab)
            ]
            arrive(head_x)
            for d in range(slab):
                hzout[d] = hd[lax.div(match_ref[d, 2 * xpos + (1 - zhalf)], 2)]
            head_z = start([remote(hzout, hzin, z_s.at[slab], z_r.at[slab], z_mate)])
        slw[pair] = slope_of(y)
        slo[pair] = slope_of(y2)

    hidden = act.reshape(cells, 128)

    col_class = lax.broadcasted_iota(jnp.int32, (plane, 128), 1)
    real = col_class < classes
    spread_r = lax.broadcasted_iota(jnp.int32, (cells, slab * rows), 0)
    spread_c = lax.broadcasted_iota(jnp.int32, (cells, slab * rows), 1)
    spread = jnp.where(lax.div(spread_r, 16) == spread_c, 1.0, 0.0).astype(BF16)
    lab = nn(spread, lab_ref[...].reshape(slab * rows, 64).astype(F32).astype(BF16))
    vox = lax.broadcasted_iota(jnp.int32, (cells, 64), 1)
    own = lax.rem(lax.broadcasted_iota(jnp.int32, (cells, 64), 0), 16)
    lab = jnp.where(lax.div(vox, 4) == own, lab, 0.0).astype(BF16)
    pick_r = lax.broadcasted_iota(jnp.int32, (64, 512), 0)
    pick_c = lax.broadcasted_iota(jnp.int32, (64, 512), 1)
    pick = jnp.where(lax.rem(pick_r, 4) == lax.div(pick_c, 128), 1.0, 0.0).astype(BF16)
    class_of = nn(lab, pick)

    def softmax(act_plane, heads):
        logits = nn(act_plane, heads)
        out = []
        for a in range(4):
            ex = jnp.where(real, jnp.exp(logits[:, a * 128 : (a + 1) * 128]), 0.0)
            out.append(ex / jnp.sum(ex, axis=1, keepdims=True))
        return out

    col_f = col_class.astype(F32)
    for d in range(slab):
        probs = softmax(hidden[d * plane : (d + 1) * plane], hcat[...])
        for a in range(4):
            mark = jnp.where(class_of[d * plane : (d + 1) * plane, a * 128 : (a + 1) * 128] == col_f, 0.5, 0.0)
            part[d, :, a * 128 : (a + 1) * 128] = probs[a] - mark

    act_z = []
    for d in range(slab):
        arrive(act_x[d])
        zout[d] = hall[d][lax.div(match_ref[d, 2 * xpos + (1 - zhalf)], 2)]
        act_z.append(start([remote(zout.at[d], zin.at[d], z_s.at[d], z_r.at[d], z_mate)]))
    arrive(head_z)
    grad_rows = []
    for d in range(slab):
        source = match_ref[d, peer]
        near_half = lax.rem(source, 2) == zhalf
        near_at = lax.div(source, 2)
        target_head = jnp.where(near_half, hd[near_at].astype(F32), hzin[d].astype(F32)).astype(BF16)
        for a in range(4):
            tcat[d, a * 32 : (a + 1) * 32, a * 128 : (a + 1) * 128] = target_head
        arrive(act_z[d])
        target_act = jnp.where(near_half, hall[d][near_at].astype(F32), zin[d].astype(F32)).astype(BF16)
        target = softmax(target_act, tcat[d])
        grad_rows.append(
            jnp.concatenate(
                [
                    (part[d, :, a * 128 : (a + 1) * 128] - 0.5 * target[a].astype(BF16).astype(F32)).astype(BF16)
                    for a in range(4)
                ],
                axis=1,
            )
        )
    dlogits = jnp.concatenate(grad_rows, axis=0)
    g = nt(dlogits, hcat[...]).reshape(slab, rows, 16, 128) * slo[1]

    group32 = lax.div(lax.broadcasted_iota(jnp.int32, (32, 128), 1), 32)
    group288 = lax.div(lax.broadcasted_iota(jnp.int32, (288, 128), 1), 32)
    own_chunks = 8 // nr
    from_next = lane < 32
    from_last = lane >= 96

    def weight_grad(layer, g, cols):
        g = g.reshape(-1, 16, 128)
        ahead = jnp.where(from_next & (block < 15), pltpu.roll(g, 15, 1), 0.0)
        edge = jnp.where(from_last & (block > 0), pltpu.roll(g, 1, 1), ahead)
        both = jnp.concatenate([g.reshape(cells, 128), edge.reshape(cells, 128)], axis=1).astype(BF16).T
        prod = nn(both, cols)

        def take(at):
            return jnp.concatenate([prod[at : at + 32, ij * 128 : (ij + 1) * 128] for ij in range(9)], axis=0)

        s0 = jnp.where(group288 == 3, take(128), take(0))
        s3 = jnp.where(group288 == 0, take(224), take(96))
        total = take(32) + pltpu.roll(s0, 32, 1) + pltpu.roll(take(64), 96, 1) + pltpu.roll(s3, 64, 1)
        for t in range(7):
            tile = None
            ks = [(gr, *divmod(4 * t + gr, 3)) for gr in range(4) if 4 * t + gr < 27]
            for ij in sorted({ij for _, ij, _ in ks}):
                first = [(gr, k) for gr, at, k in ks if at == ij][0]
                moved = rolled(total[ij * 32 : (ij + 1) * 32], first[0] - first[1])
                tile = moved if tile is None else jnp.where(group32 >= first[0], moved, tile)
            pk[layer, t // own_chunks, t % own_chunks] = tile.astype(BF16)
        if layer < layers - 1:
            pk[layer, 7 // own_chunks, 7 % own_chunks] = jnp.zeros((32, 128), BF16)

    def span(layer_set):
        return pl.ds(layer_set[0], len(layer_set)), layer_set[0]

    def send_row(layer_set):
        at, n = span(layer_set)
        return start(
            [
                remote(pk.at[at, lax.rem(row + s, nr)], rsin.at[at, s], rs_s.at[n, s], rs_r.at[n, s], row_mate(s))
                for s in range(1, nr)
            ]
        )

    def send_depth(layer_set, copies):
        arrive(copies)
        at, n = span(layer_set)
        for layer in layer_set:
            total = pk[layer, row].astype(F32)
            for s in range(1, nr):
                total = total + rsin[layer, s].astype(F32)
            dep[layer, depth] = total.astype(BF16)
        return start(
            [
                remote(dep.at[at, depth], dep.at[at, depth], dp_s.at[n, s], dp_r.at[n, s], depth_mate(s))
                for s in range(1, nd)
            ]
        )

    def send_all(layer_set, copies):
        arrive(copies)
        at, n = span(layer_set)
        for layer in layer_set:
            total = dep[layer, 0].astype(F32)
            for s in range(1, nd):
                total = total + dep[layer, s].astype(F32)
            fin[layer, row] = total.astype(BF16)
        return start(
            [
                remote(fin.at[at, row], fin.at[at, row], ag_s.at[n, s], ag_r.at[n, s], row_mate(s))
                for s in range(1, nr)
            ]
        )

    def finish(layer_set, copies):
        arrive(copies)
        for layer in layer_set:
            for t in range(7):
                lanes = min(128, 27 * 32 - t * 128)
                cg_ref[layer, :, t * 128 : t * 128 + lanes] = fin[layer, t // own_chunks, t % own_chunks].astype(F32)[:, :lanes]
            if layer == layers - 1:
                hg_ref[...] = fin[layer, 7 // own_chunks, 7 % own_chunks].astype(F32)[:, :classes]

    gh[1, own_p, own_r] = g.astype(BF16)
    halo = start(halo_copies(gh, 1, 3))
    wide_heads = nn(hidden.T, dlogits)
    heads = wide_heads[0:32, 0:128]
    for a in range(1, 4):
        heads = heads + wide_heads[a * 32 : (a + 1) * 32, a * 128 : (a + 1) * 128]
    pk[3, 7 // own_chunks, 7 % own_chunks] = heads.astype(BF16)
    weight_grad(3, g, windows(xo, 1, mine, 0, OFFSETS))
    first = send_row([3])
    arrive(halo)
    g3 = backward(3, windows(gh, 1, wide, 0, mirrored), wide) * slw[1]
    put_near(go, 1, g3)
    g2 = backward(2, windows(go, 1, mine, 0, mirrored), mine) * slo[0]
    gh[0, own_p, own_r] = g2.astype(BF16)
    halo = start(halo_copies(gh, 0, 2))
    weight_grad(2, g3[1 : slab + 1, 1 : rows + 1], windows(xh, 1, mine, 1, OFFSETS))
    weight_grad(1, g2, windows(xo, 0, mine, 0, OFFSETS))
    second = send_row([1, 2])
    first = send_depth([3], first)
    arrive(halo)
    g1 = backward(1, windows(gh, 0, wide, 0, mirrored), wide) * slw[0]
    put_near(go, 0, g1)
    weight_grad(0, g1[1 : slab + 1, 1 : rows + 1], windows(xh, 0, mine, 1, OFFSETS))
    last = send_row([0])
    second = send_depth([1, 2], second)
    first = send_all([3], first)
    back = backward(0, windows(go, 0, mine, 0, mirrored), mine)
    tmp[...] = back.reshape(cells, 128)
    for d in range(slab):
        for b in range(16):
            ig_ref[d, :, b * 128 : (b + 1) * 128] = tmp[pl.ds(d * plane + b, rows, stride=16), :].astype(BF16)
    last = send_depth([0], last)
    second = send_all([1, 2], second)
    finish([3], first)
    last = send_all([0], last)
    finish([1, 2], second)
    for copy in started:
        copy.wait_send()
    finish([0], last)


def write_out(cg_ref, hg_ref, ig_ref, cg_out, hg_out, ig_out, sem):
    copies = [
        pltpu.make_async_copy(src, dst, sem.at[n])
        for n, (src, dst) in enumerate([(cg_ref, cg_out), (ig_ref, ig_out), (hg_ref, hg_out)])
    ]
    for copy in copies:
        copy.start()
    for copy in copies:
        copy.wait()


def X_ORDER(nx):
    return [s for s in (2, 1, 3) if s < nx]


def solution(mesh):
    np_, nd, nr = mesh.shape["peer"], mesh.shape["depth"], mesh.shape["row"]
    nx = np_ // 2

    def body(features, labels, conv_weights, head_weights, matching):
        slab, rows, merged = features.shape
        layers = conv_weights.shape[1]
        classes = head_weights.shape[2]
        cells = slab * rows * 16
        chunk = (8 // nr, 32, 128)
        far = (2, slab + 8, rows + 8, 16, 128)
        close = (2, slab + 4, rows + 4, 16, 128)
        vmem = pl.BlockSpec(memory_space=pltpu.VMEM)
        hbm = pl.BlockSpec(memory_space=pltpu.HBM)
        dma = pltpu.SemaphoreType.DMA
        scratch = [
            pltpu.VMEM((slab, rows, merged), BF16),
            pltpu.VMEM((slab, rows, merged // 32), jnp.int32),
            pltpu.VMEM((layers, 32, 27 * 32), BF16),
            pltpu.VMEM((32, classes), BF16),
            pltpu.SMEM((slab, np_), jnp.int32),
            pltpu.VMEM(far, BF16),
            pltpu.VMEM(far, BF16),
            pltpu.VMEM(close, BF16),
            pltpu.VMEM(close, BF16),
            pltpu.VMEM((9, 2, 4, layers * 32, 128), BF16),
            pltpu.VMEM((layers * 32, 896), F32),
            pltpu.VMEM((cells, 128), F32),
            pltpu.VMEM((2, slab, rows, 16, 128), F32),
            pltpu.VMEM((2, slab + 2, rows + 2, 16, 128), F32),
            pltpu.VMEM((128, 512), BF16),
            pltpu.VMEM((slab, 128, 512), BF16),
            pltpu.VMEM((nx, 32, 128), BF16),
            pltpu.VMEM((slab, 32, 128), BF16),
            pltpu.VMEM((slab, 32, 128), BF16),
            [pltpu.VMEM((nx, rows * 16, 128), BF16) for _ in range(slab)],
            pltpu.VMEM((slab, rows * 16, 128), BF16),
            pltpu.VMEM((slab, rows * 16, 128), BF16),
            pltpu.VMEM((slab, rows * 16, 512), F32),
            pltpu.VMEM((layers, nr) + chunk, BF16),
            pltpu.VMEM((layers, nr) + chunk, BF16),
            pltpu.VMEM((layers, nd) + chunk, BF16),
            pltpu.VMEM((layers, nr) + chunk, BF16),
            dma((5,)),
            dma((4, 8)), dma((4, 8)),
            dma((nx,)), dma((nx,)),
            dma((slab, nx)), dma((slab, nx)),
            dma((slab + 1,)), dma((slab + 1,)),
            dma((layers, nr)), dma((layers, nr)),
            dma((layers, nd)), dma((layers, nd)),
            dma((layers, nr)), dma((layers, nr)),
        ]
        sizes = (nx, nd, nr, slab, rows, classes, layers)
        cg, hg, ig = pl.pallas_call(
            functools.partial(kernel, sizes),
            out_shape=(
                pltpu.VMEM((layers, 32, 27 * 32), F32),
                pltpu.VMEM((32, classes), F32),
                pltpu.VMEM((slab, rows, merged), BF16),
            ),
            in_specs=[hbm] * 5,
            out_specs=(vmem,) * 3,
            scratch_shapes=scratch,
            compiler_params=pltpu.CompilerParams(collective_id=0, has_side_effects=True, vmem_limit_bytes=40 * 2**20),
        )(
            *(
                pltpu.with_memory_space_constraint(v, pltpu.HBM)
                for v in (features, labels, conv_weights[0].transpose(0, 2, 1), head_weights[0], matching)
            )
        )
        cg, hg, ig = pl.pallas_call(
            write_out,
            out_shape=tuple(jax.ShapeDtypeStruct(v.shape, v.dtype) for v in (cg, hg, ig)),
            in_specs=[vmem] * 3,
            out_specs=(hbm,) * 3,
            scratch_shapes=[dma((3,))],
            compiler_params=pltpu.CompilerParams(vmem_limit_bytes=2**20),
        )(cg, hg, ig)
        return cg.transpose(0, 2, 1)[None], hg[None], ig[None]

    return jax.shard_map(
        body,
        mesh=mesh,
        in_specs=(
            P("depth", "row", None),
            P("depth", "row", None),
            P("peer", None, None, None),
            P("peer", None, None),
            P("depth", None),
        ),
        out_specs=(
            P("peer", None, None, None),
            P("peer", None, None),
            P("peer", "depth", "row", None),
        ),
        check_vma=False,
    )
```

```python
import functools

import jax
import jax.numpy as jnp
from jax import lax
from jax.experimental import pallas as pl
from jax.experimental.pallas import tpu as pltpu
from jax.sharding import PartitionSpec as P

MESH = pl.DeviceIdType.MESH
F32 = jnp.float32
BF16 = jnp.bfloat16
OFFSETS = [(i, j) for i in range(3) for j in range(3)]
NEIGHBOURS = [(1, 1), (1, -1), (-1, 1), (-1, -1), (1, 0), (-1, 0), (0, 1), (0, -1)]


def nt(a, b):
    return lax.dot_general(a, b, (((1,), (1,)), ((), ())), preferred_element_type=F32)


def nn(a, b):
    return lax.dot_general(a, b, (((1,), (0,)), ((), ())), preferred_element_type=F32)


def slope(pre):
    s = 1.0 / (1.0 + jnp.exp(-pre))
    return s * (1.0 + pre * (1.0 - s))


def kernel(
    sizes,
    x_any, lab_any, w_any, head_any, match_any,
    cg_ref, hg_ref, ig_ref,
    x_ref, lab_ref, w_ref, head_ref, match_ref,
    xh, gh, xo, go, wt, wpad, tmp, slo, slw, hcat, tcat, hd, hzin, hzout, hall, zin, zout, far_in, far_out, pick_in, pick_out, part,
    pk, rsin, dep, fin,
    in_s, halo_s, halo_r, hx_s, hx_r, ax_s, ax_r, z_s, z_r, bx_s, bx_r, bz_s, bz_r, rs_s, rs_r, dp_s, dp_r, ag_s, ag_r,
):
    nx, nd, nr, slab, rows, classes, layers = sizes
    cells = slab * rows * 16
    plane = rows * 16
    part_rows = plane // 2
    own_p, own_r = slice(2, slab + 2), slice(2, rows + 2)
    peer = lax.axis_index("peer")
    depth = lax.axis_index("depth")
    row = lax.axis_index("row")
    xpos, zhalf = lax.div(peer, 2), lax.rem(peer, 2)
    zpos = zhalf * nd + depth

    def near(dp, dr):
        where = {}
        if dr:
            where["row"] = lax.rem(row + dr + nr, nr)
        if dp:
            z = lax.rem(zpos + dp + 2 * nd, 2 * nd)
            where["peer"] = 2 * xpos + lax.div(z, nd)
            where["depth"] = lax.rem(z, nd)
        return where

    def x_mate(s):
        return {"peer": 2 * lax.rem(xpos + s, nx) + zhalf}

    z_mate = {"peer": 2 * xpos + (1 - zhalf)}

    def row_mate(s):
        return {"row": lax.rem(row + s, nr)}

    def depth_mate(s):
        return {"depth": lax.rem(depth + s, nd)}

    loads = [
        pltpu.make_async_copy(src, dst, in_s.at[n])
        for n, (src, dst) in enumerate(
            [(x_any, x_ref), (head_any, head_ref), (w_any, w_ref), (lab_any, lab_ref), (match_any, match_ref)]
        )
    ]
    for load in loads:
        load.start()

    mates = [near(*step) for step in NEIGHBOURS] + [near(2, 0), near(-2, 0)]
    mates += [x_mate(s) for s in range(1, nx)]
    mates += [row_mate(s) for s in range(2, nr - 1)]
    barrier = pltpu.get_barrier_semaphore()
    for mate in mates:
        pl.semaphore_signal(barrier, inc=1, device_id=mate, device_id_type=MESH)

    started = []

    def remote(src, dst, send, recv, mate):
        return pltpu.make_async_remote_copy(
            src_ref=src, dst_ref=dst, send_sem=send, recv_sem=recv, device_id=mate, device_id_type=MESH
        )

    def start(copies):
        for copy in copies:
            copy.start()
        started.extend(copies)
        return copies

    def arrive(copies):
        for copy in copies:
            copy.wait_recv()

    loads[0].wait()
    for d in range(slab):
        for b in range(16):
            tmp[pl.ds(d * plane + b, rows, stride=16), :] = x_ref[d, :, b * 128 : (b + 1) * 128].astype(F32)
    xh[0, own_p, own_r] = tmp[...].reshape(slab, rows, 16, 128).astype(BF16)

    loads[1].wait()
    tmp[0:32, :] = jnp.zeros((32, 128), F32)
    tmp[0:32, 0:classes] = head_ref[...].astype(F32)
    head = tmp[0:32, :].astype(BF16)
    hd[xpos] = head

    pl.semaphore_wait(barrier, len(mates))

    def halo_copies(buf, at, ex):
        copies = []
        for n, (dp, dr) in enumerate(NEIGHBOURS):
            if dp == 0:
                src_p, dst_p = pl.ds(2, slab), pl.ds(2, slab)
            elif dp == 1:
                src_p = pl.ds(slab, 2)
                dst_p = pl.ds(jnp.where(depth == nd - 1, slab + 4, 0), 2)
            else:
                src_p = pl.ds(2, 2)
                dst_p = pl.ds(jnp.where(depth == 0, slab + 6, slab + 2), 2)
            if dr == 0:
                src_r, dst_r = pl.ds(2, rows), pl.ds(2, rows)
            elif dr == 1:
                src_r = pl.ds(rows, 2)
                dst_r = pl.ds(jnp.where(row == nr - 1, rows + 4, 0), 2)
            else:
                src_r = pl.ds(2, 2)
                dst_r = pl.ds(jnp.where(row == 0, rows + 6, rows + 2), 2)
            copies.append(
                remote(
                    buf.at[at, src_p, src_r], buf.at[at, dst_p, dst_r],
                    halo_s.at[ex, n], halo_r.at[ex, n], near(dp, dr),
                )
            )
        return copies

    halo = start(halo_copies(xh, 0, 0))
    head_x = start(
        [remote(hd.at[xpos], hd.at[xpos], hx_s.at[s], hx_r.at[s], x_mate(s)) for s in range(1, nx)]
    )

    def clear_wide(buf, at):
        zero_p = jnp.zeros((2, rows + 4, 16, 128), BF16)
        buf[at, pl.ds(jnp.where(depth == 0, 0, slab + 4), 2), 0 : rows + 4] = zero_p
        buf[at, pl.ds(jnp.where(depth == nd - 1, slab + 2, slab + 6), 2), 0 : rows + 4] = zero_p
        zero_r = jnp.zeros((slab + 4, 2, 16, 128), BF16)
        buf[at, 0 : slab + 4, pl.ds(jnp.where(row == 0, 0, rows + 4), 2)] = zero_r
        buf[at, 0 : slab + 4, pl.ds(jnp.where(row == nr - 1, rows + 2, rows + 6), 2)] = zero_r

    def put_near(buf, at, value):
        buf[at, 0 : slab + 2, 0 : rows + 2] = value.astype(BF16)
        zero_p = jnp.zeros((1, rows + 2, 16, 128), BF16)
        buf[at, pl.ds(jnp.where(depth == 0, 0, slab + 2), 1), 0 : rows + 2] = zero_p
        buf[at, pl.ds(jnp.where(depth == nd - 1, slab + 1, slab + 3), 1), 0 : rows + 2] = zero_p
        zero_r = jnp.zeros((slab + 2, 1, 16, 128), BF16)
        buf[at, 0 : slab + 2, pl.ds(jnp.where(row == 0, 0, rows + 2), 1)] = zero_r
        buf[at, 0 : slab + 2, pl.ds(jnp.where(row == nr - 1, rows + 1, rows + 3), 1)] = zero_r

    for at in range(2):
        clear_wide(xh, at)
        clear_wide(gh, at)
    hcat[...] = jnp.zeros_like(hcat)
    tcat[...] = jnp.zeros_like(tcat)
    for a in range(4):
        hcat[a * 32 : (a + 1) * 32, a * 128 : (a + 1) * 128] = head

    lane = lax.broadcasted_iota(jnp.int32, (1, 16, 128), 2)
    block = lax.broadcasted_iota(jnp.int32, (1, 16, 128), 1)
    low = lane < 64
    inside = jnp.where(low, block, 15 - block) > 0

    def spill(y, shape):
        e = y[:, 128:].reshape(-1, 16, 128)
        moved = jnp.where(low, pltpu.roll(e, 1, 1), pltpu.roll(e, 15, 1))
        return (y[:, :128].reshape(-1, 16, 128) + jnp.where(inside, moved, 0.0)).reshape(*shape, 16, 128)

    loads[2].wait()
    wpad[:, 0 : 27 * 32] = w_ref[...].reshape(layers * 32, 27 * 32).astype(F32)
    wt[:, 1, 1:3] = jnp.zeros((9, 2, layers * 32, 128), BF16)
    group = lax.div(lax.broadcasted_iota(jnp.int32, (layers * 32, 128), 1), 32)

    def rolled(v, groups):
        shift = (groups * 32) % 128
        return v if shift == 0 else pltpu.roll(v, shift, 1)

    for ij in range(9):
        blk = None
        for k in range(3):
            t, g = divmod(3 * ij + k, 4)
            piece = rolled(wpad[:, t * 128 : (t + 1) * 128], k - g)
            blk = piece if blk is None else jnp.where(group == k, piece, blk)
        r0 = rolled(blk, -1)
        wt[ij, 0, 0] = jnp.where(group < 2, r0, 0.0).astype(BF16)
        wt[ij, 1, 0] = jnp.where(group == 3, r0, 0.0).astype(BF16)
        wt[ij, 0, 1] = jnp.where(group < 3, blk, 0.0).astype(BF16)
        wt[ij, 0, 2] = jnp.where(group > 0, rolled(blk, 1), 0.0).astype(BF16)
        r3 = rolled(blk, 2)
        wt[ij, 0, 3] = jnp.where(group > 1, r3, 0.0).astype(BF16)
        wt[ij, 1, 3] = jnp.where(group == 0, r3, 0.0).astype(BF16)

    def weights(layer, ij, half):
        return wt[ij, half, :, layer * 32 : (layer + 1) * 32, :].reshape(128, 128)

    def windows(buf, at, shape, base, order):
        return jnp.concatenate(
            [
                buf[at, base + i : base + i + shape[0], base + j : base + j + shape[1]].reshape(-1, 128)
                for i, j in order
            ],
            axis=1,
        )

    def forward(layer, cols, shape):
        band = jnp.concatenate(
            [jnp.concatenate([weights(layer, ij, 0), weights(layer, ij, 1)], axis=0) for ij in range(9)], axis=1
        )
        return spill(nt(cols, band), shape)

    def backward(layer, cols, shape):
        band = jnp.concatenate(
            [jnp.concatenate([weights(layer, ij, 0), weights(layer, ij, 1)], axis=1) for ij in range(9)], axis=0
        )
        return spill(nn(cols, band), shape)

    def silu(y):
        return (y / (1.0 + jnp.exp(-y))).astype(BF16)

    def slope_of(y):
        return slope(y.astype(BF16).astype(F32))

    mine = (slab, rows)
    wide = (slab + 2, rows + 2)
    mirrored = [(2 - i, 2 - j) for i, j in OFFSETS]

    loads[3].wait()
    loads[4].wait()

    for pair in range(2):
        arrive(halo)
        y = forward(2 * pair, windows(xh, pair, wide, 0, OFFSETS), wide)
        put_near(xo, pair, silu(y))
        y2 = forward(2 * pair + 1, windows(xo, pair, mine, 0, OFFSETS), mine)
        act = silu(y2)
        if pair == 0:
            xh[1, own_p, own_r] = act
            halo = start(halo_copies(xh, 1, 1))
        else:
            for d in range(slab):
                tiles = act[d].reshape(plane, 128)
                hall[d][xpos] = tiles[:part_rows]
                far_out[d] = tiles[part_rows:]
            far = [start([remote(far_out.at[d], far_in.at[d], bz_s.at[d], bz_r.at[d], z_mate)]) for d in range(slab)]
            act_x = [
                start(
                    [
                        remote(hall[d].at[xpos], hall[d].at[xpos], ax_s.at[d, s], ax_r.at[d, s], x_mate(s))
                        for s in X_ORDER(nx)
                    ]
                )
                for d in range(slab)
            ]
            arrive(head_x)
            for d in range(slab):
                hzout[d] = hd[lax.div(match_ref[d, 2 * xpos + (1 - zhalf)], 2)]
            head_z = start([remote(hzout, hzin, z_s.at[slab], z_r.at[slab], z_mate)])
        slw[pair] = slope_of(y)
        slo[pair] = slope_of(y2)

    hidden = act.reshape(cells, 128)

    col_class = lax.broadcasted_iota(jnp.int32, (plane, 128), 1)
    real = col_class < classes
    spread_r = lax.broadcasted_iota(jnp.int32, (cells, slab * rows), 0)
    spread_c = lax.broadcasted_iota(jnp.int32, (cells, slab * rows), 1)
    spread = jnp.where(lax.div(spread_r, 16) == spread_c, 1.0, 0.0).astype(BF16)
    lab = nn(spread, lab_ref[...].reshape(slab * rows, 64).astype(F32).astype(BF16))
    vox = lax.broadcasted_iota(jnp.int32, (cells, 64), 1)
    own = lax.rem(lax.broadcasted_iota(jnp.int32, (cells, 64), 0), 16)
    lab = jnp.where(lax.div(vox, 4) == own, lab, 0.0).astype(BF16)
    pick_r = lax.broadcasted_iota(jnp.int32, (64, 512), 0)
    pick_c = lax.broadcasted_iota(jnp.int32, (64, 512), 1)
    pick = jnp.where(lax.rem(pick_r, 4) == lax.div(pick_c, 128), 1.0, 0.0).astype(BF16)
    class_of = nn(lab, pick)

    def softmax(act_plane, heads):
        logits = nn(act_plane, heads)
        out = []
        for a in range(4):
            ex = jnp.where(real, jnp.exp(logits[:, a * 128 : (a + 1) * 128]), 0.0)
            out.append(ex / jnp.sum(ex, axis=1, keepdims=True))
        return out

    col_f = col_class.astype(F32)
    for d in range(slab):
        probs = softmax(hidden[d * plane : (d + 1) * plane], hcat[...])
        for a in range(4):
            mark = jnp.where(class_of[d * plane : (d + 1) * plane, a * 128 : (a + 1) * 128] == col_f, 0.5, 0.0)
            part[d, :, a * 128 : (a + 1) * 128] = probs[a] - mark

    act_z = []
    for d in range(slab):
        arrive(act_x[d])
        zout[d] = hall[d][lax.div(match_ref[d, 2 * xpos + (1 - zhalf)], 2)]
        act_z.append(start([remote(zout.at[d], zin.at[d], z_s.at[d], z_r.at[d], z_mate)]))
    act_b = []
    for d in range(slab):
        arrive(far[d])
        for s in range(nx):
            source = match_ref[d, 2 * lax.rem(xpos + s, nx) + zhalf]
            chosen = jnp.where(
                lax.rem(source, 2) == zhalf, far_out[d].astype(F32), far_in[d].astype(F32)
            ).astype(BF16)
            if s == 0:
                pick_in[d][xpos] = chosen
            else:
                pick_out[s, d] = chosen
        act_b.append(
            start(
                [
                    remote(pick_out.at[s, d], pick_in[d].at[xpos], bx_s.at[d, s], bx_r.at[d, s], x_mate(s))
                    for s in X_ORDER(nx)
                ]
            )
        )
    arrive(head_z)
    grad_rows = []
    for d in range(slab):
        source = match_ref[d, peer]
        near_half = lax.rem(source, 2) == zhalf
        near_at = lax.div(source, 2)
        target_head = jnp.where(near_half, hd[near_at].astype(F32), hzin[d].astype(F32)).astype(BF16)
        for a in range(4):
            tcat[d, a * 32 : (a + 1) * 32, a * 128 : (a + 1) * 128] = target_head
        arrive(act_z[d])
        arrive(act_b[d])
        target_act = jnp.concatenate(
            [
                jnp.where(near_half, hall[d][near_at].astype(F32), zin[d].astype(F32)).astype(BF16),
                pick_in[d][near_at],
            ],
            axis=0,
        )
        target = softmax(target_act, tcat[d])
        grad_rows.append(
            jnp.concatenate(
                [
                    (part[d, :, a * 128 : (a + 1) * 128] - 0.5 * target[a].astype(BF16).astype(F32)).astype(BF16)
                    for a in range(4)
                ],
                axis=1,
            )
        )
    dlogits = jnp.concatenate(grad_rows, axis=0)
    g = nt(dlogits, hcat[...]).reshape(slab, rows, 16, 128) * slo[1]

    group32 = lax.div(lax.broadcasted_iota(jnp.int32, (32, 128), 1), 32)
    group288 = lax.div(lax.broadcasted_iota(jnp.int32, (288, 128), 1), 32)
    own_chunks = 8 // nr
    from_next = lane < 32
    from_last = lane >= 96

    def weight_grad(layer, g, cols):
        g = g.reshape(-1, 16, 128)
        ahead = jnp.where(from_next & (block < 15), pltpu.roll(g, 15, 1), 0.0)
        edge = jnp.where(from_last & (block > 0), pltpu.roll(g, 1, 1), ahead)
        both = jnp.concatenate([g.reshape(cells, 128), edge.reshape(cells, 128)], axis=1).astype(BF16).T
        prod = nn(both, cols)

        def take(at):
            return jnp.concatenate([prod[at : at + 32, ij * 128 : (ij + 1) * 128] for ij in range(9)], axis=0)

        s0 = jnp.where(group288 == 3, take(128), take(0))
        s3 = jnp.where(group288 == 0, take(224), take(96))
        total = take(32) + pltpu.roll(s0, 32, 1) + pltpu.roll(take(64), 96, 1) + pltpu.roll(s3, 64, 1)
        for t in range(7):
            tile = None
            ks = [(gr, *divmod(4 * t + gr, 3)) for gr in range(4) if 4 * t + gr < 27]
            for ij in sorted({ij for _, ij, _ in ks}):
                first = [(gr, k) for gr, at, k in ks if at == ij][0]
                moved = rolled(total[ij * 32 : (ij + 1) * 32], first[0] - first[1])
                tile = moved if tile is None else jnp.where(group32 >= first[0], moved, tile)
            pk[layer, t // own_chunks, t % own_chunks] = tile.astype(BF16)
        if layer < layers - 1:
            pk[layer, 7 // own_chunks, 7 % own_chunks] = jnp.zeros((32, 128), BF16)

    def span(layer_set):
        return pl.ds(layer_set[0], len(layer_set)), layer_set[0]

    def send_row(layer_set):
        at, n = span(layer_set)
        return start(
            [
                remote(pk.at[at, lax.rem(row + s, nr)], rsin.at[at, s], rs_s.at[n, s], rs_r.at[n, s], row_mate(s))
                for s in range(1, nr)
            ]
        )

    def send_depth(layer_set, copies):
        arrive(copies)
        at, n = span(layer_set)
        for layer in layer_set:
            total = pk[layer, row].astype(F32)
            for s in range(1, nr):
                total = total + rsin[layer, s].astype(F32)
            dep[layer, depth] = total.astype(BF16)
        return start(
            [
                remote(dep.at[at, depth], dep.at[at, depth], dp_s.at[n, s], dp_r.at[n, s], depth_mate(s))
                for s in range(1, nd)
            ]
        )

    def send_all(layer_set, copies):
        arrive(copies)
        at, n = span(layer_set)
        for layer in layer_set:
            total = dep[layer, 0].astype(F32)
            for s in range(1, nd):
                total = total + dep[layer, s].astype(F32)
            fin[layer, row] = total.astype(BF16)
        return start(
            [
                remote(fin.at[at, row], fin.at[at, row], ag_s.at[n, s], ag_r.at[n, s], row_mate(s))
                for s in range(1, nr)
            ]
        )

    def finish(layer_set, copies):
        arrive(copies)
        for layer in layer_set:
            for t in range(7):
                lanes = min(128, 27 * 32 - t * 128)
                cg_ref[layer, :, t * 128 : t * 128 + lanes] = fin[layer, t // own_chunks, t % own_chunks].astype(F32)[:, :lanes]
            if layer == layers - 1:
                hg_ref[...] = fin[layer, 7 // own_chunks, 7 % own_chunks].astype(F32)[:, :classes]

    gh[1, own_p, own_r] = g.astype(BF16)
    halo = start(halo_copies(gh, 1, 3))
    wide_heads = nn(hidden.T, dlogits)
    heads = wide_heads[0:32, 0:128]
    for a in range(1, 4):
        heads = heads + wide_heads[a * 32 : (a + 1) * 32, a * 128 : (a + 1) * 128]
    pk[3, 7 // own_chunks, 7 % own_chunks] = heads.astype(BF16)
    weight_grad(3, g, windows(xo, 1, mine, 0, OFFSETS))
    first = send_row([3])
    arrive(halo)
    g3 = backward(3, windows(gh, 1, wide, 0, mirrored), wide) * slw[1]
    put_near(go, 1, g3)
    g2 = backward(2, windows(go, 1, mine, 0, mirrored), mine) * slo[0]
    gh[0, own_p, own_r] = g2.astype(BF16)
    halo = start(halo_copies(gh, 0, 2))
    weight_grad(2, g3[1 : slab + 1, 1 : rows + 1], windows(xh, 1, mine, 1, OFFSETS))
    weight_grad(1, g2, windows(xo, 0, mine, 0, OFFSETS))
    second = send_row([1, 2])
    first = send_depth([3], first)
    arrive(halo)
    g1 = backward(1, windows(gh, 0, wide, 0, mirrored), wide) * slw[0]
    put_near(go, 0, g1)
    first = send_all([3], first)
    weight_grad(0, g1[1 : slab + 1, 1 : rows + 1], windows(xh, 0, mine, 1, OFFSETS))
    last = send_row([0])
    second = send_depth([1, 2], second)
    back = backward(0, windows(go, 0, mine, 0, mirrored), mine)
    tmp[...] = back.reshape(cells, 128)
    for d in range(slab):
        for b in range(16):
            ig_ref[d, :, b * 128 : (b + 1) * 128] = tmp[pl.ds(d * plane + b, rows, stride=16), :].astype(BF16)
    second = send_all([1, 2], second)
    finish([3], first)
    last = send_depth([0], last)
    last = send_all([0], last)
    finish([1, 2], second)
    for copy in started:
        copy.wait_send()
    finish([0], last)


def write_out(cg_ref, hg_ref, ig_ref, cg_out, hg_out, ig_out, sem):
    copies = [
        pltpu.make_async_copy(src, dst, sem.at[n])
        for n, (src, dst) in enumerate([(cg_ref, cg_out), (ig_ref, ig_out), (hg_ref, hg_out)])
    ]
    for copy in copies:
        copy.start()
    for copy in copies:
        copy.wait()


def X_ORDER(nx):
    return [s for s in (2, 1, 3) if s < nx]


def solution(mesh):
    np_, nd, nr = mesh.shape["peer"], mesh.shape["depth"], mesh.shape["row"]
    nx = np_ // 2

    def body(features, labels, conv_weights, head_weights, matching):
        slab, rows, merged = features.shape
        layers = conv_weights.shape[1]
        classes = head_weights.shape[2]
        cells = slab * rows * 16
        chunk = (8 // nr, 32, 128)
        far = (2, slab + 8, rows + 8, 16, 128)
        close = (2, slab + 4, rows + 4, 16, 128)
        vmem = pl.BlockSpec(memory_space=pltpu.VMEM)
        hbm = pl.BlockSpec(memory_space=pltpu.HBM)
        dma = pltpu.SemaphoreType.DMA
        scratch = [
            pltpu.VMEM((slab, rows, merged), BF16),
            pltpu.VMEM((slab, rows, merged // 32), jnp.int32),
            pltpu.VMEM((layers, 32, 27 * 32), BF16),
            pltpu.VMEM((32, classes), BF16),
            pltpu.SMEM((slab, np_), jnp.int32),
            pltpu.VMEM(far, BF16),
            pltpu.VMEM(far, BF16),
            pltpu.VMEM(close, BF16),
            pltpu.VMEM(close, BF16),
            pltpu.VMEM((9, 2, 4, layers * 32, 128), BF16),
            pltpu.VMEM((layers * 32, 896), F32),
            pltpu.VMEM((cells, 128), F32),
            pltpu.VMEM((2, slab, rows, 16, 128), F32),
            pltpu.VMEM((2, slab + 2, rows + 2, 16, 128), F32),
            pltpu.VMEM((128, 512), BF16),
            pltpu.VMEM((slab, 128, 512), BF16),
            pltpu.VMEM((nx, 32, 128), BF16),
            pltpu.VMEM((slab, 32, 128), BF16),
            pltpu.VMEM((slab, 32, 128), BF16),
            [pltpu.VMEM((nx, rows * 8, 128), BF16) for _ in range(slab)],
            pltpu.VMEM((slab, rows * 8, 128), BF16),
            pltpu.VMEM((slab, rows * 8, 128), BF16),
            pltpu.VMEM((slab, rows * 8, 128), BF16),
            pltpu.VMEM((slab, rows * 8, 128), BF16),
            [pltpu.VMEM((nx, rows * 8, 128), BF16) for _ in range(slab)],
            pltpu.VMEM((nx, slab, rows * 8, 128), BF16),
            pltpu.VMEM((slab, rows * 16, 512), F32),
            pltpu.VMEM((layers, nr) + chunk, BF16),
            pltpu.VMEM((layers, nr) + chunk, BF16),
            pltpu.VMEM((layers, nd) + chunk, BF16),
            pltpu.VMEM((layers, nr) + chunk, BF16),
            dma((5,)),
            dma((4, 8)), dma((4, 8)),
            dma((nx,)), dma((nx,)),
            dma((slab, nx)), dma((slab, nx)),
            dma((slab + 1,)), dma((slab + 1,)),
            dma((slab, nx)), dma((slab, nx)),
            dma((slab,)), dma((slab,)),
            dma((layers, nr)), dma((layers, nr)),
            dma((layers, nd)), dma((layers, nd)),
            dma((layers, nr)), dma((layers, nr)),
        ]
        sizes = (nx, nd, nr, slab, rows, classes, layers)
        cg, hg, ig = pl.pallas_call(
            functools.partial(kernel, sizes),
            out_shape=(
                pltpu.VMEM((layers, 32, 27 * 32), F32),
                pltpu.VMEM((32, classes), F32),
                pltpu.VMEM((slab, rows, merged), BF16),
            ),
            in_specs=[hbm] * 5,
            out_specs=(vmem,) * 3,
            scratch_shapes=scratch,
            compiler_params=pltpu.CompilerParams(collective_id=0, has_side_effects=True, vmem_limit_bytes=40 * 2**20),
        )(
            *(
                pltpu.with_memory_space_constraint(v, pltpu.HBM)
                for v in (features, labels, conv_weights[0].transpose(0, 2, 1), head_weights[0], matching)
            )
        )
        cg, hg, ig = pl.pallas_call(
            write_out,
            out_shape=tuple(jax.ShapeDtypeStruct(v.shape, v.dtype) for v in (cg, hg, ig)),
            in_specs=[vmem] * 3,
            out_specs=(hbm,) * 3,
            scratch_shapes=[dma((3,))],
            compiler_params=pltpu.CompilerParams(vmem_limit_bytes=2**20),
        )(cg, hg, ig)
        return cg.transpose(0, 2, 1)[None], hg[None], ig[None]

    return jax.shard_map(
        body,
        mesh=mesh,
        in_specs=(
            P("depth", "row", None),
            P("depth", "row", None),
            P("peer", None, None, None),
            P("peer", None, None),
            P("depth", None),
        ),
        out_specs=(
            P("peer", None, None, None),
            P("peer", None, None),
            P("peer", "depth", "row", None),
        ),
        check_vma=False,
    )
```

```python
import functools

import jax
import jax.numpy as jnp
from jax import lax
from jax.experimental import pallas as pl
from jax.experimental.pallas import tpu as pltpu
from jax.sharding import PartitionSpec as P

MESH = pl.DeviceIdType.MESH
F32 = jnp.float32
BF16 = jnp.bfloat16
OFFSETS = [(i, j) for i in range(3) for j in range(3)]
NEIGHBOURS = [(1, 1), (1, -1), (-1, 1), (-1, -1), (1, 0), (-1, 0), (0, 1), (0, -1)]


def nt(a, b):
    return lax.dot_general(a, b, (((1,), (1,)), ((), ())), preferred_element_type=F32)


def nn(a, b):
    return lax.dot_general(a, b, (((1,), (0,)), ((), ())), preferred_element_type=F32)


def slope(pre):
    s = 1.0 / (1.0 + jnp.exp(-pre))
    return s * (1.0 + pre * (1.0 - s))


def kernel(
    sizes,
    x_any, lab_any, w_any, head_any, match_any,
    cg_ref, hg_ref, ig_ref,
    x_ref, lab_ref, w_ref, head_ref, match_ref,
    xh, gh, xo, go, wt, wpad, tmp, slo, slw, hcat, tcat, hd, hzin, hzout, hall, zin, zout, far_in, far_out, pick_in, pick_out, acc, part,
    pk, rsin, dep, fin,
    in_s, halo_s, halo_r, hx_s, hx_r, ax_s, ax_r, z_s, z_r, bx_s, bx_r, bz_s, bz_r, rs_s, rs_r, dp_s, dp_r, ag_s, ag_r,
):
    nx, nd, nr, slab, rows, classes, layers = sizes
    cells = slab * rows * 16
    plane = rows * 16
    part_rows = plane // 2
    own_p, own_r = slice(2, slab + 2), slice(2, rows + 2)
    peer = lax.axis_index("peer")
    depth = lax.axis_index("depth")
    row = lax.axis_index("row")
    xpos, zhalf = lax.div(peer, 2), lax.rem(peer, 2)
    zpos = zhalf * nd + depth

    def near(dp, dr):
        where = {}
        if dr:
            where["row"] = lax.rem(row + dr + nr, nr)
        if dp:
            z = lax.rem(zpos + dp + 2 * nd, 2 * nd)
            where["peer"] = 2 * xpos + lax.div(z, nd)
            where["depth"] = lax.rem(z, nd)
        return where

    def x_mate(s):
        return {"peer": 2 * lax.rem(xpos + s, nx) + zhalf}

    z_mate = {"peer": 2 * xpos + (1 - zhalf)}

    def row_mate(s):
        return {"row": lax.rem(row + s, nr)}

    def depth_mate(s):
        return {"depth": lax.rem(depth + s, nd)}

    loads = [
        pltpu.make_async_copy(src, dst, in_s.at[n])
        for n, (src, dst) in enumerate(
            [(x_any, x_ref), (head_any, head_ref), (w_any, w_ref), (lab_any, lab_ref), (match_any, match_ref)]
        )
    ]
    for load in loads:
        load.start()

    mates = [near(*step) for step in NEIGHBOURS] + [near(2, 0), near(-2, 0)]
    mates += [x_mate(s) for s in range(1, nx)]
    mates += [row_mate(s) for s in range(2, nr - 1)]
    barrier = pltpu.get_barrier_semaphore()
    for mate in mates:
        pl.semaphore_signal(barrier, inc=1, device_id=mate, device_id_type=MESH)

    started = []

    def remote(src, dst, send, recv, mate):
        return pltpu.make_async_remote_copy(
            src_ref=src, dst_ref=dst, send_sem=send, recv_sem=recv, device_id=mate, device_id_type=MESH
        )

    def start(copies):
        for copy in copies:
            copy.start()
        started.extend(copies)
        return copies

    def arrive(copies):
        for copy in copies:
            copy.wait_recv()

    loads[0].wait()
    for d in range(slab):
        for b in range(16):
            tmp[pl.ds(d * plane + b, rows, stride=16), :] = x_ref[d, :, b * 128 : (b + 1) * 128].astype(F32)
    xh[0, own_p, own_r] = tmp[...].reshape(slab, rows, 16, 128).astype(BF16)

    loads[1].wait()
    tmp[0:32, :] = jnp.zeros((32, 128), F32)
    tmp[0:32, 0:classes] = head_ref[...].astype(F32)
    head = tmp[0:32, :].astype(BF16)
    hd[xpos] = head

    pl.semaphore_wait(barrier, len(mates))

    def halo_copies(buf, at, ex):
        copies = []
        for n, (dp, dr) in enumerate(NEIGHBOURS):
            if dp == 0:
                src_p, dst_p = pl.ds(2, slab), pl.ds(2, slab)
            elif dp == 1:
                src_p = pl.ds(slab, 2)
                dst_p = pl.ds(jnp.where(depth == nd - 1, slab + 4, 0), 2)
            else:
                src_p = pl.ds(2, 2)
                dst_p = pl.ds(jnp.where(depth == 0, slab + 6, slab + 2), 2)
            if dr == 0:
                src_r, dst_r = pl.ds(2, rows), pl.ds(2, rows)
            elif dr == 1:
                src_r = pl.ds(rows, 2)
                dst_r = pl.ds(jnp.where(row == nr - 1, rows + 4, 0), 2)
            else:
                src_r = pl.ds(2, 2)
                dst_r = pl.ds(jnp.where(row == 0, rows + 6, rows + 2), 2)
            copies.append(
                remote(
                    buf.at[at, src_p, src_r], buf.at[at, dst_p, dst_r],
                    halo_s.at[ex, n], halo_r.at[ex, n], near(dp, dr),
                )
            )
        return copies

    halo = start(halo_copies(xh, 0, 0))
    head_x = start(
        [remote(hd.at[xpos], hd.at[xpos], hx_s.at[s], hx_r.at[s], x_mate(s)) for s in range(1, nx)]
    )

    def clear_wide(buf, at):
        zero_p = jnp.zeros((2, rows + 4, 16, 128), BF16)
        buf[at, pl.ds(jnp.where(depth == 0, 0, slab + 4), 2), 0 : rows + 4] = zero_p
        buf[at, pl.ds(jnp.where(depth == nd - 1, slab + 2, slab + 6), 2), 0 : rows + 4] = zero_p
        zero_r = jnp.zeros((slab + 4, 2, 16, 128), BF16)
        buf[at, 0 : slab + 4, pl.ds(jnp.where(row == 0, 0, rows + 4), 2)] = zero_r
        buf[at, 0 : slab + 4, pl.ds(jnp.where(row == nr - 1, rows + 2, rows + 6), 2)] = zero_r

    def put_near(buf, at, value):
        buf[at, 0 : slab + 2, 0 : rows + 2] = value.astype(BF16)
        zero_p = jnp.zeros((1, rows + 2, 16, 128), BF16)
        buf[at, pl.ds(jnp.where(depth == 0, 0, slab + 2), 1), 0 : rows + 2] = zero_p
        buf[at, pl.ds(jnp.where(depth == nd - 1, slab + 1, slab + 3), 1), 0 : rows + 2] = zero_p
        zero_r = jnp.zeros((slab + 2, 1, 16, 128), BF16)
        buf[at, 0 : slab + 2, pl.ds(jnp.where(row == 0, 0, rows + 2), 1)] = zero_r
        buf[at, 0 : slab + 2, pl.ds(jnp.where(row == nr - 1, rows + 1, rows + 3), 1)] = zero_r

    for at in range(2):
        clear_wide(xh, at)
        clear_wide(gh, at)
    hcat[...] = jnp.zeros_like(hcat)
    tcat[...] = jnp.zeros_like(tcat)
    for a in range(4):
        hcat[a * 32 : (a + 1) * 32, a * 128 : (a + 1) * 128] = head

    lane = lax.broadcasted_iota(jnp.int32, (1, 16, 128), 2)
    block = lax.broadcasted_iota(jnp.int32, (1, 16, 128), 1)
    low = lane < 64
    inside = jnp.where(low, block, 15 - block) > 0

    def spill(y, shape):
        e = y[:, 128:].reshape(-1, 16, 128)
        moved = jnp.where(low, pltpu.roll(e, 1, 1), pltpu.roll(e, 15, 1))
        return (y[:, :128].reshape(-1, 16, 128) + jnp.where(inside, moved, 0.0)).reshape(*shape, 16, 128)

    loads[2].wait()
    wpad[:, 0 : 27 * 32] = w_ref[...].reshape(layers * 32, 27 * 32).astype(F32)
    wt[:, 1, 1:3] = jnp.zeros((9, 2, layers * 32, 128), BF16)
    group = lax.div(lax.broadcasted_iota(jnp.int32, (layers * 32, 128), 1), 32)

    def rolled(v, groups):
        shift = (groups * 32) % 128
        return v if shift == 0 else pltpu.roll(v, shift, 1)

    for ij in range(9):
        blk = None
        for k in range(3):
            t, g = divmod(3 * ij + k, 4)
            piece = rolled(wpad[:, t * 128 : (t + 1) * 128], k - g)
            blk = piece if blk is None else jnp.where(group == k, piece, blk)
        r0 = rolled(blk, -1)
        wt[ij, 0, 0] = jnp.where(group < 2, r0, 0.0).astype(BF16)
        wt[ij, 1, 0] = jnp.where(group == 3, r0, 0.0).astype(BF16)
        wt[ij, 0, 1] = jnp.where(group < 3, blk, 0.0).astype(BF16)
        wt[ij, 0, 2] = jnp.where(group > 0, rolled(blk, 1), 0.0).astype(BF16)
        r3 = rolled(blk, 2)
        wt[ij, 0, 3] = jnp.where(group > 1, r3, 0.0).astype(BF16)
        wt[ij, 1, 3] = jnp.where(group == 0, r3, 0.0).astype(BF16)

    def weights(layer, ij, half):
        return wt[ij, half, :, layer * 32 : (layer + 1) * 32, :].reshape(128, 128)

    def windows(buf, at, shape, base, order):
        return jnp.concatenate(
            [
                buf[at, base + i : base + i + shape[0], base + j : base + j + shape[1]].reshape(-1, 128)
                for i, j in order
            ],
            axis=1,
        )

    def forward(layer, cols, shape):
        band = jnp.concatenate(
            [jnp.concatenate([weights(layer, ij, 0), weights(layer, ij, 1)], axis=0) for ij in range(9)], axis=1
        )
        return spill(nt(cols, band), shape)

    def backward(layer, cols, shape):
        band = jnp.concatenate(
            [jnp.concatenate([weights(layer, ij, 0), weights(layer, ij, 1)], axis=1) for ij in range(9)], axis=0
        )
        return spill(nn(cols, band), shape)

    def ahead_of_depth(layer, buf, at, halo, back):
        def planes(*ps):
            return jnp.concatenate(
                [
                    jnp.concatenate([buf[at, p, j : j + rows + 2].reshape(-1, 128) for p in ps], axis=0)
                    for j in range(3)
                ],
                axis=1,
            )

        def band(i):
            if back:
                at_ij = [3 * (2 - i) + 2 - j for j in range(3)]
                return jnp.concatenate(
                    [jnp.concatenate([weights(layer, ij, 0), weights(layer, ij, 1)], axis=1) for ij in at_ij], axis=0
                )
            return jnp.concatenate(
                [
                    jnp.concatenate([weights(layer, 3 * i + j, 0), weights(layer, 3 * i + j, 1)], axis=0)
                    for j in range(3)
                ],
                axis=1,
            )

        dot = nn if back else nt
        n = (rows + 2) * 16
        arrive(halo[6:])
        own = [dot(planes(*range(2, slab + 2)), band(i)) for i in range(3)]
        for p in range(slab + 2):
            terms = [own[i][(p + i - 2) * n : (p + i - 1) * n] for i in range(3) if 0 <= p + i - 2 < slab]
            acc[p * n : (p + 1) * n] = functools.reduce(jnp.add, terms)
        arrive(halo[:6])
        first = dot(planes(0, 1), band(0))
        middle = dot(planes(1, slab + 2), band(1))
        final = dot(planes(slab + 2, slab + 3), band(2))
        more = {0: first[:n] + middle[:n], 1: first[n:], slab: final[:n], slab + 1: middle[n:] + final[n:]}
        return spill(
            jnp.concatenate(
                [acc[p * n : (p + 1) * n] + more[p] if p in more else acc[p * n : (p + 1) * n] for p in range(slab + 2)],
                axis=0,
            ),
            wide,
        )

    def silu(y):
        return (y / (1.0 + jnp.exp(-y))).astype(BF16)

    def slope_of(y):
        return slope(y.astype(BF16).astype(F32))

    mine = (slab, rows)
    wide = (slab + 2, rows + 2)
    mirrored = [(2 - i, 2 - j) for i, j in OFFSETS]

    loads[3].wait()
    loads[4].wait()

    for pair in range(2):
        y = ahead_of_depth(2 * pair, xh, pair, halo, False)
        put_near(xo, pair, silu(y))
        y2 = forward(2 * pair + 1, windows(xo, pair, mine, 0, OFFSETS), mine)
        act = silu(y2)
        if pair == 0:
            xh[1, own_p, own_r] = act
            halo = start(halo_copies(xh, 1, 1))
        else:
            for d in range(slab):
                tiles = act[d].reshape(plane, 128)
                hall[d][xpos] = tiles[:part_rows]
                far_out[d] = tiles[part_rows:]
            far = [start([remote(far_out.at[d], far_in.at[d], bz_s.at[d], bz_r.at[d], z_mate)]) for d in range(slab)]
            act_x = [
                start(
                    [
                        remote(hall[d].at[xpos], hall[d].at[xpos], ax_s.at[d, s], ax_r.at[d, s], x_mate(s))
                        for s in X_ORDER(nx)
                    ]
                )
                for d in range(slab)
            ]
            arrive(head_x)
            for d in range(slab):
                hzout[d] = hd[lax.div(match_ref[d, 2 * xpos + (1 - zhalf)], 2)]
            head_z = start([remote(hzout, hzin, z_s.at[slab], z_r.at[slab], z_mate)])
        slw[pair] = slope_of(y)
        slo[pair] = slope_of(y2)

    hidden = act.reshape(cells, 128)

    col_class = lax.broadcasted_iota(jnp.int32, (plane, 128), 1)
    real = col_class < classes
    spread_r = lax.broadcasted_iota(jnp.int32, (cells, slab * rows), 0)
    spread_c = lax.broadcasted_iota(jnp.int32, (cells, slab * rows), 1)
    spread = jnp.where(lax.div(spread_r, 16) == spread_c, 1.0, 0.0).astype(BF16)
    lab = nn(spread, lab_ref[...].reshape(slab * rows, 64).astype(F32).astype(BF16))
    vox = lax.broadcasted_iota(jnp.int32, (cells, 64), 1)
    own = lax.rem(lax.broadcasted_iota(jnp.int32, (cells, 64), 0), 16)
    lab = jnp.where(lax.div(vox, 4) == own, lab, 0.0).astype(BF16)
    pick_r = lax.broadcasted_iota(jnp.int32, (64, 512), 0)
    pick_c = lax.broadcasted_iota(jnp.int32, (64, 512), 1)
    pick = jnp.where(lax.rem(pick_r, 4) == lax.div(pick_c, 128), 1.0, 0.0).astype(BF16)
    class_of = nn(lab, pick)

    def softmax(act_plane, heads):
        logits = nn(act_plane, heads)
        out = []
        for a in range(4):
            ex = jnp.where(real, jnp.exp(logits[:, a * 128 : (a + 1) * 128]), 0.0)
            out.append(ex / jnp.sum(ex, axis=1, keepdims=True))
        return out

    col_f = col_class.astype(F32)
    for d in range(slab):
        probs = softmax(hidden[d * plane : (d + 1) * plane], hcat[...])
        for a in range(4):
            mark = jnp.where(class_of[d * plane : (d + 1) * plane, a * 128 : (a + 1) * 128] == col_f, 0.5, 0.0)
            part[d, :, a * 128 : (a + 1) * 128] = probs[a] - mark

    act_z = []
    for d in range(slab):
        arrive(act_x[d])
        zout[d] = hall[d][lax.div(match_ref[d, 2 * xpos + (1 - zhalf)], 2)]
        act_z.append(start([remote(zout.at[d], zin.at[d], z_s.at[d], z_r.at[d], z_mate)]))
    act_b = []
    for d in range(slab):
        arrive(far[d])
        for s in range(nx):
            source = match_ref[d, 2 * lax.rem(xpos + s, nx) + zhalf]
            chosen = jnp.where(
                lax.rem(source, 2) == zhalf, far_out[d].astype(F32), far_in[d].astype(F32)
            ).astype(BF16)
            if s == 0:
                pick_in[d][xpos] = chosen
            else:
                pick_out[s, d] = chosen
        act_b.append(
            start(
                [
                    remote(pick_out.at[s, d], pick_in[d].at[xpos], bx_s.at[d, s], bx_r.at[d, s], x_mate(s))
                    for s in X_ORDER(nx)
                ]
            )
        )
    arrive(head_z)
    grad_rows = []
    for d in range(slab):
        source = match_ref[d, peer]
        near_half = lax.rem(source, 2) == zhalf
        near_at = lax.div(source, 2)
        target_head = jnp.where(near_half, hd[near_at].astype(F32), hzin[d].astype(F32)).astype(BF16)
        for a in range(4):
            tcat[d, a * 32 : (a + 1) * 32, a * 128 : (a + 1) * 128] = target_head
        arrive(act_z[d])
        arrive(act_b[d])
        target_act = jnp.concatenate(
            [
                jnp.where(near_half, hall[d][near_at].astype(F32), zin[d].astype(F32)).astype(BF16),
                pick_in[d][near_at],
            ],
            axis=0,
        )
        target = softmax(target_act, tcat[d])
        grad_rows.append(
            jnp.concatenate(
                [
                    (part[d, :, a * 128 : (a + 1) * 128] - 0.5 * target[a].astype(BF16).astype(F32)).astype(BF16)
                    for a in range(4)
                ],
                axis=1,
            )
        )
    dlogits = jnp.concatenate(grad_rows, axis=0)
    g = nt(dlogits, hcat[...]).reshape(slab, rows, 16, 128) * slo[1]

    group32 = lax.div(lax.broadcasted_iota(jnp.int32, (32, 128), 1), 32)
    group288 = lax.div(lax.broadcasted_iota(jnp.int32, (288, 128), 1), 32)
    own_chunks = 8 // nr
    from_next = lane < 32
    from_last = lane >= 96

    def weight_grad(layer, g, cols):
        g = g.reshape(-1, 16, 128)
        ahead = jnp.where(from_next & (block < 15), pltpu.roll(g, 15, 1), 0.0)
        edge = jnp.where(from_last & (block > 0), pltpu.roll(g, 1, 1), ahead)
        both = jnp.concatenate([g.reshape(cells, 128), edge.reshape(cells, 128)], axis=1).astype(BF16).T
        prod = nn(both, cols)

        def take(at):
            return jnp.concatenate([prod[at : at + 32, ij * 128 : (ij + 1) * 128] for ij in range(9)], axis=0)

        s0 = jnp.where(group288 == 3, take(128), take(0))
        s3 = jnp.where(group288 == 0, take(224), take(96))
        total = take(32) + pltpu.roll(s0, 32, 1) + pltpu.roll(take(64), 96, 1) + pltpu.roll(s3, 64, 1)
        for t in range(7):
            tile = None
            ks = [(gr, *divmod(4 * t + gr, 3)) for gr in range(4) if 4 * t + gr < 27]
            for ij in sorted({ij for _, ij, _ in ks}):
                first = [(gr, k) for gr, at, k in ks if at == ij][0]
                moved = rolled(total[ij * 32 : (ij + 1) * 32], first[0] - first[1])
                tile = moved if tile is None else jnp.where(group32 >= first[0], moved, tile)
            pk[layer, t // own_chunks, t % own_chunks] = tile.astype(BF16)
        if layer < layers - 1:
            pk[layer, 7 // own_chunks, 7 % own_chunks] = jnp.zeros((32, 128), BF16)

    def span(layer_set):
        return pl.ds(layer_set[0], len(layer_set)), layer_set[0]

    def send_row(layer_set):
        at, n = span(layer_set)
        return start(
            [
                remote(pk.at[at, lax.rem(row + s, nr)], rsin.at[at, s], rs_s.at[n, s], rs_r.at[n, s], row_mate(s))
                for s in range(1, nr)
            ]
        )

    def send_depth(layer_set, copies):
        arrive(copies)
        at, n = span(layer_set)
        for layer in layer_set:
            total = pk[layer, row].astype(F32)
            for s in range(1, nr):
                total = total + rsin[layer, s].astype(F32)
            dep[layer, depth] = total.astype(BF16)
        return start(
            [
                remote(dep.at[at, depth], dep.at[at, depth], dp_s.at[n, s], dp_r.at[n, s], depth_mate(s))
                for s in range(1, nd)
            ]
        )

    def send_all(layer_set, copies):
        arrive(copies)
        at, n = span(layer_set)
        for layer in layer_set:
            total = dep[layer, 0].astype(F32)
            for s in range(1, nd):
                total = total + dep[layer, s].astype(F32)
            fin[layer, row] = total.astype(BF16)
        return start(
            [
                remote(fin.at[at, row], fin.at[at, row], ag_s.at[n, s], ag_r.at[n, s], row_mate(s))
                for s in range(1, nr)
            ]
        )

    def finish(layer_set, copies):
        arrive(copies)
        for layer in layer_set:
            for t in range(7):
                lanes = min(128, 27 * 32 - t * 128)
                cg_ref[layer, :, t * 128 : t * 128 + lanes] = fin[layer, t // own_chunks, t % own_chunks].astype(F32)[:, :lanes]
            if layer == layers - 1:
                hg_ref[...] = fin[layer, 7 // own_chunks, 7 % own_chunks].astype(F32)[:, :classes]

    gh[1, own_p, own_r] = g.astype(BF16)
    halo = start(halo_copies(gh, 1, 3))
    wide_heads = nn(hidden.T, dlogits)
    heads = wide_heads[0:32, 0:128]
    for a in range(1, 4):
        heads = heads + wide_heads[a * 32 : (a + 1) * 32, a * 128 : (a + 1) * 128]
    pk[3, 7 // own_chunks, 7 % own_chunks] = heads.astype(BF16)
    weight_grad(3, g, windows(xo, 1, mine, 0, OFFSETS))
    first = send_row([3])
    g3 = ahead_of_depth(3, gh, 1, halo, True) * slw[1]
    put_near(go, 1, g3)
    g2 = backward(2, windows(go, 1, mine, 0, mirrored), mine) * slo[0]
    gh[0, own_p, own_r] = g2.astype(BF16)
    halo = start(halo_copies(gh, 0, 2))
    weight_grad(2, g3[1 : slab + 1, 1 : rows + 1], windows(xh, 1, mine, 1, OFFSETS))
    weight_grad(1, g2, windows(xo, 0, mine, 0, OFFSETS))
    second = send_row([1, 2])
    first = send_depth([3], first)
    g1 = ahead_of_depth(1, gh, 0, halo, True) * slw[0]
    put_near(go, 0, g1)
    first = send_all([3], first)
    weight_grad(0, g1[1 : slab + 1, 1 : rows + 1], windows(xh, 0, mine, 1, OFFSETS))
    last = send_row([0])
    second = send_depth([1, 2], second)
    back = backward(0, windows(go, 0, mine, 0, mirrored), mine)
    tmp[...] = back.reshape(cells, 128)
    for d in range(slab):
        for b in range(16):
            ig_ref[d, :, b * 128 : (b + 1) * 128] = tmp[pl.ds(d * plane + b, rows, stride=16), :].astype(BF16)
    last = send_depth([0], last)
    second = send_all([1, 2], second)
    finish([3], first)
    last = send_all([0], last)
    finish([1, 2], second)
    for copy in started:
        copy.wait_send()
    finish([0], last)


def write_out(cg_ref, hg_ref, ig_ref, cg_out, hg_out, ig_out, sem):
    copies = [
        pltpu.make_async_copy(src, dst, sem.at[n])
        for n, (src, dst) in enumerate([(cg_ref, cg_out), (ig_ref, ig_out), (hg_ref, hg_out)])
    ]
    for copy in copies:
        copy.start()
    for copy in copies:
        copy.wait()


def X_ORDER(nx):
    return [s for s in (2, 1, 3) if s < nx]


def solution(mesh):
    np_, nd, nr = mesh.shape["peer"], mesh.shape["depth"], mesh.shape["row"]
    nx = np_ // 2

    def body(features, labels, conv_weights, head_weights, matching):
        slab, rows, merged = features.shape
        layers = conv_weights.shape[1]
        classes = head_weights.shape[2]
        cells = slab * rows * 16
        chunk = (8 // nr, 32, 128)
        far = (2, slab + 8, rows + 8, 16, 128)
        close = (2, slab + 4, rows + 4, 16, 128)
        vmem = pl.BlockSpec(memory_space=pltpu.VMEM)
        hbm = pl.BlockSpec(memory_space=pltpu.HBM)
        dma = pltpu.SemaphoreType.DMA
        scratch = [
            pltpu.VMEM((slab, rows, merged), BF16),
            pltpu.VMEM((slab, rows, merged // 32), jnp.int32),
            pltpu.VMEM((layers, 32, 27 * 32), BF16),
            pltpu.VMEM((32, classes), BF16),
            pltpu.SMEM((slab, np_), jnp.int32),
            pltpu.VMEM(far, BF16),
            pltpu.VMEM(far, BF16),
            pltpu.VMEM(close, BF16),
            pltpu.VMEM(close, BF16),
            pltpu.VMEM((9, 2, 4, layers * 32, 128), BF16),
            pltpu.VMEM((layers * 32, 896), F32),
            pltpu.VMEM((cells, 128), F32),
            pltpu.VMEM((2, slab, rows, 16, 128), F32),
            pltpu.VMEM((2, slab + 2, rows + 2, 16, 128), F32),
            pltpu.VMEM((128, 512), BF16),
            pltpu.VMEM((slab, 128, 512), BF16),
            pltpu.VMEM((nx, 32, 128), BF16),
            pltpu.VMEM((slab, 32, 128), BF16),
            pltpu.VMEM((slab, 32, 128), BF16),
            [pltpu.VMEM((nx, rows * 8, 128), BF16) for _ in range(slab)],
            pltpu.VMEM((slab, rows * 8, 128), BF16),
            pltpu.VMEM((slab, rows * 8, 128), BF16),
            pltpu.VMEM((slab, rows * 8, 128), BF16),
            pltpu.VMEM((slab, rows * 8, 128), BF16),
            [pltpu.VMEM((nx, rows * 8, 128), BF16) for _ in range(slab)],
            pltpu.VMEM((nx, slab, rows * 8, 128), BF16),
            pltpu.VMEM(((slab + 2) * (rows + 2) * 16, 256), F32),
            pltpu.VMEM((slab, rows * 16, 512), F32),
            pltpu.VMEM((layers, nr) + chunk, BF16),
            pltpu.VMEM((layers, nr) + chunk, BF16),
            pltpu.VMEM((layers, nd) + chunk, BF16),
            pltpu.VMEM((layers, nr) + chunk, BF16),
            dma((5,)),
            dma((4, 8)), dma((4, 8)),
            dma((nx,)), dma((nx,)),
            dma((slab, nx)), dma((slab, nx)),
            dma((slab + 1,)), dma((slab + 1,)),
            dma((slab, nx)), dma((slab, nx)),
            dma((slab,)), dma((slab,)),
            dma((layers, nr)), dma((layers, nr)),
            dma((layers, nd)), dma((layers, nd)),
            dma((layers, nr)), dma((layers, nr)),
        ]
        sizes = (nx, nd, nr, slab, rows, classes, layers)
        cg, hg, ig = pl.pallas_call(
            functools.partial(kernel, sizes),
            out_shape=(
                pltpu.VMEM((layers, 32, 27 * 32), F32),
                pltpu.VMEM((32, classes), F32),
                pltpu.VMEM((slab, rows, merged), BF16),
            ),
            in_specs=[hbm] * 5,
            out_specs=(vmem,) * 3,
            scratch_shapes=scratch,
            compiler_params=pltpu.CompilerParams(collective_id=0, has_side_effects=True, vmem_limit_bytes=40 * 2**20),
        )(
            *(
                pltpu.with_memory_space_constraint(v, pltpu.HBM)
                for v in (features, labels, conv_weights[0].transpose(0, 2, 1), head_weights[0], matching)
            )
        )
        cg, hg, ig = pl.pallas_call(
            write_out,
            out_shape=tuple(jax.ShapeDtypeStruct(v.shape, v.dtype) for v in (cg, hg, ig)),
            in_specs=[vmem] * 3,
            out_specs=(hbm,) * 3,
            scratch_shapes=[dma((3,))],
            compiler_params=pltpu.CompilerParams(vmem_limit_bytes=2**20),
        )(cg, hg, ig)
        return cg.transpose(0, 2, 1)[None], hg[None], ig[None]

    return jax.shard_map(
        body,
        mesh=mesh,
        in_specs=(
            P("depth", "row", None),
            P("depth", "row", None),
            P("peer", None, None, None),
            P("peer", None, None),
            P("depth", None),
        ),
        out_specs=(
            P("peer", None, None, None),
            P("peer", None, None),
            P("peer", "depth", "row", None),
        ),
        check_vma=False,
    )
```

```python
import functools

import jax
import jax.numpy as jnp
from jax import lax
from jax.experimental import pallas as pl
from jax.experimental.pallas import tpu as pltpu
from jax.sharding import PartitionSpec as P

MESH = pl.DeviceIdType.MESH
F32 = jnp.float32
BF16 = jnp.bfloat16
OFFSETS = [(i, j) for i in range(3) for j in range(3)]
NEIGHBOURS = [(1, 1), (1, -1), (-1, 1), (-1, -1), (1, 0), (-1, 0), (0, 1), (0, -1)]


def nt(a, b):
    return lax.dot_general(a, b, (((1,), (1,)), ((), ())), preferred_element_type=F32)


def nn(a, b):
    return lax.dot_general(a, b, (((1,), (0,)), ((), ())), preferred_element_type=F32)


def slope(pre):
    s = 0.5 * jnp.tanh(0.5 * pre) + 0.5
    return s * (1.0 + pre * (1.0 - s))


def kernel(
    sizes,
    x_any, lab_any, w_any, head_any, match_any,
    cg_ref, hg_ref, ig_ref,
    x_ref, lab_ref, w_ref, head_ref, match_ref,
    xh, gh, xo, go, wt, wpad, tmp, slo, slw, hcat, tcat, hd, hzin, hzout, hall, zin, zout, far_in, far_out, pick_in, pick_out, acc, part,
    pk, rsin, dep, fin,
    in_s, halo_s, halo_r, hx_s, hx_r, ax_s, ax_r, z_s, z_r, bx_s, bx_r, bz_s, bz_r, rs_s, rs_r, dp_s, dp_r, ag_s, ag_r,
):
    nx, nd, nr, slab, rows, classes, layers = sizes
    cells = slab * rows * 16
    plane = rows * 16
    part_rows = plane // 2
    own_p, own_r = slice(2, slab + 2), slice(2, rows + 2)
    peer = lax.axis_index("peer")
    depth = lax.axis_index("depth")
    row = lax.axis_index("row")
    xpos, zhalf = lax.div(peer, 2), lax.rem(peer, 2)
    zpos = zhalf * nd + depth

    def near(dp, dr):
        where = {}
        if dr:
            where["row"] = lax.rem(row + dr + nr, nr)
        if dp:
            z = lax.rem(zpos + dp + 2 * nd, 2 * nd)
            where["peer"] = 2 * xpos + lax.div(z, nd)
            where["depth"] = lax.rem(z, nd)
        return where

    def x_mate(s):
        return {"peer": 2 * lax.rem(xpos + s, nx) + zhalf}

    z_mate = {"peer": 2 * xpos + (1 - zhalf)}

    def row_mate(s):
        return {"row": lax.rem(row + s, nr)}

    def depth_mate(s):
        return {"depth": lax.rem(depth + s, nd)}

    loads = [
        pltpu.make_async_copy(src, dst, in_s.at[n])
        for n, (src, dst) in enumerate(
            [(x_any, x_ref), (head_any, head_ref), (w_any, w_ref), (lab_any, lab_ref), (match_any, match_ref)]
        )
    ]
    for load in loads:
        load.start()

    mates = [near(*step) for step in NEIGHBOURS] + [near(2, 0), near(-2, 0)]
    mates += [x_mate(s) for s in range(1, nx)]
    mates += [row_mate(s) for s in range(2, nr - 1)]
    barrier = pltpu.get_barrier_semaphore()
    for mate in mates:
        pl.semaphore_signal(barrier, inc=1, device_id=mate, device_id_type=MESH)

    started = []

    def remote(src, dst, send, recv, mate):
        return pltpu.make_async_remote_copy(
            src_ref=src, dst_ref=dst, send_sem=send, recv_sem=recv, device_id=mate, device_id_type=MESH
        )

    def send(jobs, total, send_sem, recv_sem):
        for src, dst, mate in jobs:
            remote(src, dst, send_sem, recv_sem, mate).start()
        if jobs:
            whole = remote(total, total, send_sem, recv_sem, jobs[0][2])
            started.append(whole)
            return whole

    def arrive(whole):
        if whole is not None:
            whole.wait_recv()

    loads[0].wait()
    for d in range(slab):
        for b in range(16):
            tmp[pl.ds(d * plane + b, rows, stride=16), :] = x_ref[d, :, b * 128 : (b + 1) * 128].astype(F32)
    xh[0, own_p, own_r] = tmp[...].reshape(slab, rows, 16, 128).astype(BF16)

    loads[1].wait()
    tmp[0:32, :] = jnp.zeros((32, 128), F32)
    tmp[0:32, 0:classes] = head_ref[...].astype(F32)
    head = tmp[0:32, :].astype(BF16)
    hd[xpos] = head

    pl.semaphore_wait(barrier, len(mates))

    def send_halo(buf, at, ex):
        jobs = []
        for dp, dr in NEIGHBOURS:
            if dp == 0:
                src_p, dst_p = pl.ds(2, slab), pl.ds(2, slab)
            elif dp == 1:
                src_p = pl.ds(slab, 2)
                dst_p = pl.ds(jnp.where(depth == nd - 1, slab + 4, 0), 2)
            else:
                src_p = pl.ds(2, 2)
                dst_p = pl.ds(jnp.where(depth == 0, slab + 6, slab + 2), 2)
            if dr == 0:
                src_r, dst_r = pl.ds(2, rows), pl.ds(2, rows)
            elif dr == 1:
                src_r = pl.ds(rows, 2)
                dst_r = pl.ds(jnp.where(row == nr - 1, rows + 4, 0), 2)
            else:
                src_r = pl.ds(2, 2)
                dst_r = pl.ds(jnp.where(row == 0, rows + 6, rows + 2), 2)
            jobs.append((buf.at[at, src_p, src_r], buf.at[at, dst_p, dst_r], near(dp, dr)))
        far = send(jobs[:6], buf.at[at, pl.ds(0, 4), pl.ds(0, rows + 4)], halo_s.at[ex, 0], halo_r.at[ex, 0])
        beside = send(jobs[6:], buf.at[at, pl.ds(0, slab), pl.ds(0, 4)], halo_s.at[ex, 1], halo_r.at[ex, 1])
        return far, beside

    halo = send_halo(xh, 0, 0)
    some_x = pl.ds(0, nx - 1)
    head_x = send(
        [(hd.at[xpos], hd.at[xpos], x_mate(s)) for s in range(1, nx)], hd.at[some_x], hx_s.at[0], hx_r.at[0]
    )

    def clear_wide(buf, at):
        zero_p = jnp.zeros((2, rows + 4, 16, 128), BF16)
        buf[at, pl.ds(jnp.where(depth == 0, 0, slab + 4), 2), 0 : rows + 4] = zero_p
        buf[at, pl.ds(jnp.where(depth == nd - 1, slab + 2, slab + 6), 2), 0 : rows + 4] = zero_p
        zero_r = jnp.zeros((slab + 4, 2, 16, 128), BF16)
        buf[at, 0 : slab + 4, pl.ds(jnp.where(row == 0, 0, rows + 4), 2)] = zero_r
        buf[at, 0 : slab + 4, pl.ds(jnp.where(row == nr - 1, rows + 2, rows + 6), 2)] = zero_r

    def put_near(buf, at, value):
        buf[at, 0 : slab + 2, 0 : rows + 2] = value.astype(BF16)
        zero_p = jnp.zeros((1, rows + 2, 16, 128), BF16)
        buf[at, pl.ds(jnp.where(depth == 0, 0, slab + 2), 1), 0 : rows + 2] = zero_p
        buf[at, pl.ds(jnp.where(depth == nd - 1, slab + 1, slab + 3), 1), 0 : rows + 2] = zero_p
        zero_r = jnp.zeros((slab + 2, 1, 16, 128), BF16)
        buf[at, 0 : slab + 2, pl.ds(jnp.where(row == 0, 0, rows + 2), 1)] = zero_r
        buf[at, 0 : slab + 2, pl.ds(jnp.where(row == nr - 1, rows + 1, rows + 3), 1)] = zero_r

    for at in range(2):
        clear_wide(xh, at)
        clear_wide(gh, at)
    hcat[...] = jnp.zeros_like(hcat)
    tcat[...] = jnp.zeros_like(tcat)
    for a in range(4):
        hcat[a * 32 : (a + 1) * 32, a * 128 : (a + 1) * 128] = head

    lane = lax.broadcasted_iota(jnp.int32, (1, 16, 128), 2)
    block = lax.broadcasted_iota(jnp.int32, (1, 16, 128), 1)
    low = lane < 64
    inside = jnp.where(low, block, 15 - block) > 0

    def spill(y, shape):
        e = y[:, 128:].reshape(-1, 16, 128)
        moved = jnp.where(low, pltpu.roll(e, 1, 1), pltpu.roll(e, 15, 1))
        return (y[:, :128].reshape(-1, 16, 128) + jnp.where(inside, moved, 0.0)).reshape(*shape, 16, 128)

    loads[2].wait()
    wpad[:, 0 : 27 * 32] = w_ref[...].reshape(layers * 32, 27 * 32).astype(F32)
    wt[:, 1, 1:3] = jnp.zeros((9, 2, layers * 32, 128), BF16)
    group = lax.div(lax.broadcasted_iota(jnp.int32, (layers * 32, 128), 1), 32)

    def rolled(v, groups):
        shift = (groups * 32) % 128
        return v if shift == 0 else pltpu.roll(v, shift, 1)

    for ij in range(9):
        blk = None
        for k in range(3):
            t, g = divmod(3 * ij + k, 4)
            piece = rolled(wpad[:, t * 128 : (t + 1) * 128], k - g)
            blk = piece if blk is None else jnp.where(group == k, piece, blk)
        r0 = rolled(blk, -1)
        wt[ij, 0, 0] = jnp.where(group < 2, r0, 0.0).astype(BF16)
        wt[ij, 1, 0] = jnp.where(group == 3, r0, 0.0).astype(BF16)
        wt[ij, 0, 1] = jnp.where(group < 3, blk, 0.0).astype(BF16)
        wt[ij, 0, 2] = jnp.where(group > 0, rolled(blk, 1), 0.0).astype(BF16)
        r3 = rolled(blk, 2)
        wt[ij, 0, 3] = jnp.where(group > 1, r3, 0.0).astype(BF16)
        wt[ij, 1, 3] = jnp.where(group == 0, r3, 0.0).astype(BF16)

    def weights(layer, ij, half):
        return wt[ij, half, :, layer * 32 : (layer + 1) * 32, :].reshape(128, 128)

    def windows(buf, at, shape, base, order):
        return jnp.concatenate(
            [
                buf[at, base + i : base + i + shape[0], base + j : base + j + shape[1]].reshape(-1, 128)
                for i, j in order
            ],
            axis=1,
        )

    def forward(layer, cols, shape):
        band = jnp.concatenate(
            [jnp.concatenate([weights(layer, ij, 0), weights(layer, ij, 1)], axis=0) for ij in range(9)], axis=1
        )
        return spill(nt(cols, band), shape)

    def backward(layer, cols, shape):
        band = jnp.concatenate(
            [jnp.concatenate([weights(layer, ij, 0), weights(layer, ij, 1)], axis=1) for ij in range(9)], axis=0
        )
        return spill(nn(cols, band), shape)

    def ahead_of_depth(layer, buf, at, halo, back):
        def planes(*ps):
            return jnp.concatenate(
                [
                    jnp.concatenate([buf[at, p, j : j + rows + 2].reshape(-1, 128) for p in ps], axis=0)
                    for j in range(3)
                ],
                axis=1,
            )

        def band(i):
            if back:
                at_ij = [3 * (2 - i) + 2 - j for j in range(3)]
                return jnp.concatenate(
                    [jnp.concatenate([weights(layer, ij, 0), weights(layer, ij, 1)], axis=1) for ij in at_ij], axis=0
                )
            return jnp.concatenate(
                [
                    jnp.concatenate([weights(layer, 3 * i + j, 0), weights(layer, 3 * i + j, 1)], axis=0)
                    for j in range(3)
                ],
                axis=1,
            )

        dot = nn if back else nt
        n = (rows + 2) * 16
        arrive(halo[1])
        own = [dot(planes(*range(2, slab + 2)), band(i)) for i in range(3)]
        for p in range(slab + 2):
            terms = [own[i][(p + i - 2) * n : (p + i - 1) * n] for i in range(3) if 0 <= p + i - 2 < slab]
            acc[p * n : (p + 1) * n] = functools.reduce(jnp.add, terms)
        arrive(halo[0])
        first = dot(planes(0, 1), band(0))
        middle = dot(planes(1, slab + 2), band(1))
        final = dot(planes(slab + 2, slab + 3), band(2))
        more = {0: first[:n] + middle[:n], 1: first[n:], slab: final[:n], slab + 1: middle[n:] + final[n:]}
        return spill(
            jnp.concatenate(
                [acc[p * n : (p + 1) * n] + more[p] if p in more else acc[p * n : (p + 1) * n] for p in range(slab + 2)],
                axis=0,
            ),
            wide,
        )

    def silu(y):
        return (y * (0.5 * jnp.tanh(0.5 * y) + 0.5)).astype(BF16)

    def slope_of(y):
        return slope(y.astype(BF16).astype(F32))

    mine = (slab, rows)
    wide = (slab + 2, rows + 2)
    mirrored = [(2 - i, 2 - j) for i, j in OFFSETS]

    loads[3].wait()
    loads[4].wait()

    for pair in range(2):
        y = ahead_of_depth(2 * pair, xh, pair, halo, False)
        put_near(xo, pair, silu(y))
        y2 = forward(2 * pair + 1, windows(xo, pair, mine, 0, OFFSETS), mine)
        act = silu(y2)
        if pair == 0:
            xh[1, own_p, own_r] = act
            halo = send_halo(xh, 1, 1)
        else:
            for d in range(slab):
                tiles = act[d].reshape(plane, 128)
                hall[d][xpos] = tiles[:part_rows]
                far_out[d] = tiles[part_rows:]
            far = [
                send([(far_out.at[d], far_in.at[d], z_mate)], far_in.at[d], bz_s.at[d], bz_r.at[d]) for d in range(slab)
            ]
            act_x = [
                send(
                    [(hall[d].at[xpos], hall[d].at[xpos], x_mate(s)) for s in X_ORDER(nx)],
                    hall[d].at[some_x], ax_s.at[d], ax_r.at[d],
                )
                for d in range(slab)
            ]
            arrive(head_x)
            for d in range(slab):
                hzout[d] = hd[lax.div(match_ref[d, 2 * xpos + (1 - zhalf)], 2)]
            head_z = send([(hzout, hzin, z_mate)], hzin, z_s.at[slab], z_r.at[slab])
        slw[pair] = slope_of(y)
        slo[pair] = slope_of(y2)

    hidden = act.reshape(cells, 128)

    col_class = lax.broadcasted_iota(jnp.int32, (plane, 128), 1)
    real = col_class < classes
    spread_r = lax.broadcasted_iota(jnp.int32, (cells, slab * rows), 0)
    spread_c = lax.broadcasted_iota(jnp.int32, (cells, slab * rows), 1)
    spread = jnp.where(lax.div(spread_r, 16) == spread_c, 1.0, 0.0).astype(BF16)
    lab = nn(spread, lab_ref[...].reshape(slab * rows, 64).astype(F32).astype(BF16))
    vox = lax.broadcasted_iota(jnp.int32, (cells, 64), 1)
    own = lax.rem(lax.broadcasted_iota(jnp.int32, (cells, 64), 0), 16)
    lab = jnp.where(lax.div(vox, 4) == own, lab, 0.0).astype(BF16)
    pick_r = lax.broadcasted_iota(jnp.int32, (64, 512), 0)
    pick_c = lax.broadcasted_iota(jnp.int32, (64, 512), 1)
    pick = jnp.where(lax.rem(pick_r, 4) == lax.div(pick_c, 128), 1.0, 0.0).astype(BF16)
    class_of = nn(lab, pick)

    def softmax(act_plane, heads):
        logits = nn(act_plane, heads)
        out = []
        for a in range(4):
            ex = jnp.where(real, jnp.exp(logits[:, a * 128 : (a + 1) * 128]), 0.0)
            out.append(ex / jnp.sum(ex, axis=1, keepdims=True))
        return out

    col_f = col_class.astype(F32)
    for d in range(slab):
        probs = softmax(hidden[d * plane : (d + 1) * plane], hcat[...])
        for a in range(4):
            mark = jnp.where(class_of[d * plane : (d + 1) * plane, a * 128 : (a + 1) * 128] == col_f, 0.5, 0.0)
            part[d, :, a * 128 : (a + 1) * 128] = probs[a] - mark

    act_z = []
    for d in range(slab):
        arrive(act_x[d])
        zout[d] = hall[d][lax.div(match_ref[d, 2 * xpos + (1 - zhalf)], 2)]
        act_z.append(send([(zout.at[d], zin.at[d], z_mate)], zin.at[d], z_s.at[d], z_r.at[d]))
    act_b = []
    for d in range(slab):
        arrive(far[d])
        for s in range(nx):
            source = match_ref[d, 2 * lax.rem(xpos + s, nx) + zhalf]
            chosen = jnp.where(
                lax.rem(source, 2) == zhalf, far_out[d].astype(F32), far_in[d].astype(F32)
            ).astype(BF16)
            if s == 0:
                pick_in[d][xpos] = chosen
            else:
                pick_out[s, d] = chosen
        act_b.append(
            send(
                [(pick_out.at[s, d], pick_in[d].at[xpos], x_mate(s)) for s in X_ORDER(nx)],
                pick_in[d].at[some_x], bx_s.at[d], bx_r.at[d],
            )
        )
    arrive(head_z)
    at_x, is_near = [], []
    for d in range(slab):
        source = match_ref[d, peer]
        is_near.append(lax.rem(source, 2) == zhalf)
        at_x.append(lax.div(source, 2))
        target_head = jnp.where(is_near[d], hd[at_x[d]].astype(F32), hzin[d].astype(F32)).astype(BF16)
        for a in range(4):
            tcat[d, a * 32 : (a + 1) * 32, a * 128 : (a + 1) * 128] = target_head
    g_planes, grad_rows = [], []
    for d in range(slab):
        arrive(act_z[d])
        arrive(act_b[d])
        target_act = jnp.concatenate(
            [
                jnp.where(is_near[d], hall[d][at_x[d]].astype(F32), zin[d].astype(F32)).astype(BF16),
                pick_in[d][at_x[d]],
            ],
            axis=0,
        )
        target = softmax(target_act, tcat[d])
        grad = jnp.concatenate(
            [
                (part[d, :, a * 128 : (a + 1) * 128] - 0.5 * target[a].astype(BF16).astype(F32)).astype(BF16)
                for a in range(4)
            ],
            axis=1,
        )
        grad_rows.append(grad)
        g_d = nt(grad, hcat[...]).reshape(rows, 16, 128) * slo[1, d]
        gh[1, 2 + d, own_r] = g_d.astype(BF16)
        g_planes.append(g_d)
    halo = send_halo(gh, 1, 3)
    dlogits = jnp.concatenate(grad_rows, axis=0)
    g = jnp.stack(g_planes)

    group32 = lax.div(lax.broadcasted_iota(jnp.int32, (32, 128), 1), 32)
    group288 = lax.div(lax.broadcasted_iota(jnp.int32, (288, 128), 1), 32)
    own_chunks = 8 // nr
    from_next = lane < 32
    from_last = lane >= 96

    def weight_grad(layer, g, cols):
        g = g.reshape(-1, 16, 128)
        ahead = jnp.where(from_next & (block < 15), pltpu.roll(g, 15, 1), 0.0)
        edge = jnp.where(from_last & (block > 0), pltpu.roll(g, 1, 1), ahead)
        both = jnp.concatenate([g.reshape(cells, 128), edge.reshape(cells, 128)], axis=1).astype(BF16).T
        prod = nn(jnp.concatenate([both[0:160], both[224:256]], axis=0), cols)

        def take(at):
            return jnp.concatenate([prod[at : at + 32, ij * 128 : (ij + 1) * 128] for ij in range(9)], axis=0)

        s0 = jnp.where(group288 == 3, take(128), take(0))
        s3 = jnp.where(group288 == 0, take(160), take(96))
        total = take(32) + pltpu.roll(s0, 32, 1) + pltpu.roll(take(64), 96, 1) + pltpu.roll(s3, 64, 1)
        for t in range(7):
            tile = None
            ks = [(gr, *divmod(4 * t + gr, 3)) for gr in range(4) if 4 * t + gr < 27]
            for ij in sorted({ij for _, ij, _ in ks}):
                first = [(gr, k) for gr, at, k in ks if at == ij][0]
                moved = rolled(total[ij * 32 : (ij + 1) * 32], first[0] - first[1])
                tile = moved if tile is None else jnp.where(group32 >= first[0], moved, tile)
            pk[layer, t // own_chunks, t % own_chunks] = tile.astype(BF16)
        if layer < layers - 1:
            pk[layer, 7 // own_chunks, 7 % own_chunks] = jnp.zeros((32, 128), BF16)

    def span(layer_set):
        return pl.ds(layer_set[0], len(layer_set)), min(layer_set[0], layers - 2)

    def send_row(layer_set):
        at, n = span(layer_set)
        return send(
            [(pk.at[at, lax.rem(row + s, nr)], rsin.at[at, s], row_mate(s)) for s in range(1, nr)],
            rsin.at[at, pl.ds(1, nr - 1)], rs_s.at[n], rs_r.at[n],
        )

    def send_depth(layer_set, whole):
        arrive(whole)
        at, n = span(layer_set)
        for layer in layer_set:
            total = pk[layer, row].astype(F32)
            for s in range(1, nr):
                total = total + rsin[layer, s].astype(F32)
            dep[layer, depth] = total.astype(BF16)
        return send(
            [(dep.at[at, depth], dep.at[at, depth], depth_mate(s)) for s in range(1, nd)],
            dep.at[at, pl.ds(0, nd - 1)], dp_s.at[n], dp_r.at[n],
        )

    def send_all(layer_set, whole):
        arrive(whole)
        at, n = span(layer_set)
        for layer in layer_set:
            total = dep[layer, 0].astype(F32)
            for s in range(1, nd):
                total = total + dep[layer, s].astype(F32)
            fin[layer, row] = total.astype(BF16)
        return send(
            [(fin.at[at, row], fin.at[at, row], row_mate(s)) for s in range(1, nr)],
            fin.at[at, pl.ds(0, nr - 1)], ag_s.at[n], ag_r.at[n],
        )

    def finish(layer_set, whole):
        arrive(whole)
        for layer in layer_set:
            for t in range(7):
                lanes = min(128, 27 * 32 - t * 128)
                cg_ref[layer, :, t * 128 : t * 128 + lanes] = fin[layer, t // own_chunks, t % own_chunks].astype(F32)[:, :lanes]
            if layer == layers - 1:
                hg_ref[...] = fin[layer, 7 // own_chunks, 7 % own_chunks].astype(F32)[:, :classes]

    wide_heads = nn(hidden.T, dlogits)
    heads = wide_heads[0:32, 0:128]
    for a in range(1, 4):
        heads = heads + wide_heads[a * 32 : (a + 1) * 32, a * 128 : (a + 1) * 128]
    pk[3, 7 // own_chunks, 7 % own_chunks] = heads.astype(BF16)
    weight_grad(3, g, windows(xo, 1, mine, 0, OFFSETS))
    first = send_row([3])
    g3 = ahead_of_depth(3, gh, 1, halo, True) * slw[1]
    put_near(go, 1, g3)
    g2 = backward(2, windows(go, 1, mine, 0, mirrored), mine) * slo[0]
    gh[0, own_p, own_r] = g2.astype(BF16)
    halo = send_halo(gh, 0, 2)
    weight_grad(2, g3[1 : slab + 1, 1 : rows + 1], windows(xh, 1, mine, 1, OFFSETS))
    weight_grad(1, g2, windows(xo, 0, mine, 0, OFFSETS))
    second = send_row([1, 2])
    first = send_depth([3], first)
    g1 = ahead_of_depth(1, gh, 0, halo, True) * slw[0]
    put_near(go, 0, g1)
    first = send_all([3], first)
    weight_grad(0, g1[1 : slab + 1, 1 : rows + 1], windows(xh, 0, mine, 1, OFFSETS))
    last = send_row([0])
    second = send_depth([1, 2], second)
    back = backward(0, windows(go, 0, mine, 0, mirrored), mine)
    tmp[...] = back.reshape(cells, 128)
    for d in range(slab):
        for b in range(16):
            ig_ref[d, :, b * 128 : (b + 1) * 128] = tmp[pl.ds(d * plane + b, rows, stride=16), :].astype(BF16)
    last = send_depth([0], last)
    second = send_all([1, 2], second)
    finish([3], first)
    last = send_all([0], last)
    finish([1, 2], second)
    for whole in started:
        whole.wait_send()
    finish([0], last)


def write_out(cg_ref, hg_ref, ig_ref, cg_out, hg_out, ig_out, sem):
    copies = [
        pltpu.make_async_copy(src, dst, sem.at[n])
        for n, (src, dst) in enumerate(
            [(cg_ref.at[i], cg_out.at[i]) for i in range(cg_ref.shape[0])] + [(ig_ref, ig_out), (hg_ref, hg_out)]
        )
    ]
    for copy in copies:
        copy.start()
    for copy in copies:
        copy.wait()


def X_ORDER(nx):
    return [s for s in (2, 1, 3) if s < nx]


def solution(mesh):
    np_, nd, nr = mesh.shape["peer"], mesh.shape["depth"], mesh.shape["row"]
    nx = np_ // 2

    def body(features, labels, conv_weights, head_weights, matching):
        slab, rows, merged = features.shape
        layers = conv_weights.shape[1]
        classes = head_weights.shape[2]
        cells = slab * rows * 16
        chunk = (8 // nr, 32, 128)
        far = (2, slab + 8, rows + 8, 16, 128)
        close = (2, slab + 4, rows + 4, 16, 128)
        vmem = pl.BlockSpec(memory_space=pltpu.VMEM)
        hbm = pl.BlockSpec(memory_space=pltpu.HBM)
        dma = pltpu.SemaphoreType.DMA
        scratch = [
            pltpu.VMEM((slab, rows, merged), BF16),
            pltpu.VMEM((slab, rows, merged // 32), jnp.int32),
            pltpu.VMEM((layers, 32, 27 * 32), BF16),
            pltpu.VMEM((32, classes), BF16),
            pltpu.SMEM((slab, np_), jnp.int32),
            pltpu.VMEM(far, BF16),
            pltpu.VMEM(far, BF16),
            pltpu.VMEM(close, BF16),
            pltpu.VMEM(close, BF16),
            pltpu.VMEM((9, 2, 4, layers * 32, 128), BF16),
            pltpu.VMEM((layers * 32, 896), F32),
            pltpu.VMEM((cells, 128), F32),
            pltpu.VMEM((2, slab, rows, 16, 128), F32),
            pltpu.VMEM((2, slab + 2, rows + 2, 16, 128), F32),
            pltpu.VMEM((128, 512), BF16),
            pltpu.VMEM((slab, 128, 512), BF16),
            pltpu.VMEM((nx, 32, 128), BF16),
            pltpu.VMEM((slab, 32, 128), BF16),
            pltpu.VMEM((slab, 32, 128), BF16),
            [pltpu.VMEM((nx, rows * 8, 128), BF16) for _ in range(slab)],
            pltpu.VMEM((slab, rows * 8, 128), BF16),
            pltpu.VMEM((slab, rows * 8, 128), BF16),
            pltpu.VMEM((slab, rows * 8, 128), BF16),
            pltpu.VMEM((slab, rows * 8, 128), BF16),
            [pltpu.VMEM((nx, rows * 8, 128), BF16) for _ in range(slab)],
            pltpu.VMEM((nx, slab, rows * 8, 128), BF16),
            pltpu.VMEM(((slab + 2) * (rows + 2) * 16, 256), F32),
            pltpu.VMEM((slab, rows * 16, 512), F32),
            pltpu.VMEM((layers, nr) + chunk, BF16),
            pltpu.VMEM((layers, nr) + chunk, BF16),
            pltpu.VMEM((layers, nd) + chunk, BF16),
            pltpu.VMEM((layers, nr) + chunk, BF16),
            dma((5,)),
            dma((4, 2)), dma((4, 2)),
            dma((1,)), dma((1,)),
            dma((slab,)), dma((slab,)),
            dma((slab + 1,)), dma((slab + 1,)),
            dma((slab,)), dma((slab,)),
            dma((slab,)), dma((slab,)),
            dma((layers - 1,)), dma((layers - 1,)),
            dma((layers - 1,)), dma((layers - 1,)),
            dma((layers - 1,)), dma((layers - 1,)),
        ]
        sizes = (nx, nd, nr, slab, rows, classes, layers)
        cg, hg, ig = pl.pallas_call(
            functools.partial(kernel, sizes),
            out_shape=(
                pltpu.VMEM((layers, 32, 27 * 32), F32),
                pltpu.VMEM((32, classes), F32),
                pltpu.VMEM((slab, rows, merged), BF16),
            ),
            in_specs=[hbm] * 5,
            out_specs=(vmem,) * 3,
            scratch_shapes=scratch,
            compiler_params=pltpu.CompilerParams(collective_id=0, has_side_effects=True, vmem_limit_bytes=40 * 2**20),
        )(
            *(
                pltpu.with_memory_space_constraint(v, pltpu.HBM)
                for v in (features, labels, conv_weights[0].transpose(0, 2, 1), head_weights[0], matching)
            )
        )
        cg, hg, ig = pl.pallas_call(
            write_out,
            out_shape=tuple(jax.ShapeDtypeStruct(v.shape, v.dtype) for v in (cg, hg, ig)),
            in_specs=[vmem] * 3,
            out_specs=(hbm,) * 3,
            scratch_shapes=[dma((layers + 2,))],
            compiler_params=pltpu.CompilerParams(vmem_limit_bytes=2**20),
        )(cg, hg, ig)
        return cg.transpose(0, 2, 1)[None], hg[None], ig[None]

    return jax.shard_map(
        body,
        mesh=mesh,
        in_specs=(
            P("depth", "row", None),
            P("depth", "row", None),
            P("peer", None, None, None),
            P("peer", None, None),
            P("depth", None),
        ),
        out_specs=(
            P("peer", None, None, None),
            P("peer", None, None),
            P("peer", "depth", "row", None),
        ),
        check_vma=False,
    )
```

```python
import functools

import jax
import jax.numpy as jnp
from jax import lax
from jax.experimental import pallas as pl
from jax.experimental.pallas import tpu as pltpu
from jax.sharding import PartitionSpec as P

MESH = pl.DeviceIdType.MESH
F32 = jnp.float32
BF16 = jnp.bfloat16
OFFSETS = [(i, j) for i in range(3) for j in range(3)]
NEIGHBOURS = [(1, 1), (1, -1), (-1, 1), (-1, -1), (1, 0), (-1, 0), (0, 1), (0, -1)]


def nt(a, b):
    return lax.dot_general(a, b, (((1,), (1,)), ((), ())), preferred_element_type=F32)


def nn(a, b):
    return lax.dot_general(a, b, (((1,), (0,)), ((), ())), preferred_element_type=F32)


def slope(pre):
    s = 0.5 * jnp.tanh(0.5 * pre) + 0.5
    return s * (1.0 + pre * (1.0 - s))


def kernel(
    sizes,
    x_any, lab_any, w_any, head_any, match_any,
    cg_ref, hg_ref, ig_ref,
    x_ref, lab_ref, w_ref, head_ref, match_ref,
    xh, gh, xo, go, wt, wpad, tmp, slo, slw, hcat, tcat, hd, hzin, hzout, hall, zin, zout, far_in, far_out, pick_in, pick_out, acc, part,
    pk, rsin, dep, fin,
    in_s, halo_s, halo_r, hx_s, hx_r, ax_s, ax_r, z_s, z_r, bx_s, bx_r, bz_s, bz_r, rs_s, rs_r, dp_s, dp_r, ag_s, ag_r,
):
    nx, nd, nr, slab, rows, classes, layers = sizes
    cells = slab * rows * 16
    plane = rows * 16
    part_rows = plane // 2
    own_p, own_r = slice(2, slab + 2), slice(2, rows + 2)
    peer = lax.axis_index("peer")
    depth = lax.axis_index("depth")
    row = lax.axis_index("row")
    xpos, zhalf = lax.div(peer, 2), lax.rem(peer, 2)
    zpos = zhalf * nd + depth

    def near(dp, dr):
        where = {}
        if dr:
            where["row"] = lax.rem(row + dr + nr, nr)
        if dp:
            z = lax.rem(zpos + dp + 2 * nd, 2 * nd)
            where["peer"] = 2 * xpos + lax.div(z, nd)
            where["depth"] = lax.rem(z, nd)
        return where

    def x_mate(s):
        return {"peer": 2 * lax.rem(xpos + s, nx) + zhalf}

    z_mate = {"peer": 2 * xpos + (1 - zhalf)}

    def row_mate(s):
        return {"row": lax.rem(row + s, nr)}

    def depth_mate(s):
        return {"depth": lax.rem(depth + s, nd)}

    loads = [
        pltpu.make_async_copy(src, dst, in_s.at[n])
        for n, (src, dst) in enumerate(
            [(x_any, x_ref), (head_any, head_ref), (w_any, w_ref), (lab_any, lab_ref), (match_any, match_ref)]
        )
    ]
    for load in loads:
        load.start()

    mates = [near(*step) for step in NEIGHBOURS] + [near(2, 0), near(-2, 0)]
    mates += [x_mate(s) for s in range(1, nx)]
    mates += [row_mate(s) for s in range(2, nr - 1)]
    barrier = pltpu.get_barrier_semaphore()
    for mate in mates:
        pl.semaphore_signal(barrier, inc=1, device_id=mate, device_id_type=MESH)

    started = []

    def remote(src, dst, send, recv, mate):
        return pltpu.make_async_remote_copy(
            src_ref=src, dst_ref=dst, send_sem=send, recv_sem=recv, device_id=mate, device_id_type=MESH
        )

    def send(jobs, total, send_sem, recv_sem):
        for src, dst, mate in jobs:
            remote(src, dst, send_sem, recv_sem, mate).start()
        if jobs:
            whole = remote(total, total, send_sem, recv_sem, jobs[0][2])
            started.append(whole)
            return whole

    def arrive(whole):
        if whole is not None:
            whole.wait_recv()

    loads[0].wait()
    for d in range(slab):
        for b in range(16):
            tmp[pl.ds(d * plane + b, rows, stride=16), :] = x_ref[d, :, b * 128 : (b + 1) * 128].astype(F32)
    xh[0, own_p, own_r] = tmp[...].reshape(slab, rows, 16, 128).astype(BF16)

    loads[1].wait()
    tmp[0:32, :] = jnp.zeros((32, 128), F32)
    tmp[0:32, 0:classes] = head_ref[...].astype(F32)
    head = tmp[0:32, :].astype(BF16)
    hd[xpos] = head

    pl.semaphore_wait(barrier, len(mates))

    def send_halo(buf, at, ex):
        def job(dp, dr, step):
            if dp == 0:
                src_p, dst_p = pl.ds(2, slab), pl.ds(2, slab)
            elif dp == 1:
                src_p = pl.ds(slab + 1 - step, 1)
                dst_p = pl.ds(jnp.where(depth == nd - 1, slab + 4, 0) + 1 - step, 1)
            else:
                src_p = pl.ds(2 + step, 1)
                dst_p = pl.ds(jnp.where(depth == 0, slab + 6, slab + 2) + step, 1)
            if dr == 0:
                src_r, dst_r = pl.ds(2, rows), pl.ds(2, rows)
            elif dr == 1:
                src_r = pl.ds(rows, 2)
                dst_r = pl.ds(jnp.where(row == nr - 1, rows + 4, 0), 2)
            else:
                src_r = pl.ds(2, 2)
                dst_r = pl.ds(jnp.where(row == 0, rows + 6, rows + 2), 2)
            return buf.at[at, src_p, src_r], buf.at[at, dst_p, dst_r], near(dp, dr)

        beside = send(
            [job(*step, 0) for step in NEIGHBOURS[6:]], buf.at[at, pl.ds(0, slab), pl.ds(0, 4)], halo_s.at[ex, 2], halo_r.at[ex, 2]
        )
        planes = [
            send(
                [job(*step, n) for step in NEIGHBOURS[:6]],
                buf.at[at, pl.ds(0, 2), pl.ds(0, rows + 4)], halo_s.at[ex, n], halo_r.at[ex, n],
            )
            for n in range(2)
        ]
        return beside, *planes

    halo = send_halo(xh, 0, 0)
    some_x = pl.ds(0, nx - 1)
    head_x = send(
        [(hd.at[xpos], hd.at[xpos], x_mate(s)) for s in range(1, nx)], hd.at[some_x], hx_s.at[0], hx_r.at[0]
    )

    def clear_wide(buf, at):
        zero_p = jnp.zeros((2, rows + 4, 16, 128), BF16)
        buf[at, pl.ds(jnp.where(depth == 0, 0, slab + 4), 2), 0 : rows + 4] = zero_p
        buf[at, pl.ds(jnp.where(depth == nd - 1, slab + 2, slab + 6), 2), 0 : rows + 4] = zero_p
        zero_r = jnp.zeros((slab + 4, 2, 16, 128), BF16)
        buf[at, 0 : slab + 4, pl.ds(jnp.where(row == 0, 0, rows + 4), 2)] = zero_r
        buf[at, 0 : slab + 4, pl.ds(jnp.where(row == nr - 1, rows + 2, rows + 6), 2)] = zero_r

    def clear_near(buf, at):
        zero_p = jnp.zeros((1, rows + 2, 16, 128), BF16)
        buf[at, pl.ds(jnp.where(depth == 0, 0, slab + 2), 1), 0 : rows + 2] = zero_p
        buf[at, pl.ds(jnp.where(depth == nd - 1, slab + 1, slab + 3), 1), 0 : rows + 2] = zero_p
        zero_r = jnp.zeros((slab + 2, 1, 16, 128), BF16)
        buf[at, 0 : slab + 2, pl.ds(jnp.where(row == 0, 0, rows + 2), 1)] = zero_r
        buf[at, 0 : slab + 2, pl.ds(jnp.where(row == nr - 1, rows + 1, rows + 3), 1)] = zero_r

    for at in range(2):
        clear_wide(xh, at)
        clear_wide(gh, at)
    hcat[...] = jnp.zeros_like(hcat)
    tcat[...] = jnp.zeros_like(tcat)
    for a in range(4):
        hcat[a * 32 : (a + 1) * 32, a * 128 : (a + 1) * 128] = head

    lane = lax.broadcasted_iota(jnp.int32, (1, 16, 128), 2)
    block = lax.broadcasted_iota(jnp.int32, (1, 16, 128), 1)
    low = lane < 64
    inside = jnp.where(low, block, 15 - block) > 0

    def spill(y, shape):
        e = y[:, 128:].reshape(-1, 16, 128)
        moved = jnp.where(low, pltpu.roll(e, 1, 1), pltpu.roll(e, 15, 1))
        return (y[:, :128].reshape(-1, 16, 128) + jnp.where(inside, moved, 0.0)).reshape(*shape, 16, 128)

    loads[2].wait()
    wpad[:, 0 : 27 * 32] = w_ref[...].reshape(layers * 32, 27 * 32).astype(F32)
    wt[:, 1, 1:3] = jnp.zeros((9, 2, layers * 32, 128), BF16)
    group = lax.div(lax.broadcasted_iota(jnp.int32, (layers * 32, 128), 1), 32)

    def rolled(v, groups):
        shift = (groups * 32) % 128
        return v if shift == 0 else pltpu.roll(v, shift, 1)

    for ij in range(9):
        blk = None
        for k in range(3):
            t, g = divmod(3 * ij + k, 4)
            piece = rolled(wpad[:, t * 128 : (t + 1) * 128], k - g)
            blk = piece if blk is None else jnp.where(group == k, piece, blk)
        r0 = rolled(blk, -1)
        wt[ij, 0, 0] = jnp.where(group < 2, r0, 0.0).astype(BF16)
        wt[ij, 1, 0] = jnp.where(group == 3, r0, 0.0).astype(BF16)
        wt[ij, 0, 1] = jnp.where(group < 3, blk, 0.0).astype(BF16)
        wt[ij, 0, 2] = jnp.where(group > 0, rolled(blk, 1), 0.0).astype(BF16)
        r3 = rolled(blk, 2)
        wt[ij, 0, 3] = jnp.where(group > 1, r3, 0.0).astype(BF16)
        wt[ij, 1, 3] = jnp.where(group == 0, r3, 0.0).astype(BF16)

    def weights(layer, ij, half):
        return wt[ij, half, :, layer * 32 : (layer + 1) * 32, :].reshape(128, 128)

    def windows(buf, at, shape, base, order):
        return jnp.concatenate(
            [
                buf[at, base + i : base + i + shape[0], base + j : base + j + shape[1]].reshape(-1, 128)
                for i, j in order
            ],
            axis=1,
        )

    def forward(layer, cols, shape):
        band = jnp.concatenate(
            [jnp.concatenate([weights(layer, ij, 0), weights(layer, ij, 1)], axis=0) for ij in range(9)], axis=1
        )
        return spill(nt(cols, band), shape)

    def backward(layer, cols, shape):
        band = jnp.concatenate(
            [jnp.concatenate([weights(layer, ij, 0), weights(layer, ij, 1)], axis=1) for ij in range(9)], axis=0
        )
        return spill(nn(cols, band), shape)

    def ahead_of_depth(layer, buf, at, halo, back, emit):
        def planes(*ps):
            return jnp.concatenate(
                [
                    jnp.concatenate([buf[at, p, j : j + rows + 2].reshape(-1, 128) for p in ps], axis=0)
                    for j in range(3)
                ],
                axis=1,
            )

        def band(i):
            if back:
                at_ij = [3 * (2 - i) + 2 - j for j in range(3)]
                return jnp.concatenate(
                    [jnp.concatenate([weights(layer, ij, 0), weights(layer, ij, 1)], axis=1) for ij in at_ij], axis=0
                )
            return jnp.concatenate(
                [
                    jnp.concatenate([weights(layer, 3 * i + j, 0), weights(layer, 3 * i + j, 1)], axis=0)
                    for j in range(3)
                ],
                axis=1,
            )

        dot = nn if back else nt
        n = (rows + 2) * 16
        arrive(halo[0])
        own = [dot(planes(*range(2, slab + 2)), band(i)) for i in range(3)]
        for p in range(slab + 2):
            terms = [own[i][(p + i - 2) * n : (p + i - 1) * n] for i in range(3) if 0 <= p + i - 2 < slab]
            acc[p * n : (p + 1) * n] = functools.reduce(jnp.add, terms)
        arrive(halo[1])
        inner = [
            acc[n : 2 * n] + dot(planes(1), band(0)),
            acc[2 * n : slab * n],
            acc[slab * n : (slab + 1) * n] + dot(planes(slab + 2), band(2)),
        ]
        emit(spill(jnp.concatenate(inner, axis=0), (slab, rows + 2)), 1)
        middle = dot(planes(1, slab + 2), band(1))
        acc[0:n] = acc[0:n] + middle[:n]
        acc[(slab + 1) * n : (slab + 2) * n] = acc[(slab + 1) * n : (slab + 2) * n] + middle[n:]
        yield
        arrive(halo[2])
        emit(spill(acc[0:n] + dot(planes(0), band(0)), (1, rows + 2)), 0)
        emit(spill(acc[(slab + 1) * n : (slab + 2) * n] + dot(planes(slab + 3), band(2)), (1, rows + 2)), slab + 1)

    def silu(y):
        return (y * (0.5 * jnp.tanh(0.5 * y) + 0.5)).astype(BF16)

    def slope_of(y):
        return slope(y.astype(BF16).astype(F32))

    mine = (slab, rows)
    mirrored = [(2 - i, 2 - j) for i, j in OFFSETS]

    loads[3].wait()
    loads[4].wait()

    for pair in range(2):
        wide_y = {}

        def emit_act(y, p, pair=pair, wide_y=wide_y):
            xo[pair, p : p + y.shape[0], 0 : rows + 2] = silu(y)
            wide_y[p] = y

        for _ in ahead_of_depth(2 * pair, xh, pair, halo, False, emit_act):
            pass
        clear_near(xo, pair)
        y2 = forward(2 * pair + 1, windows(xo, pair, mine, 0, OFFSETS), mine)
        act = silu(y2)
        if pair == 0:
            xh[1, own_p, own_r] = act
            halo = send_halo(xh, 1, 1)
        else:
            for d in range(slab):
                tiles = act[d].reshape(plane, 128)
                hall[d][xpos] = tiles[:part_rows]
                far_out[d] = tiles[part_rows:]
            far = [
                send([(far_out.at[d], far_in.at[d], z_mate)], far_in.at[d], bz_s.at[d], bz_r.at[d]) for d in range(slab)
            ]
            act_x = [
                send(
                    [(hall[d].at[xpos], hall[d].at[xpos], x_mate(s)) for s in X_ORDER(nx)],
                    hall[d].at[some_x], ax_s.at[d], ax_r.at[d],
                )
                for d in range(slab)
            ]
            arrive(head_x)
            for d in range(slab):
                hzout[d] = hd[lax.div(match_ref[d, 2 * xpos + (1 - zhalf)], 2)]
            head_z = send([(hzout, hzin, z_mate)], hzin, z_s.at[slab], z_r.at[slab])
        for p, y in wide_y.items():
            slw[pair, p : p + y.shape[0]] = slope_of(y)
        slo[pair] = slope_of(y2)

    hidden = act.reshape(cells, 128)

    col_class = lax.broadcasted_iota(jnp.int32, (plane, 128), 1)
    real = col_class < classes
    spread_r = lax.broadcasted_iota(jnp.int32, (cells, slab * rows), 0)
    spread_c = lax.broadcasted_iota(jnp.int32, (cells, slab * rows), 1)
    spread = jnp.where(lax.div(spread_r, 16) == spread_c, 1.0, 0.0).astype(BF16)
    lab = nn(spread, lab_ref[...].reshape(slab * rows, 64).astype(F32).astype(BF16))
    vox = lax.broadcasted_iota(jnp.int32, (cells, 64), 1)
    own = lax.rem(lax.broadcasted_iota(jnp.int32, (cells, 64), 0), 16)
    lab = jnp.where(lax.div(vox, 4) == own, lab, 0.0).astype(BF16)
    pick_r = lax.broadcasted_iota(jnp.int32, (64, 512), 0)
    pick_c = lax.broadcasted_iota(jnp.int32, (64, 512), 1)
    pick = jnp.where(lax.rem(pick_r, 4) == lax.div(pick_c, 128), 1.0, 0.0).astype(BF16)
    class_of = nn(lab, pick)

    def softmax(act_plane, heads):
        logits = nn(act_plane, heads)
        out = []
        for a in range(4):
            ex = jnp.where(real, jnp.exp(logits[:, a * 128 : (a + 1) * 128]), 0.0)
            out.append(ex / jnp.sum(ex, axis=1, keepdims=True))
        return out

    col_f = col_class.astype(F32)
    for d in range(slab):
        probs = softmax(hidden[d * plane : (d + 1) * plane], hcat[...])
        for a in range(4):
            mark = jnp.where(class_of[d * plane : (d + 1) * plane, a * 128 : (a + 1) * 128] == col_f, 0.5, 0.0)
            part[d, :, a * 128 : (a + 1) * 128] = probs[a] - mark

    act_z = []
    for d in range(slab):
        arrive(act_x[d])
        zout[d] = hall[d][lax.div(match_ref[d, 2 * xpos + (1 - zhalf)], 2)]
        act_z.append(send([(zout.at[d], zin.at[d], z_mate)], zin.at[d], z_s.at[d], z_r.at[d]))
    act_b = []
    for d in range(slab):
        arrive(far[d])
        for s in range(nx):
            source = match_ref[d, 2 * lax.rem(xpos + s, nx) + zhalf]
            chosen = jnp.where(
                lax.rem(source, 2) == zhalf, far_out[d].astype(F32), far_in[d].astype(F32)
            ).astype(BF16)
            if s == 0:
                pick_in[d][xpos] = chosen
            else:
                pick_out[s, d] = chosen
        act_b.append(
            send(
                [(pick_out.at[s, d], pick_in[d].at[xpos], x_mate(s)) for s in X_ORDER(nx)],
                pick_in[d].at[some_x], bx_s.at[d], bx_r.at[d],
            )
        )
    arrive(head_z)
    at_x, is_near = [], []
    for d in range(slab):
        source = match_ref[d, peer]
        is_near.append(lax.rem(source, 2) == zhalf)
        at_x.append(lax.div(source, 2))
        target_head = jnp.where(is_near[d], hd[at_x[d]].astype(F32), hzin[d].astype(F32)).astype(BF16)
        for a in range(4):
            tcat[d, a * 32 : (a + 1) * 32, a * 128 : (a + 1) * 128] = target_head
    g_planes, grad_rows = [], []
    for d in range(slab):
        for due in {0: [0], 1: range(1, slab)}.get(d, []):
            arrive(act_z[due])
            arrive(act_b[due])
        target_act = jnp.concatenate(
            [
                jnp.where(is_near[d], hall[d][at_x[d]].astype(F32), zin[d].astype(F32)).astype(BF16),
                pick_in[d][at_x[d]],
            ],
            axis=0,
        )
        target = softmax(target_act, tcat[d])
        grad = jnp.concatenate(
            [
                (part[d, :, a * 128 : (a + 1) * 128] - 0.5 * target[a].astype(BF16).astype(F32)).astype(BF16)
                for a in range(4)
            ],
            axis=1,
        )
        grad_rows.append(grad)
        g_d = nt(grad, hcat[...]).reshape(rows, 16, 128) * slo[1, d]
        gh[1, 2 + d, own_r] = g_d.astype(BF16)
        g_planes.append(g_d)
    halo = send_halo(gh, 1, 3)
    dlogits = jnp.concatenate(grad_rows, axis=0)
    g = jnp.stack(g_planes)

    group32 = lax.div(lax.broadcasted_iota(jnp.int32, (32, 128), 1), 32)
    group288 = lax.div(lax.broadcasted_iota(jnp.int32, (288, 128), 1), 32)
    own_chunks = 8 // nr
    from_next = lane < 32
    from_last = lane >= 96

    def weight_grad(layer, g, cols):
        g = g.reshape(-1, 16, 128)
        ahead = jnp.where(from_next & (block < 15), pltpu.roll(g, 15, 1), 0.0)
        edge = jnp.where(from_last & (block > 0), pltpu.roll(g, 1, 1), ahead)
        both = jnp.concatenate([g.reshape(cells, 128), edge.reshape(cells, 128)], axis=1).astype(BF16).T
        prod = nn(jnp.concatenate([both[0:160], both[224:256]], axis=0), cols)

        def take(at):
            return jnp.concatenate([prod[at : at + 32, ij * 128 : (ij + 1) * 128] for ij in range(9)], axis=0)

        s0 = jnp.where(group288 == 3, take(128), take(0))
        s3 = jnp.where(group288 == 0, take(160), take(96))
        total = take(32) + pltpu.roll(s0, 32, 1) + pltpu.roll(take(64), 96, 1) + pltpu.roll(s3, 64, 1)
        for t in range(7):
            tile = None
            ks = [(gr, *divmod(4 * t + gr, 3)) for gr in range(4) if 4 * t + gr < 27]
            for ij in sorted({ij for _, ij, _ in ks}):
                first = [(gr, k) for gr, at, k in ks if at == ij][0]
                moved = rolled(total[ij * 32 : (ij + 1) * 32], first[0] - first[1])
                tile = moved if tile is None else jnp.where(group32 >= first[0], moved, tile)
            pk[layer, t // own_chunks, t % own_chunks] = tile.astype(BF16)
        if layer < layers - 1:
            pk[layer, 7 // own_chunks, 7 % own_chunks] = jnp.zeros((32, 128), BF16)

    def span(layer_set):
        return pl.ds(layer_set[0], len(layer_set)), min(layer_set[0], layers - 2)

    far_first = sorted(range(1, nr), key=lambda s: -min(s, nr - s))

    def send_row(layer_set):
        at, n = span(layer_set)
        return send(
            [(pk.at[at, lax.rem(row + s, nr)], rsin.at[at, s], row_mate(s)) for s in far_first],
            rsin.at[at, pl.ds(1, nr - 1)], rs_s.at[n], rs_r.at[n],
        )

    def send_depth(layer_set, whole):
        arrive(whole)
        at, n = span(layer_set)
        for layer in layer_set:
            total = pk[layer, row].astype(F32)
            for s in range(1, nr):
                total = total + rsin[layer, s].astype(F32)
            dep[layer, depth] = total.astype(BF16)
        return send(
            [(dep.at[at, depth], dep.at[at, depth], depth_mate(s)) for s in range(1, nd)],
            dep.at[at, pl.ds(0, nd - 1)], dp_s.at[n], dp_r.at[n],
        )

    def send_all(layer_set, whole):
        arrive(whole)
        at, n = span(layer_set)
        for layer in layer_set:
            total = dep[layer, 0].astype(F32)
            for s in range(1, nd):
                total = total + dep[layer, s].astype(F32)
            fin[layer, row] = total.astype(BF16)
        return send(
            [(fin.at[at, row], fin.at[at, row], row_mate(s)) for s in far_first],
            fin.at[at, pl.ds(0, nr - 1)], ag_s.at[n], ag_r.at[n],
        )

    def finish(layer_set, whole):
        arrive(whole)
        for layer in layer_set:
            for t in range(7):
                lanes = min(128, 27 * 32 - t * 128)
                cg_ref[layer, :, t * 128 : t * 128 + lanes] = fin[layer, t // own_chunks, t % own_chunks].astype(F32)[:, :lanes]
            if layer == layers - 1:
                hg_ref[...] = fin[layer, 7 // own_chunks, 7 % own_chunks].astype(F32)[:, :classes]

    wide_heads = nn(hidden.T, dlogits)
    heads = wide_heads[0:32, 0:128]
    for a in range(1, 4):
        heads = heads + wide_heads[a * 32 : (a + 1) * 32, a * 128 : (a + 1) * 128]
    pk[3, 7 // own_chunks, 7 % own_chunks] = heads.astype(BF16)
    weight_grad(3, g, windows(xo, 1, mine, 0, OFFSETS))
    first = send_row([3])
    inner_g = {}

    def emit_grad(at):
        def emit(y, p):
            g = y * slw[at, p : p + y.shape[0]]
            go[at, p : p + y.shape[0], 0 : rows + 2] = g.astype(BF16)
            if p == 1:
                inner_g[at] = g[:, 1 : rows + 1]

        return emit

    for _ in ahead_of_depth(3, gh, 1, halo, True, emit_grad(1)):
        pass
    clear_near(go, 1)
    g2 = backward(2, windows(go, 1, mine, 0, mirrored), mine) * slo[0]
    gh[0, own_p, own_r] = g2.astype(BF16)
    halo = send_halo(gh, 0, 2)
    weight_grad(2, inner_g[1], windows(xh, 1, mine, 1, OFFSETS))
    weight_grad(1, g2, windows(xo, 0, mine, 0, OFFSETS))
    second = send_row([1, 2])
    first = send_depth([3], first)
    for _ in ahead_of_depth(1, gh, 0, halo, True, emit_grad(0)):
        weight_grad(0, inner_g[0], windows(xh, 0, mine, 1, OFFSETS))
        last = send_row([0])
    clear_near(go, 0)
    first = send_all([3], first)
    second = send_depth([1, 2], second)
    back = backward(0, windows(go, 0, mine, 0, mirrored), mine)
    tmp[...] = back.reshape(cells, 128)
    for d in range(slab):
        for b in range(16):
            ig_ref[d, :, b * 128 : (b + 1) * 128] = tmp[pl.ds(d * plane + b, rows, stride=16), :].astype(BF16)
    last = send_depth([0], last)
    second = send_all([1, 2], second)
    finish([3], first)
    last = send_all([0], last)
    finish([1, 2], second)
    for whole in started:
        whole.wait_send()
    finish([0], last)


def write_out(cg_ref, hg_ref, ig_ref, cg_out, hg_out, ig_out, sem):
    copies = [
        pltpu.make_async_copy(src, dst, sem.at[n])
        for n, (src, dst) in enumerate([(cg_ref, cg_out), (ig_ref, ig_out), (hg_ref, hg_out)])
    ]
    for copy in copies:
        copy.start()
    for copy in copies:
        copy.wait()


def X_ORDER(nx):
    return [s for s in (2, 1, 3) if s < nx]


def solution(mesh):
    np_, nd, nr = mesh.shape["peer"], mesh.shape["depth"], mesh.shape["row"]
    nx = np_ // 2

    def body(features, labels, conv_weights, head_weights, matching):
        slab, rows, merged = features.shape
        layers = conv_weights.shape[1]
        classes = head_weights.shape[2]
        cells = slab * rows * 16
        chunk = (8 // nr, 32, 128)
        far = (2, slab + 8, rows + 8, 16, 128)
        close = (2, slab + 4, rows + 4, 16, 128)
        vmem = pl.BlockSpec(memory_space=pltpu.VMEM)
        hbm = pl.BlockSpec(memory_space=pltpu.HBM)
        dma = pltpu.SemaphoreType.DMA
        scratch = [
            pltpu.VMEM((slab, rows, merged), BF16),
            pltpu.VMEM((slab, rows, merged // 32), jnp.int32),
            pltpu.VMEM((layers, 32, 27 * 32), BF16),
            pltpu.VMEM((32, classes), BF16),
            pltpu.SMEM((slab, np_), jnp.int32),
            pltpu.VMEM(far, BF16),
            pltpu.VMEM(far, BF16),
            pltpu.VMEM(close, BF16),
            pltpu.VMEM(close, BF16),
            pltpu.VMEM((9, 2, 4, layers * 32, 128), BF16),
            pltpu.VMEM((layers * 32, 896), F32),
            pltpu.VMEM((cells, 128), F32),
            pltpu.VMEM((2, slab, rows, 16, 128), F32),
            pltpu.VMEM((2, slab + 2, rows + 2, 16, 128), F32),
            pltpu.VMEM((128, 512), BF16),
            pltpu.VMEM((slab, 128, 512), BF16),
            pltpu.VMEM((nx, 32, 128), BF16),
            pltpu.VMEM((slab, 32, 128), BF16),
            pltpu.VMEM((slab, 32, 128), BF16),
            [pltpu.VMEM((nx, rows * 8, 128), BF16) for _ in range(slab)],
            pltpu.VMEM((slab, rows * 8, 128), BF16),
            pltpu.VMEM((slab, rows * 8, 128), BF16),
            pltpu.VMEM((slab, rows * 8, 128), BF16),
            pltpu.VMEM((slab, rows * 8, 128), BF16),
            [pltpu.VMEM((nx, rows * 8, 128), BF16) for _ in range(slab)],
            pltpu.VMEM((nx, slab, rows * 8, 128), BF16),
            pltpu.VMEM(((slab + 2) * (rows + 2) * 16, 256), F32),
            pltpu.VMEM((slab, rows * 16, 512), F32),
            pltpu.VMEM((layers, nr) + chunk, BF16),
            pltpu.VMEM((layers, nr) + chunk, BF16),
            pltpu.VMEM((layers, nd) + chunk, BF16),
            pltpu.VMEM((layers, nr) + chunk, BF16),
            dma((5,)),
            dma((4, 3)), dma((4, 3)),
            dma((1,)), dma((1,)),
            dma((slab,)), dma((slab,)),
            dma((slab + 1,)), dma((slab + 1,)),
            dma((slab,)), dma((slab,)),
            dma((slab,)), dma((slab,)),
            dma((layers - 1,)), dma((layers - 1,)),
            dma((layers - 1,)), dma((layers - 1,)),
            dma((layers - 1,)), dma((layers - 1,)),
        ]
        sizes = (nx, nd, nr, slab, rows, classes, layers)
        cg, hg, ig = pl.pallas_call(
            functools.partial(kernel, sizes),
            out_shape=(
                pltpu.VMEM((layers, 32, 27 * 32), F32),
                pltpu.VMEM((32, classes), F32),
                pltpu.VMEM((slab, rows, merged), BF16),
            ),
            in_specs=[hbm] * 5,
            out_specs=(vmem,) * 3,
            scratch_shapes=scratch,
            compiler_params=pltpu.CompilerParams(collective_id=0, has_side_effects=True, vmem_limit_bytes=40 * 2**20),
        )(
            *(
                pltpu.with_memory_space_constraint(v, pltpu.HBM)
                for v in (features, labels, conv_weights[0].transpose(0, 2, 1), head_weights[0], matching)
            )
        )
        cg, hg, ig = pl.pallas_call(
            write_out,
            out_shape=tuple(jax.ShapeDtypeStruct(v.shape, v.dtype) for v in (cg, hg, ig)),
            in_specs=[vmem] * 3,
            out_specs=(hbm,) * 3,
            scratch_shapes=[dma((3,))],
            compiler_params=pltpu.CompilerParams(vmem_limit_bytes=2**20),
        )(cg, hg, ig)
        return cg.transpose(0, 2, 1)[None], hg[None], ig[None]

    return jax.shard_map(
        body,
        mesh=mesh,
        in_specs=(
            P("depth", "row", None),
            P("depth", "row", None),
            P("peer", None, None, None),
            P("peer", None, None),
            P("depth", None),
        ),
        out_specs=(
            P("peer", None, None, None),
            P("peer", None, None),
            P("peer", "depth", "row", None),
        ),
        check_vma=False,
    )
```

```python
import functools

import jax
import jax.numpy as jnp
from jax import lax
from jax.experimental import pallas as pl
from jax.experimental.pallas import tpu as pltpu
from jax.sharding import PartitionSpec as P

MESH = pl.DeviceIdType.MESH
F32 = jnp.float32
BF16 = jnp.bfloat16
OFFSETS = [(i, j) for i in range(3) for j in range(3)]
NEIGHBOURS = [(1, 1), (1, -1), (-1, 1), (-1, -1), (1, 0), (-1, 0), (0, 1), (0, -1)]


def nt(a, b):
    return lax.dot_general(a, b, (((1,), (1,)), ((), ())), preferred_element_type=F32)


def nn(a, b):
    return lax.dot_general(a, b, (((1,), (0,)), ((), ())), preferred_element_type=F32)


def slope(pre):
    s = 0.5 * jnp.tanh(0.5 * pre) + 0.5
    return s * (1.0 + pre * (1.0 - s))


def kernel(
    sizes,
    x_any, lab_any, w_any, head_any, match_any,
    cg_ref, hg_ref, ig_ref,
    x_ref, lab_ref, w_ref, head_ref, match_ref,
    xh, gh, xo, go, wt, wpad, tmp, slo, slw, hcat, tcat, hd, hzin, hzout, hall, zin, zout, far_in, far_out, pick_in, pick_out, acc, part,
    pk, rsin, dep, fin,
    in_s, halo_s, halo_r, hx_s, hx_r, ax_s, ax_r, z_s, z_r, bx_s, bx_r, bz_s, bz_r, rs_s, rs_r, dp_s, dp_r, ag_s, ag_r,
):
    nx, nd, nr, slab, rows, classes, layers = sizes
    cells = slab * rows * 16
    plane = rows * 16
    part_rows = plane // 2
    own_p, own_r = slice(2, slab + 2), slice(2, rows + 2)
    peer = lax.axis_index("peer")
    depth = lax.axis_index("depth")
    row = lax.axis_index("row")
    xpos, zhalf = lax.div(peer, 2), lax.rem(peer, 2)
    zpos = zhalf * nd + depth

    def near(dp, dr):
        where = {}
        if dr:
            where["row"] = lax.rem(row + dr + nr, nr)
        if dp:
            z = lax.rem(zpos + dp + 2 * nd, 2 * nd)
            where["peer"] = 2 * xpos + lax.div(z, nd)
            where["depth"] = lax.rem(z, nd)
        return where

    def x_mate(s):
        return {"peer": 2 * lax.rem(xpos + s, nx) + zhalf}

    z_mate = {"peer": 2 * xpos + (1 - zhalf)}

    def row_mate(s):
        return {"row": lax.rem(row + s, nr)}

    def depth_mate(s):
        return {"depth": lax.rem(depth + s, nd)}

    loads = [
        pltpu.make_async_copy(src, dst, in_s.at[n])
        for n, (src, dst) in enumerate(
            [(x_any, x_ref), (head_any, head_ref), (w_any, w_ref), (lab_any, lab_ref), (match_any, match_ref)]
        )
    ]
    for load in loads:
        load.start()

    mates = [near(*step) for step in NEIGHBOURS] + [near(2, 0), near(-2, 0)]
    mates += [x_mate(s) for s in range(1, nx)]
    mates += [row_mate(s) for s in range(2, nr - 1)]
    barrier = pltpu.get_barrier_semaphore()
    for mate in mates:
        pl.semaphore_signal(barrier, inc=1, device_id=mate, device_id_type=MESH)

    started = []

    def remote(src, dst, send, recv, mate):
        return pltpu.make_async_remote_copy(
            src_ref=src, dst_ref=dst, send_sem=send, recv_sem=recv, device_id=mate, device_id_type=MESH
        )

    def send(jobs, total, send_sem, recv_sem):
        for src, dst, mate in jobs:
            remote(src, dst, send_sem, recv_sem, mate).start()
        if jobs:
            whole = remote(total, total, send_sem, recv_sem, jobs[0][2])
            started.append(whole)
            return whole

    def arrive(whole):
        if whole is not None:
            whole.wait_recv()

    loads[0].wait()
    for d in range(slab):
        for b in range(16):
            tmp[pl.ds(d * plane + b, rows, stride=16), :] = x_ref[d, :, b * 128 : (b + 1) * 128].astype(F32)
    xh[0, own_p, own_r] = tmp[...].reshape(slab, rows, 16, 128).astype(BF16)

    loads[1].wait()
    tmp[0:32, :] = jnp.zeros((32, 128), F32)
    tmp[0:32, 0:classes] = head_ref[...].astype(F32)
    head = tmp[0:32, :].astype(BF16)
    hd[xpos] = head

    pl.semaphore_wait(barrier, len(mates))

    def send_halo(buf, at, ex):
        def job(dp, dr, step):
            if dp == 0:
                src_p, dst_p = pl.ds(2, slab), pl.ds(2, slab)
            elif dp == 1:
                src_p = pl.ds(slab + 1 - step, 1)
                dst_p = pl.ds(jnp.where(depth == nd - 1, slab + 4, 0) + 1 - step, 1)
            else:
                src_p = pl.ds(2 + step, 1)
                dst_p = pl.ds(jnp.where(depth == 0, slab + 6, slab + 2) + step, 1)
            if dr == 0:
                src_r, dst_r = pl.ds(2, rows), pl.ds(2, rows)
            elif dr == 1:
                src_r = pl.ds(rows, 2)
                dst_r = pl.ds(jnp.where(row == nr - 1, rows + 4, 0), 2)
            else:
                src_r = pl.ds(2, 2)
                dst_r = pl.ds(jnp.where(row == 0, rows + 6, rows + 2), 2)
            return buf.at[at, src_p, src_r], buf.at[at, dst_p, dst_r], near(dp, dr)

        beside = send(
            [job(*step, 0) for step in NEIGHBOURS[6:]], buf.at[at, pl.ds(0, slab), pl.ds(0, 4)], halo_s.at[ex, 2], halo_r.at[ex, 2]
        )
        planes = [
            send(
                [job(*step, n) for step in NEIGHBOURS[:6]],
                buf.at[at, pl.ds(0, 2), pl.ds(0, rows + 4)], halo_s.at[ex, n], halo_r.at[ex, n],
            )
            for n in range(2)
        ]
        return beside, *planes

    halo = send_halo(xh, 0, 0)
    some_x = pl.ds(0, nx - 1)
    head_x = send(
        [(hd.at[xpos], hd.at[xpos], x_mate(s)) for s in range(1, nx)], hd.at[some_x], hx_s.at[0], hx_r.at[0]
    )

    def clear_wide(buf, at):
        zero_p = jnp.zeros((2, rows + 4, 16, 128), BF16)
        buf[at, pl.ds(jnp.where(depth == 0, 0, slab + 4), 2), 0 : rows + 4] = zero_p
        buf[at, pl.ds(jnp.where(depth == nd - 1, slab + 2, slab + 6), 2), 0 : rows + 4] = zero_p
        zero_r = jnp.zeros((slab + 4, 2, 16, 128), BF16)
        buf[at, 0 : slab + 4, pl.ds(jnp.where(row == 0, 0, rows + 4), 2)] = zero_r
        buf[at, 0 : slab + 4, pl.ds(jnp.where(row == nr - 1, rows + 2, rows + 6), 2)] = zero_r

    def clear_near(buf, at):
        zero_p = jnp.zeros((1, rows + 2, 16, 128), BF16)
        buf[at, pl.ds(jnp.where(depth == 0, 0, slab + 2), 1), 0 : rows + 2] = zero_p
        buf[at, pl.ds(jnp.where(depth == nd - 1, slab + 1, slab + 3), 1), 0 : rows + 2] = zero_p
        zero_r = jnp.zeros((slab + 2, 1, 16, 128), BF16)
        buf[at, 0 : slab + 2, pl.ds(jnp.where(row == 0, 0, rows + 2), 1)] = zero_r
        buf[at, 0 : slab + 2, pl.ds(jnp.where(row == nr - 1, rows + 1, rows + 3), 1)] = zero_r

    for at in range(2):
        clear_wide(xh, at)
        clear_wide(gh, at)
    hcat[...] = jnp.zeros_like(hcat)
    tcat[...] = jnp.zeros_like(tcat)
    for a in range(4):
        hcat[a * 32 : (a + 1) * 32, a * 128 : (a + 1) * 128] = head

    lane = lax.broadcasted_iota(jnp.int32, (1, 16, 128), 2)
    block = lax.broadcasted_iota(jnp.int32, (1, 16, 128), 1)
    low = lane < 64
    inside = jnp.where(low, block, 15 - block) > 0

    def spill(y, shape):
        e = y[:, 128:].reshape(-1, 16, 128)
        moved = jnp.where(low, pltpu.roll(e, 1, 1), pltpu.roll(e, 15, 1))
        return (y[:, :128].reshape(-1, 16, 128) + jnp.where(inside, moved, 0.0)).reshape(*shape, 16, 128)

    loads[2].wait()
    wpad[:, 0 : 27 * 32] = w_ref[...].reshape(layers * 32, 27 * 32).astype(F32)
    wt[:, 1, 1:3] = jnp.zeros((9, 2, layers * 32, 128), BF16)
    group = lax.div(lax.broadcasted_iota(jnp.int32, (layers * 32, 128), 1), 32)

    def rolled(v, groups):
        shift = (groups * 32) % 128
        return v if shift == 0 else pltpu.roll(v, shift, 1)

    for ij in range(9):
        blk = None
        for k in range(3):
            t, g = divmod(3 * ij + k, 4)
            piece = rolled(wpad[:, t * 128 : (t + 1) * 128], k - g)
            blk = piece if blk is None else jnp.where(group == k, piece, blk)
        r0 = rolled(blk, -1)
        wt[ij, 0, 0] = jnp.where(group < 2, r0, 0.0).astype(BF16)
        wt[ij, 1, 0] = jnp.where(group == 3, r0, 0.0).astype(BF16)
        wt[ij, 0, 1] = jnp.where(group < 3, blk, 0.0).astype(BF16)
        wt[ij, 0, 2] = jnp.where(group > 0, rolled(blk, 1), 0.0).astype(BF16)
        r3 = rolled(blk, 2)
        wt[ij, 0, 3] = jnp.where(group > 1, r3, 0.0).astype(BF16)
        wt[ij, 1, 3] = jnp.where(group == 0, r3, 0.0).astype(BF16)

    def weights(layer, ij, half):
        return wt[ij, half, :, layer * 32 : (layer + 1) * 32, :].reshape(128, 128)

    def windows(buf, at, shape, base, order):
        return jnp.concatenate(
            [
                buf[at, base + i : base + i + shape[0], base + j : base + j + shape[1]].reshape(-1, 128)
                for i, j in order
            ],
            axis=1,
        )

    def forward(layer, cols, shape):
        band = jnp.concatenate(
            [jnp.concatenate([weights(layer, ij, 0), weights(layer, ij, 1)], axis=0) for ij in range(9)], axis=1
        )
        return spill(nt(cols, band), shape)

    def backward(layer, cols, shape):
        band = jnp.concatenate(
            [jnp.concatenate([weights(layer, ij, 0), weights(layer, ij, 1)], axis=1) for ij in range(9)], axis=0
        )
        return spill(nn(cols, band), shape)

    def ahead_of_depth(layer, buf, at, halo, back, emit):
        def planes(*ps):
            return jnp.concatenate(
                [
                    jnp.concatenate([buf[at, p, j : j + rows + 2].reshape(-1, 128) for p in ps], axis=0)
                    for j in range(3)
                ],
                axis=1,
            )

        def band(i):
            if back:
                at_ij = [3 * (2 - i) + 2 - j for j in range(3)]
                return jnp.concatenate(
                    [jnp.concatenate([weights(layer, ij, 0), weights(layer, ij, 1)], axis=1) for ij in at_ij], axis=0
                )
            return jnp.concatenate(
                [
                    jnp.concatenate([weights(layer, 3 * i + j, 0), weights(layer, 3 * i + j, 1)], axis=0)
                    for j in range(3)
                ],
                axis=1,
            )

        dot = nn if back else nt
        n = (rows + 2) * 16
        arrive(halo[0])
        own = [dot(planes(*range(2, slab + 2)), band(i)) for i in range(3)]
        for p in range(slab + 2):
            terms = [own[i][(p + i - 2) * n : (p + i - 1) * n] for i in range(3) if 0 <= p + i - 2 < slab]
            acc[p * n : (p + 1) * n] = functools.reduce(jnp.add, terms)
        arrive(halo[1])
        inner = [
            acc[n : 2 * n] + dot(planes(1), band(0)),
            acc[2 * n : slab * n],
            acc[slab * n : (slab + 1) * n] + dot(planes(slab + 2), band(2)),
        ]
        emit(spill(jnp.concatenate(inner, axis=0), (slab, rows + 2)), 1)
        middle = dot(planes(1, slab + 2), band(1))
        acc[0:n] = acc[0:n] + middle[:n]
        acc[(slab + 1) * n : (slab + 2) * n] = acc[(slab + 1) * n : (slab + 2) * n] + middle[n:]
        yield
        arrive(halo[2])
        emit(spill(acc[0:n] + dot(planes(0), band(0)), (1, rows + 2)), 0)
        emit(spill(acc[(slab + 1) * n : (slab + 2) * n] + dot(planes(slab + 3), band(2)), (1, rows + 2)), slab + 1)

    def silu(y):
        return (y * (0.5 * jnp.tanh(0.5 * y) + 0.5)).astype(BF16)

    def slope_of(y):
        return slope(y.astype(BF16).astype(F32))

    mine = (slab, rows)
    mirrored = [(2 - i, 2 - j) for i, j in OFFSETS]

    loads[3].wait()
    loads[4].wait()

    for pair in range(2):
        wide_y = {}

        def emit_act(y, p, pair=pair, wide_y=wide_y):
            xo[pair, p : p + y.shape[0], 0 : rows + 2] = silu(y)
            wide_y[p] = y

        for _ in ahead_of_depth(2 * pair, xh, pair, halo, False, emit_act):
            pass
        clear_near(xo, pair)
        y2 = forward(2 * pair + 1, windows(xo, pair, mine, 0, OFFSETS), mine)
        act = silu(y2)
        if pair == 0:
            xh[1, own_p, own_r] = act
            halo = send_halo(xh, 1, 1)
        else:
            for d in range(slab):
                tiles = act[d].reshape(plane, 128)
                hall[d][xpos] = tiles[:part_rows]
                far_out[d] = tiles[part_rows:]
            far = [
                send([(far_out.at[d], far_in.at[d], z_mate)], far_in.at[d], bz_s.at[d], bz_r.at[d]) for d in range(slab)
            ]
            act_x = [
                send(
                    [(hall[d].at[xpos], hall[d].at[xpos], x_mate(s)) for s in X_ORDER(nx)],
                    hall[d].at[some_x], ax_s.at[d], ax_r.at[d],
                )
                for d in range(slab)
            ]
            arrive(head_x)
            for d in range(slab):
                hzout[d] = hd[lax.div(match_ref[d, 2 * xpos + (1 - zhalf)], 2)]
            head_z = send([(hzout, hzin, z_mate)], hzin, z_s.at[slab], z_r.at[slab])
        for p, y in wide_y.items():
            slw[pair, p : p + y.shape[0]] = slope_of(y)
        slo[pair] = slope_of(y2)

    hidden = act.reshape(cells, 128)

    col_class = lax.broadcasted_iota(jnp.int32, (plane, 128), 1)
    real = col_class < classes
    spread_r = lax.broadcasted_iota(jnp.int32, (cells, slab * rows), 0)
    spread_c = lax.broadcasted_iota(jnp.int32, (cells, slab * rows), 1)
    spread = jnp.where(lax.div(spread_r, 16) == spread_c, 1.0, 0.0).astype(BF16)
    lab = nn(spread, lab_ref[...].reshape(slab * rows, 64).astype(F32).astype(BF16))
    vox = lax.broadcasted_iota(jnp.int32, (cells, 64), 1)
    own = lax.rem(lax.broadcasted_iota(jnp.int32, (cells, 64), 0), 16)
    lab = jnp.where(lax.div(vox, 4) == own, lab, 0.0).astype(BF16)
    pick_r = lax.broadcasted_iota(jnp.int32, (64, 512), 0)
    pick_c = lax.broadcasted_iota(jnp.int32, (64, 512), 1)
    pick = jnp.where(lax.rem(pick_r, 4) == lax.div(pick_c, 128), 1.0, 0.0).astype(BF16)
    class_of = nn(lab, pick)

    def softmax(act_plane, heads):
        logits = nn(act_plane, heads)
        out = []
        for a in range(4):
            ex = jnp.where(real, jnp.exp(logits[:, a * 128 : (a + 1) * 128]), 0.0)
            out.append(ex / jnp.sum(ex, axis=1, keepdims=True))
        return out

    col_f = col_class.astype(F32)
    for d in range(slab):
        probs = softmax(hidden[d * plane : (d + 1) * plane], hcat[...])
        for a in range(4):
            mark = jnp.where(class_of[d * plane : (d + 1) * plane, a * 128 : (a + 1) * 128] == col_f, 0.5, 0.0)
            part[d, :, a * 128 : (a + 1) * 128] = probs[a] - mark

    act_z = []
    for d in range(slab):
        arrive(act_x[d])
        zout[d] = hall[d][lax.div(match_ref[d, 2 * xpos + (1 - zhalf)], 2)]
        act_z.append(send([(zout.at[d], zin.at[d], z_mate)], zin.at[d], z_s.at[d], z_r.at[d]))
    act_b = []
    for d in range(slab):
        arrive(far[d])
        for s in range(nx):
            source = match_ref[d, 2 * lax.rem(xpos + s, nx) + zhalf]
            chosen = jnp.where(
                lax.rem(source, 2) == zhalf, far_out[d].astype(F32), far_in[d].astype(F32)
            ).astype(BF16)
            if s == 0:
                pick_in[d][xpos] = chosen
            else:
                pick_out[s, d] = chosen
        act_b.append(
            send(
                [(pick_out.at[s, d], pick_in[d].at[xpos], x_mate(s)) for s in X_ORDER(nx)],
                pick_in[d].at[some_x], bx_s.at[d], bx_r.at[d],
            )
        )
    arrive(head_z)
    at_x, is_near = [], []
    for d in range(slab):
        source = match_ref[d, peer]
        is_near.append(lax.rem(source, 2) == zhalf)
        at_x.append(lax.div(source, 2))
        target_head = jnp.where(is_near[d], hd[at_x[d]].astype(F32), hzin[d].astype(F32)).astype(BF16)
        for a in range(4):
            tcat[d, a * 32 : (a + 1) * 32, a * 128 : (a + 1) * 128] = target_head
    g_planes, grad_rows = [], []
    for d in range(slab):
        for due in {0: [0], 1: range(1, slab)}.get(d, []):
            arrive(act_z[due])
            arrive(act_b[due])
        target_act = jnp.concatenate(
            [
                jnp.where(is_near[d], hall[d][at_x[d]].astype(F32), zin[d].astype(F32)).astype(BF16),
                pick_in[d][at_x[d]],
            ],
            axis=0,
        )
        target = softmax(target_act, tcat[d])
        grad = jnp.concatenate(
            [
                (part[d, :, a * 128 : (a + 1) * 128] - 0.5 * target[a].astype(BF16).astype(F32)).astype(BF16)
                for a in range(4)
            ],
            axis=1,
        )
        grad_rows.append(grad)
        g_d = nt(grad, hcat[...]).reshape(rows, 16, 128) * slo[1, d]
        gh[1, 2 + d, own_r] = g_d.astype(BF16)
        g_planes.append(g_d)
    halo = send_halo(gh, 1, 3)
    dlogits = jnp.concatenate(grad_rows, axis=0)
    g = jnp.stack(g_planes)

    group32 = lax.div(lax.broadcasted_iota(jnp.int32, (32, 128), 1), 32)
    group288 = lax.div(lax.broadcasted_iota(jnp.int32, (288, 128), 1), 32)
    own_chunks = 8 // nr
    from_next = lane < 32
    from_last = lane >= 96

    def weight_grad(layer, g, cols):
        g = g.reshape(-1, 16, 128)
        ahead = jnp.where(from_next & (block < 15), pltpu.roll(g, 15, 1), 0.0)
        edge = jnp.where(from_last & (block > 0), pltpu.roll(g, 1, 1), ahead)
        both = jnp.concatenate([g.reshape(cells, 128), edge.reshape(cells, 128)], axis=1).astype(BF16).T
        prod = nn(jnp.concatenate([both[0:160], both[224:256]], axis=0), cols)

        def take(at):
            return jnp.concatenate([prod[at : at + 32, ij * 128 : (ij + 1) * 128] for ij in range(9)], axis=0)

        s0 = jnp.where(group288 == 3, take(128), take(0))
        s3 = jnp.where(group288 == 0, take(160), take(96))
        total = take(32) + pltpu.roll(s0, 32, 1) + pltpu.roll(take(64), 96, 1) + pltpu.roll(s3, 64, 1)
        for t in range(7):
            tile = None
            ks = [(gr, *divmod(4 * t + gr, 3)) for gr in range(4) if 4 * t + gr < 27]
            for ij in sorted({ij for _, ij, _ in ks}):
                first = [(gr, k) for gr, at, k in ks if at == ij][0]
                moved = rolled(total[ij * 32 : (ij + 1) * 32], first[0] - first[1])
                tile = moved if tile is None else jnp.where(group32 >= first[0], moved, tile)
            pk[layer, t // own_chunks, t % own_chunks] = tile.astype(BF16)
        if layer < layers - 1:
            pk[layer, 7 // own_chunks, 7 % own_chunks] = jnp.zeros((32, 128), BF16)

    def span(layer_set):
        return pl.ds(layer_set[0], len(layer_set)), min(layer_set[0], layers - 2)

    far_first = sorted(range(1, nr), key=lambda s: -min(s, nr - s))

    def send_row(layer_set):
        at, n = span(layer_set)
        return send(
            [(pk.at[at, lax.rem(row + s, nr)], rsin.at[at, s], row_mate(s)) for s in far_first],
            rsin.at[at, pl.ds(1, nr - 1)], rs_s.at[n], rs_r.at[n],
        )

    def send_depth(layer_set, whole):
        arrive(whole)
        at, n = span(layer_set)
        for layer in layer_set:
            total = pk[layer, row].astype(F32)
            for s in range(1, nr):
                total = total + rsin[layer, s].astype(F32)
            dep[layer, depth] = total.astype(BF16)
        return send(
            [(dep.at[at, depth], dep.at[at, depth], depth_mate(s)) for s in range(1, nd)],
            dep.at[at, pl.ds(0, nd - 1)], dp_s.at[n], dp_r.at[n],
        )

    def send_all(layer_set, whole):
        arrive(whole)
        at, n = span(layer_set)
        for layer in layer_set:
            total = dep[layer, 0].astype(F32)
            for s in range(1, nd):
                total = total + dep[layer, s].astype(F32)
            fin[layer, row] = total.astype(BF16)
        return send(
            [(fin.at[at, row], fin.at[at, row], row_mate(s)) for s in far_first],
            fin.at[at, pl.ds(0, nr - 1)], ag_s.at[n], ag_r.at[n],
        )

    def finish(layer_set, whole):
        arrive(whole)
        for layer in layer_set:
            for t in range(7):
                lanes = min(128, 27 * 32 - t * 128)
                cg_ref[layer, :, t * 128 : t * 128 + lanes] = fin[layer, t // own_chunks, t % own_chunks].astype(F32)[:, :lanes]
            if layer == layers - 1:
                hg_ref[...] = fin[layer, 7 // own_chunks, 7 % own_chunks].astype(F32)[:, :classes]

    wide_heads = nn(hidden.T, dlogits)
    heads = wide_heads[0:32, 0:128]
    for a in range(1, 4):
        heads = heads + wide_heads[a * 32 : (a + 1) * 32, a * 128 : (a + 1) * 128]
    pk[3, 7 // own_chunks, 7 % own_chunks] = heads.astype(BF16)
    weight_grad(3, g, windows(xo, 1, mine, 0, OFFSETS))
    first = send_row([3])
    inner_g = {}

    def emit_grad(at):
        def emit(y, p):
            g = y * slw[at, p : p + y.shape[0]]
            go[at, p : p + y.shape[0], 0 : rows + 2] = g.astype(BF16)
            if p == 1:
                inner_g[at] = g[:, 1 : rows + 1]

        return emit

    for _ in ahead_of_depth(3, gh, 1, halo, True, emit_grad(1)):
        pass
    clear_near(go, 1)
    g2 = backward(2, windows(go, 1, mine, 0, mirrored), mine) * slo[0]
    gh[0, own_p, own_r] = g2.astype(BF16)
    halo = send_halo(gh, 0, 2)
    weight_grad(2, inner_g[1], windows(xh, 1, mine, 1, OFFSETS))
    weight_grad(1, g2, windows(xo, 0, mine, 0, OFFSETS))
    second = send_row([1, 2])
    first = send_depth([3], first)
    for _ in ahead_of_depth(1, gh, 0, halo, True, emit_grad(0)):
        weight_grad(0, inner_g[0], windows(xh, 0, mine, 1, OFFSETS))
        last = send_row([0])
    clear_near(go, 0)
    second = send_depth([1, 2], second)
    back = backward(0, windows(go, 0, mine, 0, mirrored), mine)
    tmp[...] = back.reshape(cells, 128)
    for d in range(slab):
        for b in range(16):
            ig_ref[d, :, b * 128 : (b + 1) * 128] = tmp[pl.ds(d * plane + b, rows, stride=16), :].astype(BF16)
    last = send_depth([0], last)
    first = send_all([3], first)
    second = send_all([1, 2], second)
    last = send_all([0], last)
    finish([3], first)
    finish([1, 2], second)
    for whole in started:
        whole.wait_send()
    finish([0], last)


def write_out(cg_ref, hg_ref, ig_ref, cg_out, hg_out, ig_out, sem):
    copies = [
        pltpu.make_async_copy(src, dst, sem.at[n])
        for n, (src, dst) in enumerate([(cg_ref, cg_out), (ig_ref, ig_out), (hg_ref, hg_out)])
    ]
    for copy in copies:
        copy.start()
    for copy in copies:
        copy.wait()


def X_ORDER(nx):
    return [s for s in (2, 1, 3) if s < nx]


def solution(mesh):
    np_, nd, nr = mesh.shape["peer"], mesh.shape["depth"], mesh.shape["row"]
    nx = np_ // 2

    def body(features, labels, conv_weights, head_weights, matching):
        slab, rows, merged = features.shape
        layers = conv_weights.shape[1]
        classes = head_weights.shape[2]
        cells = slab * rows * 16
        chunk = (8 // nr, 32, 128)
        far = (2, slab + 8, rows + 8, 16, 128)
        close = (2, slab + 4, rows + 4, 16, 128)
        vmem = pl.BlockSpec(memory_space=pltpu.VMEM)
        hbm = pl.BlockSpec(memory_space=pltpu.HBM)
        dma = pltpu.SemaphoreType.DMA
        scratch = [
            pltpu.VMEM((slab, rows, merged), BF16),
            pltpu.VMEM((slab, rows, merged // 32), jnp.int32),
            pltpu.VMEM((layers, 32, 27 * 32), BF16),
            pltpu.VMEM((32, classes), BF16),
            pltpu.SMEM((slab, np_), jnp.int32),
            pltpu.VMEM(far, BF16),
            pltpu.VMEM(far, BF16),
            pltpu.VMEM(close, BF16),
            pltpu.VMEM(close, BF16),
            pltpu.VMEM((9, 2, 4, layers * 32, 128), BF16),
            pltpu.VMEM((layers * 32, 896), F32),
            pltpu.VMEM((cells, 128), F32),
            pltpu.VMEM((2, slab, rows, 16, 128), F32),
            pltpu.VMEM((2, slab + 2, rows + 2, 16, 128), F32),
            pltpu.VMEM((128, 512), BF16),
            pltpu.VMEM((slab, 128, 512), BF16),
            pltpu.VMEM((nx, 32, 128), BF16),
            pltpu.VMEM((slab, 32, 128), BF16),
            pltpu.VMEM((slab, 32, 128), BF16),
            [pltpu.VMEM((nx, rows * 8, 128), BF16) for _ in range(slab)],
            pltpu.VMEM((slab, rows * 8, 128), BF16),
            pltpu.VMEM((slab, rows * 8, 128), BF16),
            pltpu.VMEM((slab, rows * 8, 128), BF16),
            pltpu.VMEM((slab, rows * 8, 128), BF16),
            [pltpu.VMEM((nx, rows * 8, 128), BF16) for _ in range(slab)],
            pltpu.VMEM((nx, slab, rows * 8, 128), BF16),
            pltpu.VMEM(((slab + 2) * (rows + 2) * 16, 256), F32),
            pltpu.VMEM((slab, rows * 16, 512), F32),
            pltpu.VMEM((layers, nr) + chunk, BF16),
            pltpu.VMEM((layers, nr) + chunk, BF16),
            pltpu.VMEM((layers, nd) + chunk, BF16),
            pltpu.VMEM((layers, nr) + chunk, BF16),
            dma((5,)),
            dma((4, 3)), dma((4, 3)),
            dma((1,)), dma((1,)),
            dma((slab,)), dma((slab,)),
            dma((slab + 1,)), dma((slab + 1,)),
            dma((slab,)), dma((slab,)),
            dma((slab,)), dma((slab,)),
            dma((layers - 1,)), dma((layers - 1,)),
            dma((layers - 1,)), dma((layers - 1,)),
            dma((layers - 1,)), dma((layers - 1,)),
        ]
        sizes = (nx, nd, nr, slab, rows, classes, layers)
        cg, hg, ig = pl.pallas_call(
            functools.partial(kernel, sizes),
            out_shape=(
                pltpu.VMEM((layers, 32, 27 * 32), F32),
                pltpu.VMEM((32, classes), F32),
                pltpu.VMEM((slab, rows, merged), BF16),
            ),
            in_specs=[hbm] * 5,
            out_specs=(vmem,) * 3,
            scratch_shapes=scratch,
            compiler_params=pltpu.CompilerParams(collective_id=0, has_side_effects=True, vmem_limit_bytes=40 * 2**20),
        )(
            *(
                pltpu.with_memory_space_constraint(v, pltpu.HBM)
                for v in (features, labels, conv_weights[0].transpose(0, 2, 1), head_weights[0], matching)
            )
        )
        cg, hg, ig = pl.pallas_call(
            write_out,
            out_shape=tuple(jax.ShapeDtypeStruct(v.shape, v.dtype) for v in (cg, hg, ig)),
            in_specs=[vmem] * 3,
            out_specs=(hbm,) * 3,
            scratch_shapes=[dma((3,))],
            compiler_params=pltpu.CompilerParams(vmem_limit_bytes=2**20),
        )(cg, hg, ig)
        return cg.transpose(0, 2, 1)[None], hg[None], ig[None]

    return jax.shard_map(
        body,
        mesh=mesh,
        in_specs=(
            P("depth", "row", None),
            P("depth", "row", None),
            P("peer", None, None, None),
            P("peer", None, None),
            P("depth", None),
        ),
        out_specs=(
            P("peer", None, None, None),
            P("peer", None, None),
            P("peer", "depth", "row", None),
        ),
        check_vma=False,
    )
```
